32 devices in a mesh: dp: 8 (over y, x, core), tensor: 4 (over z).
Axes of the slice: x: 2, y: 2, z: 4, core: 2. Of those that a mesh axis runs over, the one named last changes fastest.
Arguments:
- inputs: bfloat16 [6144, 2048], P('dp'), may hold values from -6 to 6
- block_ids: int32 [8, 768], P('dp'), may hold values from 0 to 3, never falling along the last dimension, each value on 1 to 256 neighbouring positions
- first_gain: float32 [2048], replicated, may hold values from 0.5 to 1.5
- first_shift: float32 [2048], replicated, may hold values from -3 to 3
- mixing_weight: bfloat16 [2048, 3, 2048], P(None, None, 'tensor'), may hold values from -0.125 to 0.125
- mixing_bias: float32 [2, 2048], P(None, 'tensor'), may hold values from -3 to 3
- output_weight: bfloat16 [2048, 2048], P('tensor'), may hold values from -0.75 to 0.75
- output_bias: float32 [2048], replicated, may hold values from -3 to 3
- second_gain: float32 [2048], replicated, may hold values from 0.5 to 1.5
- second_shift: float32 [2048], replicated, may hold values from -3 to 3
- expand_weight: bfloat16 [2048, 8192], P(None, 'tensor'), may hold values from -0.125 to 0.125
- expand_bias: float32 [8192], P('tensor'), may hold values from -3 to 3
- shrink_weight: bfloat16 [8192, 2048], P('tensor'), may hold values from -0.0625 to 0.0625
- shrink_bias: float32 [2048], replicated, may hold values from -3 to 3
- cotangent: bfloat16 [6144, 2048], P('dp'), may hold values from -6 to 6
Outputs:
- outputs: bfloat16 [6144, 2048], P('dp')
- input_grad: bfloat16 [6144, 2048], P('dp')
- first_gain_grad: float32 [2048], replicated
- first_shift_grad: float32 [2048], replicated
- mixing_weight_grad: float32 [2048, 3, 2048], P(None, None, 'tensor')
- mixing_bias_grad: float32 [2, 2048], P(None, 'tensor')
- output_weight_grad: float32 [2048, 2048], P('tensor')
- output_bias_grad: float32 [2048], replicated
- second_gain_grad: float32 [2048], replicated
- second_shift_grad: float32 [2048], replicated
- expand_weight_grad: float32 [2048, 8192], P(None, 'tensor')
- expand_bias_grad: float32 [8192], P('tensor')
- shrink_weight_grad: float32 [8192, 2048], P('tensor')
- shrink_bias_grad: float32 [2048], replicated
The draws below stay inside these ranges and needn't reach their ends.
Inputs may be any that keep to these rules, and one draw needn't show every extreme that they name: `block_ids`: each sequence's block numbers start at 0, never fall, rise by one from block to block, give 4 blocks of 1 to 256 tokens, and one block has exactly 256 tokens.
All inputs are finite; a program needn't handle non-finite values.
Results may differ from the reference program's by a relative error of at most 0.014.
Values may be sent and summed in bfloat16 or wider, within the bound.
A program may use at most 256 MiB of HBM per device.

```python
import math
from functools import partial
import jax
import jax.numpy as jnp
import numpy as np
from jax import lax

D = 2048
H = 32
HD = 64
FF = 8192
LENGTH = 768
BLOCKS = 4
BLOCK = 256
SEQS = 8
TOKENS = 6144


def shard_levels(own_key, dims, pieces, least, high):
    factor_of, own = 1.0, jax.random.fold_in(own_key, 6)
    for axis_at, shards_of in pieces:
        steps = jnp.exp(jax.random.uniform(jax.random.fold_in(own, axis_at), (shards_of,), jnp.float32, least / len(pieces), high / len(pieces)))
        factor_of = factor_of * jnp.repeat(steps, dims[axis_at] // shards_of).reshape([-1 if axis == axis_at else 1 for axis in range(len(dims))])
    return factor_of


def length_profile(count, total, most, skew):
    portions = [(1 << 20) // math.isqrt(grade ** skew) + 1 for grade in range(2, count + 1)]
    spare, holding = total - most - (count - 1), [1] * (count - 1)
    while spare > 0:
        free = [i for i in range(count - 1) if holding[i] < most]
        mass, budget = sum([portions[i] for i in free]), spare
        for i in free:
            addition = min(most - holding[i], max(1, budget * portions[i] // mass), spare)
            holding[i] = holding[i] + addition
            spare = spare - addition
    return np.array([most] + holding)


def ragged(key, count, total, most, slope):
    if count == 2:
        one = jax.random.randint(key, (), max(1, total - most), min(most, total - 1) + 1)
        return jnp.stack([one, total - one])
    sizes = jnp.asarray(length_profile(count, total, most, slope), jnp.int32)
    twos = (count - 1) // 2
    donor, taker = sizes[1:1 + 2 * twos:2], sizes[2:2 + 2 * twos:2]
    slack = jnp.minimum(donor - 1, most - taker)
    moved = jax.random.randint(jax.random.fold_in(key, 1), (twos,), 0, 1 << 20) % (slack + 1)
    sizes = sizes.at[1:1 + 2 * twos:2].set(donor - moved).at[2:2 + 2 * twos:2].set(taker + moved)
    return sizes[jax.random.permutation(jax.random.fold_in(key, 2), count)]


def normal_values(own_key, shape, spread, bound, split=(), kind=jnp.bfloat16):
    gain = shard_levels(own_key, shape, split, -0.22, 0.18) if split else 1.0
    drawn = jax.random.normal(own_key, shape, jnp.float32) * spread * gain
    return jnp.minimum(jnp.maximum(drawn, -bound), bound).astype(kind)


def setup_inputs(seed: int = 0) -> dict:
    streams_of = jax.random.split(jax.random.key(seed), 16)
    inputs = normal_values(streams_of[0], (TOKENS, D), 1.0, 6.0, ((0, 8),))
    block_ids = jax.vmap(lambda own: jnp.searchsorted(jnp.cumsum(ragged(own, BLOCKS, LENGTH, BLOCK, 0)), jnp.arange(LENGTH), side="right"))(jax.random.split(streams_of[1], SEQS)).reshape((SEQS, LENGTH)).astype(jnp.int32)
    first_gain = jnp.clip(1.0 + 0.1 * jax.random.normal(streams_of[2], (D,), jnp.float32), 0.5, 1.5)
    first_shift = normal_values(streams_of[3], (D,), 0.3, 3.0, (), jnp.float32)
    mixing_weight = normal_values(streams_of[4], (D, 3, D), D ** -0.5, 0.125, ((2, 4),))
    mixing_bias = normal_values(streams_of[5], (2, D), 0.3, 3.0, ((1, 4),), jnp.float32)
    output_weight = normal_values(streams_of[6], (D, D), (max(D // 32, 4)) ** -0.5, 0.75, ((0, 4),))
    output_bias = normal_values(streams_of[7], (D,), 0.3, 3.0, (), jnp.float32)
    second_gain = jnp.clip(1.0 + 0.1 * jax.random.normal(streams_of[8], (D,), jnp.float32), 0.5, 1.5)
    second_shift = normal_values(streams_of[9], (D,), 0.3, 3.0, (), jnp.float32)
    expand_weight = normal_values(streams_of[10], (D, FF), D ** -0.5, 0.125, ((1, 4),))
    expand_bias = normal_values(streams_of[11], (FF,), 0.5, 3.0, ((0, 4),), jnp.float32)
    shrink_weight = normal_values(streams_of[12], (FF, D), FF ** -0.5, 0.0625, ((0, 4),))
    shrink_bias = normal_values(streams_of[13], (D,), 0.3, 3.0, (), jnp.float32)
    cotangent = normal_values(streams_of[14], (TOKENS, D), 1.0, 6.0, ((0, 8),))
    return {"inputs": inputs, "block_ids": block_ids, "first_gain": first_gain, "first_shift": first_shift, "mixing_weight": mixing_weight, "mixing_bias": mixing_bias, "output_weight": output_weight, "output_bias": output_bias, "second_gain": second_gain, "second_shift": second_shift, "expand_weight": expand_weight, "expand_bias": expand_bias, "shrink_weight": shrink_weight, "shrink_bias": shrink_bias, "cotangent": cotangent}


HIGH = lax.Precision.HIGHEST
EPS = 1e-05

@jax.custom_vjp
def low(v):
    return lax.optimization_barrier(v.astype(jnp.bfloat16)).astype(jnp.float32)

@jax.custom_vjp
def low_back(v):
    return v

def low_keep(v):
    return (low(v), None)

def low_pass(kept, grad):
    return (grad,)

def back_keep(v):
    return (v, None)

def back_low(kept, grad):
    return (low(grad),)
low.defvjp(low_keep, low_pass)
low_back.defvjp(back_keep, back_low)

def layer_norm(values, scale_gain, shift_bias):
    row_mean = lax.optimization_barrier(jnp.mean(values, axis=-1, keepdims=True))
    centred = values - row_mean
    row_var = lax.optimization_barrier(jnp.mean(centred * centred, axis=-1, keepdims=True))
    return centred * lax.rsqrt(row_var + EPS) * scale_gain + shift_bias

def matmul(left, right):
    return jnp.dot(left, right, precision=HIGH)

def layer_forward(blocks, inputs, first_gain, first_shift, mixing_weight, mixing_bias, output_weight, output_bias, second_gain, second_shift, expand_weight, expand_bias, shrink_weight, shrink_bias):
    length = inputs.shape[0]
    normed = low(layer_norm(inputs, first_gain, first_shift))
    mixed = matmul(normed, mixing_weight.reshape(D, 3 * D)).reshape(length, 3, D)
    query = low(low_back(mixed[:, 0] + mixing_bias[0])).reshape(length, H, HD)
    keys = low(low_back(mixed[:, 1])).reshape(length, H, HD)
    vals = low(low_back(mixed[:, 2] + mixing_bias[1])).reshape(length, H, HD)
    scores = jnp.einsum('qhd,khd->hqk', query, keys, precision=HIGH) * (1.0 / math.sqrt(HD))
    heads_index = jnp.arange(H).astype(jnp.float32)
    slopes = 2.0 ** (-8.0 * (heads_index + 1.0) / H)
    places = jnp.arange(length)
    offsets = (places[None, :] - places[:, None]).astype(jnp.float32)
    scores = low_back(scores + slopes[:, None, None] * offsets[None])
    allowed = blocks[None, :] <= blocks[:, None]
    masked = jnp.where(allowed[None], scores, -1e+30)
    probs = low(jax.nn.softmax(masked, axis=-1))
    attended = jnp.einsum('hqk,khd->qhd', probs, vals, precision=HIGH).reshape(length, D)
    attended = low(low_back(attended))
    resid = low_back(matmul(attended, output_weight) + output_bias)
    hidden = inputs + resid
    second = low(layer_norm(hidden, second_gain, second_shift))
    pre_act = low_back(matmul(second, expand_weight) + expand_bias)
    activ = low(jax.nn.gelu(pre_act, approximate=False))
    return hidden + matmul(activ, shrink_weight) + shrink_bias

def reference(inputs, block_ids, first_gain, first_shift, mixing_weight, mixing_bias, output_weight, output_bias, second_gain, second_shift, expand_weight, expand_bias, shrink_weight, shrink_bias, cotangent):
    params = tuple((item.astype(jnp.float32) for item in (first_gain, first_shift, mixing_weight, mixing_bias, output_weight, output_bias, second_gain, second_shift, expand_weight, expand_bias, shrink_weight, shrink_bias)))
    sequences = inputs.astype(jnp.float32).reshape(SEQS, LENGTH, D)
    upstreams = cotangent.astype(jnp.float32).reshape(SEQS, LENGTH, D)
    starting = tuple((jnp.zeros_like(item) for item in params))

    def per_sequence(totals, element):
        sequence, blocks, upstream = element
        result, pull_back = jax.vjp(partial(layer_forward, blocks), sequence, *params)
        grads = pull_back(upstream)
        totals = tuple((total + grad for total, grad in zip(totals, grads[1:])))
        return (totals, (result.astype(jnp.bfloat16), grads[0].astype(jnp.bfloat16)))
    totals, (results, in_grads) = lax.scan(per_sequence, starting, (sequences, block_ids, upstreams))
    return (results.reshape(TOKENS, D), in_grads.reshape(TOKENS, D), totals[0], totals[1], totals[2], totals[3], totals[4], totals[5], totals[6], totals[7], totals[8], totals[9], totals[10], totals[11])
```

```python
import functools
import math

import jax
import jax.numpy as jnp
from jax import lax
from jax.experimental import pallas as pl
from jax.experimental.pallas import tpu as pltpu
from jax.sharding import PartitionSpec as P

H = 32
HD = 64
EPS = 1e-05
F32 = jnp.float32
BF16 = jnp.bfloat16
MESH = pl.DeviceIdType.MESH


def layer_norm(values, scale_gain, shift_bias):
    row_mean = jnp.mean(values, axis=-1, keepdims=True)
    centred = values - row_mean
    row_var = jnp.mean(centred * centred, axis=-1, keepdims=True)
    return centred * lax.rsqrt(row_var + EPS) * scale_gain + shift_bias


def norm_backward(values, scale_gain, shift_bias, upstream):
    _, pull_back = jax.vjp(layer_norm, values, scale_gain, shift_bias)
    return pull_back(upstream)


def gelu_exact(values):
    return jax.nn.gelu(values, approximate=False)


def biased_scores(query, keys, blocks, first_head):
    length, local_heads, head_width = query.shape
    scores = jnp.einsum("qhd,khd->hqk", query, keys, preferred_element_type=F32) * (
        1.0 / math.sqrt(head_width)
    )
    heads_index = (first_head + jnp.arange(local_heads)).astype(F32)
    slopes = 2.0 ** (-8.0 * (heads_index + 1.0) / H)
    places = jnp.arange(length)
    offsets = (places[None, :] - places[:, None]).astype(F32)
    scores = scores + slopes[:, None, None] * offsets[None]
    allowed = blocks[None, :] <= blocks[:, None]
    return jnp.where(allowed[None], scores, -1e30)


def add_rows(dst, src, step):
    rows = dst.shape[0]

    def body(i, carry):
        at = pl.ds(pl.multiple_of(i * step, step), step)
        dst[at, :] = (dst[at, :].astype(F32) + src[at, :].astype(F32)).astype(BF16)
        return carry

    lax.fori_loop(0, rows // step, body, 0)


def sums_kernel(n, n_z, n_dp, chunks, pieces, *refs):
    z_in, refs = refs[:n_z], refs[n_z:]
    g_in, refs = refs[:n_dp], refs[n_dp:]
    z_out, refs = refs[0], refs[1:]
    g_out, refs = (refs[0], refs[1:]) if n_dp else (None, refs)
    part, outer_in, inner_in, load_sem, zs_in, zs_out, zr_outer, zr_inner, store_sem, *refs = refs
    if n_dp:
        fin, c0, r1, r2, gl, c0s, c0r, s1, q1, s2, q2, s3, q3, s4, q4, gstore = refs

    total_z = sum(chunks)
    total_p = sum(pieces)
    i = lax.axis_index("tensor")
    left = i < n // 2
    inner = jnp.where(left, i + 1, i - 1)
    depth = jnp.where(left, i, n - 1 - i)
    has_outer = depth > 0
    outer = jnp.where(has_outer, jnp.where(left, i - 1, i + 1), inner)
    is_mid = depth == n // 2 - 1
    lag = 2 * (n // 2 - 1 - depth) + 1

    if n_dp:
        d = lax.axis_index("dp")
        c, x, y = d % 2, (d // 2) % 2, d // 4
        to_c, to_x, to_y = d + 1 - 2 * c, d + 2 - 4 * x, d + 4 - 8 * y

    at = 0
    for k in range(n_z):
        pltpu.make_async_copy(z_in[k], part.at[pl.ds(at, chunks[k])], load_sem.at[k]).start()
        at += chunks[k]
    at = 0
    for k in range(n_dp):
        pltpu.make_async_copy(g_in[k].at[:, c], fin.at[pl.ds(at, pieces[k]), c], gl.at[k]).start()
        at += pieces[k]

    barrier = pltpu.get_barrier_semaphore()
    pl.semaphore_signal(barrier, inc=1, device_id={"tensor": inner}, device_id_type=MESH)

    @pl.when(has_outer)
    def _():
        pl.semaphore_signal(barrier, inc=1, device_id={"tensor": outer}, device_id_type=MESH)

    count = 1
    if n_dp:
        for to in (to_c, to_x, to_y):
            pl.semaphore_signal(barrier, inc=1, device_id={"dp": to}, device_id_type=MESH)
        count = 4

    @pl.when(has_outer)
    def _():
        pl.semaphore_wait(barrier, count + 1)

    @pl.when(jnp.logical_not(has_outer))
    def _():
        pl.semaphore_wait(barrier, count)

    def copy(src, dst, send, recv, axis, to):
        return pltpu.make_async_remote_copy(
            src_ref=src,
            dst_ref=dst,
            send_sem=send,
            recv_sem=recv,
            device_id={axis: to},
            device_id_type=MESH,
        )

    def inward_mid(k):
        return copy(part.at[k], inner_in.at[k], zs_in.at[k], zr_inner.at[k], "tensor", inner)

    def inward(k):
        return copy(part.at[k], outer_in.at[k], zs_in.at[k], zr_outer.at[k], "tensor", inner)

    def outward(k):
        return copy(inner_in.at[k], inner_in.at[k], zs_out.at[k], zr_inner.at[k], "tensor", outer)

    def store(k):
        return pltpu.make_async_copy(inner_in.at[k], z_out.at[k], store_sem.at[k])

    def z_reduce(k):
        at = 0
        for j in range(n_z):

            @pl.when(k == at)
            def _(j=j, at=at):
                pltpu.make_async_copy(z_in[j], part.at[pl.ds(at, chunks[j])], load_sem.at[j]).wait()

            at += chunks[j]

        @pl.when(has_outer)
        def _():
            inward(k).wait_recv()
            add_rows(part.at[k], outer_in.at[k], 16)

        @pl.when(is_mid)
        def _():
            inward_mid(k).start()

        @pl.when(jnp.logical_not(is_mid))
        def _():
            inward(k).start()

    def z_spread(k):
        inward_mid(k).wait_recv()

        @pl.when(is_mid)
        def _():
            add_rows(inner_in.at[k], part.at[k], 16)

        @pl.when(has_outer)
        def _():
            outward(k).start()

        store(k).start()

    if n_dp:

        def core_half(k, j, at):
            return copy(g_in[j].at[k - at, 1 - c], c0.at[k], c0s.at[k], c0r.at[k], "dp", to_c)

        def hop1(k):
            return (
                copy(fin.at[k, c, 0, 1 - x], r1.at[k, 0], s1.at[k, 0], q1.at[k, 0], "dp", to_x),
                copy(fin.at[k, c, 1, 1 - y], r1.at[k, 1], s1.at[k, 1], q1.at[k, 1], "dp", to_y),
            )

        def hop2(k):
            return (
                copy(fin.at[k, c, 0, x], r2.at[k, 0], s2.at[k, 0], q2.at[k, 0], "dp", to_y),
                copy(fin.at[k, c, 1, y], r2.at[k, 1], s2.at[k, 1], q2.at[k, 1], "dp", to_x),
            )

        def hop3(k):
            return (
                copy(fin.at[k, c, 0, x], fin.at[k, c, 0, x], s3.at[k, 0], q3.at[k, 0], "dp", to_x),
                copy(fin.at[k, c, 1, y], fin.at[k, c, 1, y], s3.at[k, 1], q3.at[k, 1], "dp", to_y),
            )

        def hop4(k):
            return copy(fin.at[k, c], fin.at[k, c], s4.at[k], q4.at[k], "dp", to_c)

        def g_store(k):
            return pltpu.make_async_copy(fin.at[k], g_out.at[k], gstore.at[k])

        at = 0
        for j in range(n_dp):

            def send_half(k, carry, j=j, at=at):
                core_half(k + at, j, at).start()
                return carry

            lax.fori_loop(0, pieces[j], send_half, 0)
            at += pieces[j]

        step = 32 if r1.shape[2] % 32 == 0 else 16

        def stage1(k):
            at = 0
            for j in range(n_dp):

                @pl.when(k == at)
                def _(j=j, at=at):
                    pltpu.make_async_copy(
                        g_in[j].at[:, c], fin.at[pl.ds(at, pieces[j]), c], gl.at[j]
                    ).wait()

                at += pieces[j]
            core_half(k, 0, k).wait_recv()
            for a in range(2):
                for b in range(2):
                    add_rows(fin.at[k, c, a, b], c0.at[k, a, b], step)
            for one in hop1(k):
                one.start()

        def stage2(k):
            for one in hop1(k):
                one.wait()
            add_rows(fin.at[k, c, 0, x], r1.at[k, 0], step)
            add_rows(fin.at[k, c, 1, y], r1.at[k, 1], step)
            for one in hop2(k):
                one.start()

        def stage3(k):
            for one in hop2(k):
                one.wait()
            add_rows(fin.at[k, c, 0, x], r2.at[k, 0], step)
            add_rows(fin.at[k, c, 1, y], r2.at[k, 1], step)
            for one in hop3(k):
                one.start()

        def stage4(k):
            for one in hop3(k):
                one.wait_recv()
            hop4(k).start()

        def stage5(k):
            hop4(k).wait_recv()
            g_store(k).start()

    def tick(t, carry):
        @pl.when(t < total_z)
        def _():
            z_reduce(t)

        back = t - lag

        @pl.when(jnp.logical_and(back >= 0, back < total_z))
        def _():
            z_spread(back)

        if n_dp:
            for late, stage in enumerate((stage1, stage2, stage3, stage4, stage5)):
                k = t - late

                @pl.when(jnp.logical_and(k >= 0, k < total_p))
                def _(stage=stage, k=k):
                    stage(k)

        return carry

    ticks = max(total_z + n - 1, total_p + 4 if n_dp else 0)
    lax.fori_loop(0, ticks, tick, 0)

    def drain_z(k, carry):
        @pl.when(is_mid)
        def _():
            inward_mid(k).wait_send()

        @pl.when(jnp.logical_not(is_mid))
        def _():
            inward(k).wait_send()

        @pl.when(has_outer)
        def _():
            outward(k).wait_send()

        store(k).wait()
        return carry

    lax.fori_loop(0, total_z, drain_z, 0)
    if n_dp:

        def drain_g(k, carry):
            core_half(k, 0, k).wait_send()
            for one in hop3(k) + (hop4(k),):
                one.wait_send()
            g_store(k).wait()
            return carry

        lax.fori_loop(0, total_p, drain_g, 0)


def device_sums(n, z_parts, g_parts, collective_id):
    chunks = tuple(one.shape[0] for one in z_parts)
    pieces = tuple(one.shape[0] for one in g_parts)
    nz, npc = sum(chunks), sum(pieces)
    z_block = z_parts[0].shape[1:]
    dma = pltpu.SemaphoreType.DMA
    scratch = [pltpu.VMEM((nz, *z_block), BF16)] * 3 + [dma((len(chunks),))] + [dma((nz,))] * 5
    out_shape = [jax.ShapeDtypeStruct((nz, *z_block), BF16)]
    vmem = 3 * nz * math.prod(z_block) * 2
    if g_parts:
        g_block = g_parts[0].shape[4:]
        scratch += [
            pltpu.VMEM((npc, 2, 2, 2, *g_block), BF16),
            pltpu.VMEM((npc, 2, 2, *g_block), BF16),
            pltpu.VMEM((npc, 2, *g_block), BF16),
            pltpu.VMEM((npc, 2, *g_block), BF16),
            dma((len(pieces),)),
            dma((npc,)),
            dma((npc,)),
        ]
        scratch += [dma((npc, 2))] * 6 + [dma((npc,))] * 3
        out_shape.append(jax.ShapeDtypeStruct((npc, 2, 2, 2, *g_block), BF16))
        vmem += 16 * npc * math.prod(g_block) * 2
    out = pl.pallas_call(
        functools.partial(sums_kernel, n, len(z_parts), len(g_parts), chunks, pieces),
        out_shape=out_shape,
        in_specs=[pl.BlockSpec(memory_space=pl.ANY)] * (len(z_parts) + len(g_parts)),
        out_specs=[pl.BlockSpec(memory_space=pl.ANY)] * len(out_shape),
        scratch_shapes=scratch,
        compiler_params=pltpu.CompilerParams(
            collective_id=collective_id, has_side_effects=True, vmem_limit_bytes=vmem + (2 << 20)
        ),
    )(*z_parts, *g_parts)
    return out


def on_device(
    fast,
    n_tensor,
    inputs,
    block_ids,
    first_gain,
    first_shift,
    mixing_weight,
    mixing_bias,
    output_weight,
    output_bias,
    second_gain,
    second_shift,
    expand_weight,
    expand_bias,
    shrink_weight,
    shrink_bias,
    cotangent,
):
    source = inputs.astype(F32)
    upstream = cotangent.astype(F32)
    length, width = source.shape
    blocks = block_ids[0]
    local_width = mixing_weight.shape[2]
    local_heads = local_width // HD
    units = expand_weight.shape[1]
    first_head = lax.axis_index("tensor") * local_heads
    rows = 96

    def sums(z_parts, g_parts, collective_id):
        if not fast:
            return (
                [lax.psum(one.astype(BF16), "tensor").astype(F32) for one in z_parts],
                [lax.psum(one, "dp") for one in g_parts],
            )
        z_low = [one.astype(BF16).reshape(length // rows, rows, width) for one in z_parts]
        out = device_sums(n_tensor, z_low, [one.astype(BF16) for one in g_parts], collective_id)
        z_all = out[0].reshape(len(z_parts), length, width)
        z_out = [z_all[k].astype(F32) for k in range(len(z_parts))]
        g_out, at = [], 0
        for one in g_parts:
            g_out.append(out[1][at : at + one.shape[0]].astype(F32))
            at += one.shape[0]
        return z_out, g_out

    weights = mixing_weight.transpose(1, 0, 2)
    normed_low = layer_norm(source, first_gain, first_shift).astype(BF16)

    def project(k):
        return jnp.dot(normed_low, weights[k], preferred_element_type=F32)

    query = (project(0) + mixing_bias[0]).astype(BF16).reshape(length, local_heads, HD)
    keys = project(1).astype(BF16).reshape(length, local_heads, HD)
    vals = (project(2) + mixing_bias[1]).astype(BF16).reshape(length, local_heads, HD)
    masked = biased_scores(query, keys, blocks, first_head)
    row_top = jnp.max(masked, axis=-1, keepdims=True)
    logsum = row_top + jnp.log(jnp.sum(jnp.exp(masked - row_top), axis=-1, keepdims=True))
    probs_low = jnp.exp(masked - logsum).astype(BF16)
    attended = (
        jnp.einsum("hqk,khd->qhd", probs_low, vals, preferred_element_type=F32)
        .reshape(length, local_width)
        .astype(BF16)
    )
    partial_out = jnp.dot(attended, output_weight, preferred_element_type=F32)
    (resid,), _ = sums([partial_out], [], 0)
    hidden_state = source + (resid + output_bias)
    second_low = layer_norm(hidden_state, second_gain, second_shift).astype(BF16)
    pre_act = jnp.dot(second_low, expand_weight, preferred_element_type=F32) + expand_bias
    activ_low = gelu_exact(pre_act).astype(BF16)
    partial_mlp = jnp.dot(activ_low, shrink_weight, preferred_element_type=F32)
    act_grad = jnp.einsum("td,fd->tf", cotangent, shrink_weight, preferred_element_type=F32)
    _, gelu_pull = jax.vjp(gelu_exact, pre_act)
    pre_grad = gelu_pull(act_grad)[0].astype(BF16)
    shrink_part = jnp.einsum("tf,td->fd", activ_low, cotangent, preferred_element_type=F32)
    shrink_bias_part = jnp.sum(upstream, axis=0)
    expand_part = jnp.einsum("td,tf->df", second_low, pre_grad, preferred_element_type=F32)
    expand_bias_part = jnp.sum(pre_grad.astype(F32), axis=0)
    second_part = jnp.einsum("tf,df->td", pre_grad, expand_weight, preferred_element_type=F32)

    (second_grad, mlp_sum), (shrink_sum, expand_sum) = sums(
        [second_part, partial_mlp],
        [
            shrink_part.reshape(-1, 2, 2, 2, 32, width),
            expand_part.reshape(-1, 2, 2, 2, 32, units),
        ],
        1,
    )
    shrink_weight_grad = shrink_sum.reshape(units, width)
    expand_weight_grad = expand_sum.reshape(width, units)
    outputs = (hidden_state + mlp_sum + shrink_bias).astype(BF16)
    hidden_grad, second_gain_part, second_shift_part = norm_backward(
        hidden_state, second_gain, second_shift, second_grad
    )
    hidden_grad = hidden_grad + upstream
    resid_low = hidden_grad.astype(BF16)
    output_part = jnp.einsum("tc,td->cd", attended, resid_low, preferred_element_type=F32)
    output_bias_part = jnp.sum(resid_low.astype(F32), axis=0)
    attended_grad = (
        jnp.einsum("td,cd->tc", resid_low, output_weight, preferred_element_type=F32)
        .astype(BF16)
        .reshape(length, local_heads, HD)
    )
    probs = jnp.exp(biased_scores(query, keys, blocks, first_head) - logsum)
    probs_low = probs.astype(BF16)
    prob_grad = jnp.einsum("qhd,khd->hqk", attended_grad, vals, preferred_element_type=F32)
    vals_grad = jnp.einsum(
        "hqk,qhd->khd", probs_low, attended_grad, preferred_element_type=F32
    ).astype(BF16)
    row_delta = jnp.sum(probs * prob_grad, axis=-1, keepdims=True)
    score_grad = (probs * (prob_grad - row_delta)).astype(BF16)
    scale_factor = 1.0 / math.sqrt(HD)
    query_grad = (
        jnp.einsum("hqk,khd->qhd", score_grad, keys, preferred_element_type=F32) * scale_factor
    ).astype(BF16)
    keys_grad = (
        jnp.einsum("hqk,qhd->khd", score_grad, query, preferred_element_type=F32) * scale_factor
    ).astype(BF16)
    grads = [one.reshape(length, local_width) for one in (query_grad, keys_grad, vals_grad)]
    mixing_part = jnp.stack(
        [jnp.einsum("td,tc->dc", normed_low, one, preferred_element_type=F32) for one in grads]
    )
    mixing_bias_part = jnp.stack(
        [jnp.sum(grads[0].astype(F32), axis=0), jnp.sum(grads[2].astype(F32), axis=0)]
    )
    normed_part = sum(
        jnp.einsum("tc,dc->td", one, weights[k], preferred_element_type=F32)
        for k, one in enumerate(grads)
    )
    quarters = width // local_width
    (normed_grad,), (mixing_sum, output_sum) = sums(
        [normed_part],
        [
            mixing_part.reshape(-1, 2, 2, 2, 128, local_width),
            output_part.reshape(local_width, quarters, local_width)
            .transpose(1, 0, 2)
            .reshape(-1, 2, 2, 2, 128, local_width),
        ],
        2,
    )
    mixing_weight_grad = mixing_sum.reshape(3, width, local_width).transpose(1, 0, 2)
    output_weight_grad = (
        output_sum.reshape(quarters, local_width, local_width)
        .transpose(1, 0, 2)
        .reshape(local_width, width)
    )
    source_grad, first_gain_part, first_shift_part = norm_backward(
        source, first_gain, first_shift, normed_grad
    )
    input_grad = (source_grad + hidden_grad).astype(BF16)
    small = lax.psum(
        (
            first_gain_part,
            first_shift_part,
            mixing_bias_part,
            output_bias_part,
            second_gain_part,
            second_shift_part,
            expand_bias_part,
            shrink_bias_part,
        ),
        "dp",
    )
    return (
        outputs,
        input_grad,
        small[0],
        small[1],
        mixing_weight_grad,
        small[2],
        output_weight_grad,
        small[3],
        small[4],
        small[5],
        expand_weight_grad,
        small[6],
        shrink_weight_grad,
        small[7],
    )


def solution(mesh):
    in_specs = (
        P("dp", None),
        P("dp", None),
        P(),
        P(),
        P(None, None, "tensor"),
        P(None, "tensor"),
        P("tensor", None),
        P(),
        P(),
        P(),
        P(None, "tensor"),
        P("tensor"),
        P("tensor", None),
        P(),
        P("dp", None),
    )
    out_specs = (
        P("dp", None),
        P("dp", None),
        P(),
        P(),
        P(None, None, "tensor"),
        P(None, "tensor"),
        P("tensor", None),
        P(),
        P(),
        P(),
        P(None, "tensor"),
        P("tensor"),
        P("tensor", None),
        P(),
    )
    n_tensor = mesh.shape["tensor"]
    fast = mesh.shape["dp"] == 8 and n_tensor % 2 == 0
    return jax.shard_map(
        functools.partial(on_device, fast, n_tensor),
        mesh=mesh,
        in_specs=in_specs,
        out_specs=out_specs,
        check_vma=False,
    )
```

```python
import functools
import math

import jax
import jax.numpy as jnp
from jax import lax
from jax.experimental import pallas as pl
from jax.experimental.pallas import tpu as pltpu
from jax.sharding import PartitionSpec as P

H = 32
HD = 64
EPS = 1e-05
F32 = jnp.float32
BF16 = jnp.bfloat16
MESH = pl.DeviceIdType.MESH


def layer_norm(values, scale_gain, shift_bias):
    row_mean = jnp.mean(values, axis=-1, keepdims=True)
    centred = values - row_mean
    row_var = jnp.mean(centred * centred, axis=-1, keepdims=True)
    return centred * lax.rsqrt(row_var + EPS) * scale_gain + shift_bias


def norm_backward(values, scale_gain, shift_bias, upstream):
    _, pull_back = jax.vjp(layer_norm, values, scale_gain, shift_bias)
    return pull_back(upstream)


def gelu_exact(values):
    return jax.nn.gelu(values, approximate=False)


def biased_scores(query, keys, blocks, first_head):
    length, local_heads, head_width = query.shape
    scores = jnp.einsum("qhd,khd->hqk", query, keys, preferred_element_type=F32) * (
        1.0 / math.sqrt(head_width)
    )
    heads_index = (first_head + jnp.arange(local_heads)).astype(F32)
    slopes = 2.0 ** (-8.0 * (heads_index + 1.0) / H)
    places = jnp.arange(length)
    offsets = (places[None, :] - places[:, None]).astype(F32)
    scores = scores + slopes[:, None, None] * offsets[None]
    allowed = blocks[None, :] <= blocks[:, None]
    return jnp.where(allowed[None], scores, -1e30)


def add_rows(dst, src, step):
    rows = dst.shape[0]

    def body(i, carry):
        at = pl.ds(pl.multiple_of(i * step, step), step)
        dst[at, :] = (dst[at, :].astype(F32) + src[at, :].astype(F32)).astype(BF16)
        return carry

    lax.fori_loop(0, rows // step, body, 0)


def remote(src, dst, send, recv, axis, to):
    return pltpu.make_async_remote_copy(
        src_ref=src,
        dst_ref=dst,
        send_sem=send,
        recv_sem=recv,
        device_id={axis: to},
        device_id_type=MESH,
    )


class Chain:
    def __init__(self, n, refs, slack=1):
        self.part, self.outer_in, self.inner_in, self.s_in, self.s_out, self.r_outer, self.r_inner = refs
        i = lax.axis_index("tensor")
        left = i < n // 2
        depth = jnp.where(left, i, n - 1 - i)
        self.inner = jnp.where(left, i + 1, i - 1)
        self.has_outer = depth > 0
        self.outer = jnp.where(self.has_outer, jnp.where(left, i - 1, i + 1), self.inner)
        self.is_mid = depth == n // 2 - 1
        self.lag = slack * (2 * (n // 2 - 1 - depth) + 1)
        self.most_lag = slack * (n - 1)

    @staticmethod
    def scratch(count, block):
        dma = pltpu.SemaphoreType.DMA
        return [pltpu.VMEM((count, *block), BF16)] * 3 + [dma((count,))] * 4

    def to_mid(self, k):
        return remote(
            self.part.at[k], self.inner_in.at[k], self.s_in.at[k], self.r_inner.at[k], "tensor", self.inner
        )

    def to_inner(self, k):
        return remote(
            self.part.at[k], self.outer_in.at[k], self.s_in.at[k], self.r_outer.at[k], "tensor", self.inner
        )

    def to_outer(self, k):
        return remote(
            self.inner_in.at[k], self.inner_in.at[k], self.s_out.at[k], self.r_inner.at[k], "tensor", self.outer
        )

    def greet(self, barrier):
        pl.semaphore_signal(barrier, inc=1, device_id={"tensor": self.inner}, device_id_type=MESH)

        @pl.when(self.has_outer)
        def _():
            pl.semaphore_signal(barrier, inc=1, device_id={"tensor": self.outer}, device_id_type=MESH)

    def wait_greetings(self, barrier, others):
        @pl.when(self.has_outer)
        def _():
            pl.semaphore_wait(barrier, others + 2)

        @pl.when(jnp.logical_not(self.has_outer))
        def _():
            pl.semaphore_wait(barrier, others + 1)

    def reduce(self, k):
        @pl.when(self.has_outer)
        def _():
            self.to_inner(k).wait_recv()
            add_rows(self.part.at[k], self.outer_in.at[k], 16)

        @pl.when(self.is_mid)
        def _():
            self.to_mid(k).start()

        @pl.when(jnp.logical_not(self.is_mid))
        def _():
            self.to_inner(k).start()

    def spread(self, k):
        self.to_mid(k).wait_recv()

        @pl.when(self.is_mid)
        def _():
            add_rows(self.inner_in.at[k], self.part.at[k], 16)

        @pl.when(self.has_outer)
        def _():
            self.to_outer(k).start()

    def drain(self, k):
        self.to_mid(k).wait_send()

        @pl.when(self.has_outer)
        def _():
            self.to_outer(k).wait_send()


def between(k, count):
    return jnp.logical_and(k >= 0, k < count)


ROWS = 32
SLACK = 2
BLOCK_ROWS = 256
TILE = 512


def mlp_kernel(n, length, *refs):
    (att_h, wo_h, src_h, dy_h, wu_h, wd_h, vec_h), refs = refs[:7], refs[7:]
    (tot_h, second_h, activ_h, pre_h, mlp_h, grad_h, bias_h), refs = refs[:7], refs[7:]
    (att, wo, src, dy, wu, wd, vec, second, activ, pre, mlp, grad, bias), refs = refs[:13], refs[13:]
    load, store, tot_store, *refs = refs
    chain = Chain(n, refs, SLACK)
    width = wo.shape[1]
    units = wu.shape[1]
    chunks = length // ROWS
    blocks = length // BLOCK_ROWS
    per_block = BLOCK_ROWS // ROWS
    group = 4

    loads = [
        pltpu.make_async_copy(a, b, load.at[k])
        for k, (a, b) in enumerate(
            ((att_h, att), (wo_h, wo), (vec_h, vec), (src_h, src), (wu_h, wu), (dy_h, dy), (wd_h, wd))
        )
    ]
    for one in loads:
        one.start()
    barrier = pltpu.get_barrier_semaphore()
    chain.greet(barrier)
    bias[...] = jnp.zeros_like(bias)
    chain.wait_greetings(barrier, 0)
    for one in loads[:3]:
        one.wait()

    def tot_copy(k):
        return pltpu.make_async_copy(chain.inner_in.at[k], tot_h.at[k], tot_store.at[k])

    def block_copies(b):
        at = pl.ds(pl.multiple_of(b * BLOCK_ROWS, BLOCK_ROWS), BLOCK_ROWS)
        pairs = ((second, second_h), (activ, activ_h), (pre, pre_h), (mlp, mlp_h), (grad, grad_h))
        return [
            pltpu.make_async_copy(a.at[at], h.at[at], store.at[b, j]) for j, (a, h) in enumerate(pairs)
        ]

    def produce(g):
        rows = group * ROWS
        left = att[pl.ds(pl.multiple_of(g * rows, rows), rows), :]
        for j in range(width // 512):
            cols = pl.ds(j * 512, 512)
            got = jnp.dot(left, wo[:, cols], preferred_element_type=F32).astype(BF16)
            for q in range(group):
                chain.part[g * group + q, :, cols] = got[q * ROWS : (q + 1) * ROWS]

    def normalize(b):
        step = 16

        def body(i, carry):
            at = pl.ds(pl.multiple_of(b * BLOCK_ROWS + i * step, step), step)
            k = b * per_block + i // (ROWS // step)
            inside = pl.ds(pl.multiple_of((i % (ROWS // step)) * step, step), step)
            value = src[at, :].astype(F32) + (chain.inner_in[k, inside, :].astype(F32) + vec[0:1, :width])
            centred = value - jnp.mean(value, axis=-1, keepdims=True)
            var = jnp.mean(centred * centred, axis=-1, keepdims=True)
            second[at, :] = (
                centred * lax.rsqrt(var + EPS) * vec[1:2, :width] + vec[2:3, :width]
            ).astype(BF16)
            return carry

        lax.fori_loop(0, BLOCK_ROWS // step, body, 0)

    def hidden_tile(b, j):
        at = pl.ds(pl.multiple_of(b * BLOCK_ROWS, BLOCK_ROWS), BLOCK_ROWS)
        cols = pl.ds(pl.multiple_of(j * TILE, TILE), TILE)
        value = jnp.dot(second[at, :], wu[:, cols], preferred_element_type=F32) + vec[3:4, cols]
        back = lax.dot_general(
            dy[at, :], wd[cols, :], (((1,), (1,)), ((), ())), preferred_element_type=F32
        )
        below = 0.5 + 0.5 * lax.erf(value * math.sqrt(0.5))
        density = jnp.exp(-0.5 * value * value) * (1.0 / math.sqrt(2.0 * math.pi))
        activ[at, cols] = (value * below).astype(BF16)
        low = (back * (below + value * density)).astype(BF16)
        pre[at, cols] = low
        bias[:, cols] += jnp.sum(low.astype(F32).reshape(BLOCK_ROWS // 8, 8, TILE), axis=0)

    def out_tile(b, j):
        at = pl.ds(pl.multiple_of(b * BLOCK_ROWS, BLOCK_ROWS), BLOCK_ROWS)
        cols = pl.ds(pl.multiple_of(j * TILE, TILE), TILE)
        mlp[at, cols] = jnp.dot(activ[at, :], wd[:, cols], preferred_element_type=F32).astype(BF16)
        grad[at, cols] = lax.dot_general(
            pre[at, :], wu[cols, :], (((1,), (1,)), ((), ())), preferred_element_type=F32
        ).astype(BF16)

    ahead = units // TILE
    steps = ahead + width // TILE
    per_tick = -(-steps // per_block)
    first_tick = per_block + chain.most_lag

    def tick(t, carry):
        @pl.when(jnp.logical_and(t % group == 0, t < chunks))
        def _():
            produce(t // group)

        @pl.when(t < chunks)
        def _():
            chain.reduce(t)

        back = t - chain.lag

        @pl.when(between(back, chunks))
        def _():
            chain.spread(back)
            tot_copy(back).start()

        late = t - first_tick

        @pl.when(late == 0)
        def _():
            for one in loads[3:]:
                one.wait()

        @pl.when(between(late, blocks * per_block))
        def _():
            b = late // per_block
            for q in range(per_tick):
                s = (late % per_block) * per_tick + q

                @pl.when(s == 0)
                def _():
                    normalize(b)

                @pl.when(s < ahead)
                def _():
                    hidden_tile(b, s)

                @pl.when(between(s - ahead, width // TILE))
                def _():
                    out_tile(b, s - ahead)

                @pl.when(s == steps - 1)
                def _():
                    for one in block_copies(b):
                        one.start()

        return carry

    lax.fori_loop(0, chunks + first_tick, tick, 0)
    bias_copy = pltpu.make_async_copy(bias, bias_h, load.at[0])
    bias_copy.start()

    def drain(k, carry):
        chain.drain(k)
        tot_copy(k).wait()
        return carry

    lax.fori_loop(0, chunks, drain, 0)
    for b in range(blocks):
        for one in block_copies(b):
            one.wait()
    bias_copy.wait()


def mlp_call(n, att, wo, src, dy, wu, wd, vec):
    length, width = src.shape
    units = wu.shape[1]
    chunks = length // ROWS
    dma = pltpu.SemaphoreType.DMA
    inputs = (att, wo, src, dy, wu, wd, vec)
    outs = [(chunks, ROWS, width), (length, width), (length, units), (length, units)]
    outs += [(length, width), (length, width)]
    out_shape = [jax.ShapeDtypeStruct(one, BF16) for one in outs] + [jax.ShapeDtypeStruct((8, units), F32)]
    scratch = [pltpu.VMEM(one.shape, one.dtype) for one in inputs]
    scratch += [pltpu.VMEM(one.shape, one.dtype) for one in out_shape[1:]]
    scratch += [dma((7,)), dma((length // BLOCK_ROWS, 5)), dma((chunks,))]
    scratch += Chain.scratch(chunks, (ROWS, width))
    return pl.pallas_call(
        functools.partial(mlp_kernel, n, length),
        out_shape=out_shape,
        in_specs=[pl.BlockSpec(memory_space=pl.ANY)] * len(inputs),
        out_specs=[pl.BlockSpec(memory_space=pl.ANY)] * len(out_shape),
        scratch_shapes=scratch,
        compiler_params=pltpu.CompilerParams(
            collective_id=0, has_side_effects=True, vmem_limit_bytes=60 << 20
        ),
    )(*inputs)


class Ring:
    GONE = 5

    def __init__(self, n, refs, slots):
        self.chain = Chain(n, refs)
        self.slots = slots

    def at(self, k):
        return lax.rem(k, self.slots)

    def reduce(self, k):
        self.chain.reduce(self.at(k))

    def spread(self, k):
        self.chain.spread(self.at(k))

    def retire(self, k):
        self.chain.drain(self.at(k))


class Cube:
    SLOTS = 7
    GONE = 6

    def __init__(self, refs, out, step):
        (self.fin, self.give, self.c0, self.r1, self.r2), refs = refs[:5], refs[5:]
        self.s0, self.q0, self.s1, self.q1, self.s2, self.q2, self.s3, self.q3, self.s4, self.q4, self.kept = refs
        self.out, self.step = out, step
        d = lax.axis_index("dp")
        self.c, self.x, self.y = d % 2, (d // 2) % 2, d // 4
        self.to_c, self.to_x, self.to_y = d + 1 - 2 * self.c, d + 2 - 4 * self.x, d + 4 - 8 * self.y
        self.stages = (self.stage1, self.stage2, self.stage3, self.stage4, self.stage5, self.retire)

    @classmethod
    def scratch(cls, block):
        dma, n = pltpu.SemaphoreType.DMA, cls.SLOTS
        return [
            pltpu.VMEM((n, 2, 2, 2, *block), BF16),
            pltpu.VMEM((n, 2, 2, *block), BF16),
            pltpu.VMEM((n, 2, 2, *block), BF16),
            pltpu.VMEM((n, 2, *block), BF16),
            pltpu.VMEM((n, 2, *block), BF16),
            *[dma((n,))] * 2,
            *[dma((n, 2))] * 6,
            *[dma((n,))] * 3,
        ]

    def greet(self, barrier):
        for to in (self.to_c, self.to_x, self.to_y):
            pl.semaphore_signal(barrier, inc=1, device_id={"dp": to}, device_id_type=MESH)

    def slot(self, k):
        return lax.rem(k, self.SLOTS)

    def half(self, k):
        p = self.slot(k)
        return remote(self.give.at[p], self.c0.at[p], self.s0.at[p], self.q0.at[p], "dp", self.to_c)

    def quarters(self, p):
        return self.fin.at[p, self.c, 0, self.x], self.fin.at[p, self.c, 1, self.y]

    def hop1(self, k):
        p, fin, c = self.slot(k), self.fin, self.c
        return (
            remote(fin.at[p, c, 0, 1 - self.x], self.r1.at[p, 0], self.s1.at[p, 0], self.q1.at[p, 0], "dp", self.to_x),
            remote(fin.at[p, c, 1, 1 - self.y], self.r1.at[p, 1], self.s1.at[p, 1], self.q1.at[p, 1], "dp", self.to_y),
        )

    def hop2(self, k):
        p = self.slot(k)
        a, b = self.quarters(p)
        return (
            remote(a, self.r2.at[p, 0], self.s2.at[p, 0], self.q2.at[p, 0], "dp", self.to_y),
            remote(b, self.r2.at[p, 1], self.s2.at[p, 1], self.q2.at[p, 1], "dp", self.to_x),
        )

    def hop3(self, k):
        p = self.slot(k)
        a, b = self.quarters(p)
        return (
            remote(a, a, self.s3.at[p, 0], self.q3.at[p, 0], "dp", self.to_x),
            remote(b, b, self.s3.at[p, 1], self.q3.at[p, 1], "dp", self.to_y),
        )

    def hop4(self, k):
        p = self.slot(k)
        mine = self.fin.at[p, self.c]
        return remote(mine, mine, self.s4.at[p], self.q4.at[p], "dp", self.to_c)

    def keep(self, k):
        p = self.slot(k)
        return pltpu.make_async_copy(self.fin.at[p], self.out.at[k], self.kept.at[p])

    def add_quarters(self, k, got):
        p = self.slot(k)
        for j, quarter in enumerate(self.quarters(p)):
            add_rows(quarter, got.at[p, j], self.step)

    def stage1(self, k):
        self.half(k).wait()
        p = self.slot(k)
        for a in range(2):
            for b in range(2):
                add_rows(self.fin.at[p, self.c, a, b], self.c0.at[p, a, b], self.step)
        for one in self.hop1(k):
            one.start()

    def stage2(self, k):
        for one in self.hop1(k):
            one.wait()
        self.add_quarters(k, self.r1)
        for one in self.hop2(k):
            one.start()

    def stage3(self, k):
        for one in self.hop2(k):
            one.wait()
        self.add_quarters(k, self.r2)
        for one in self.hop3(k):
            one.start()

    def stage4(self, k):
        for one in self.hop3(k):
            one.wait_recv()
        self.hop4(k).start()

    def stage5(self, k):
        self.hop4(k).wait_recv()
        self.keep(k).start()

    def retire(self, k):
        for one in self.hop3(k) + (self.hop4(k),):
            one.wait_send()
        self.keep(k).wait()

    def tick(self, t, count):
        for late, stage in reversed(tuple(enumerate(self.stages, 1))):
            k = t - late

            @pl.when(between(k, count))
            def _(stage=stage, k=k):
                stage(k)


def weighted(left, right):
    return lax.dot_general(left, right, (((0,), (0,)), ((), ())), preferred_element_type=F32).astype(BF16)


def lane_half(odd):
    return (lax.broadcasted_iota(jnp.int32, (1, 2 * HD), 1) // HD == odd).astype(F32)


def head_backward(head, q, k, v, up, lse, slope, off, tile, grads, acc):
    q_grad, k_grad, v_grad = grads
    k_acc, v_acc = acc
    length = q.shape[0]
    odd = lax.rem(head, 2)
    mask = lane_half(odd).astype(BF16)
    lanes = pl.ds(pl.multiple_of((head // 2) * 2 * HD, 2 * HD), 2 * HD)
    scale = 1.0 / math.sqrt(HD)
    gain = slope[pl.ds(head, 1), 0:1]
    nt = (((1,), (1,)), ((), ()))
    for j in range(length // tile):
        rows = slice(j * tile, (j + 1) * tile)
        most = min(length, (j + 2) * tile)
        q_here = q[rows, lanes]
        up_here = up[rows, lanes] * mask
        k_here = k[0:most, lanes] * mask
        scores = lax.dot_general(k_here, q_here, nt, preferred_element_type=F32)
        probs = jnp.exp(scores * scale + gain * off[0:most, rows] - lse[pl.ds(head, 1), rows])
        back = lax.dot_general(v[0:most, lanes], up_here, nt, preferred_element_type=F32)
        delta = jnp.sum(probs * back, axis=0, keepdims=True)
        score_grad = (probs * (back - delta)).astype(BF16)
        v_part = jnp.dot(probs.astype(BF16), up_here, preferred_element_type=F32)
        k_part = jnp.dot(score_grad, q_here * mask, preferred_element_type=F32)
        if j == 0:
            v_acc[0:most, :] = v_part
            k_acc[0:most, :] = k_part
            if most < length:
                v_acc[most:length, :] = jnp.zeros((length - most, 2 * HD), F32)
                k_acc[most:length, :] = jnp.zeros((length - most, 2 * HD), F32)
        else:
            v_acc[0:most, :] += v_part
            k_acc[0:most, :] += k_part
        q_part = lax.dot_general(k_here, score_grad, (((0,), (0,)), ((), ())), preferred_element_type=F32)
        mine = (q_part.T * scale).astype(BF16)

        @pl.when(odd == 0)
        def _(rows=rows, mine=mine):
            q_grad[rows, lanes] = mine

        @pl.when(odd == 1)
        def _(rows=rows, mine=mine):
            q_grad[rows, lanes] += mine

    for to, got, factor in ((k_grad, k_acc, scale), (v_grad, v_acc, 1.0)):

        @pl.when(odd == 0)
        def _(to=to, got=got, factor=factor):
            to[:, lanes] = (got[...] * factor).astype(BF16)

        @pl.when(odd == 1)
        def _(to=to, got=got, factor=factor):
            to[:, lanes] += (got[...] * factor).astype(BF16)


BACK_ROWS = 96
HEAD_TILE = 256


def back_kernel(n, heads, *refs):
    (grad_h, mlp_h, activ_h, dy_h, second_h, pre_h, src_h, tot_h), refs = refs[:8], refs[8:]
    smalls_h, refs = refs[:8], refs[8:]
    (sum_h, g_out, resid_h, qg_h, kg_h, vg_h, cols_h), refs = refs[:7], refs[7:]
    (left, dy, pre, src, tot, resid), refs = refs[:6], refs[6:]
    smalls, refs = refs[:8], refs[8:]
    vec, wo, q, k, v, lse, slope, off = smalls
    (up, qg, kg, vg, k_acc, v_acc, cols), refs = refs[:7], refs[7:]
    (load, left_sem, part_sem, row_sem, resid_sem, sum_sem), refs = refs[:6], refs[6:]
    slots = 8
    ring, refs = Ring(n, refs[:7], slots), refs[7:]
    chain = ring.chain
    cube = Cube(refs, g_out, 32)
    width, units = dy.shape[1], pre.shape[1]
    rows, per_sum = BACK_ROWS, grad_h.shape[0]
    total_z = 2 * per_sum
    piece = 256
    first = activ_h.shape[1] // piece
    total_p = first + second_h.shape[1] // piece

    loads = [pltpu.make_async_copy(a, b, load.at[j]) for j, (a, b) in enumerate(zip(smalls_h, smalls))]
    loads += [pltpu.make_async_copy(dy_h, dy, load.at[8]), pltpu.make_async_copy(pre_h, pre, load.at[9])]

    def part_load(j, which):
        return pltpu.make_async_copy(
            (grad_h, mlp_h)[which].at[lax.rem(j, per_sum)], chain.part.at[ring.at(j)], part_sem.at[ring.at(j)]
        )

    def part_start(j):
        @pl.when(j < per_sum)
        def _():
            part_load(j, 0).start()

        @pl.when(between(j - per_sum, per_sum))
        def _():
            part_load(j, 1).start()

    def left_load(p, which):
        at = (p - which * first) * piece
        return pltpu.make_async_copy(
            (activ_h, second_h)[which].at[:, pl.ds(pl.multiple_of(at, piece), piece)],
            left.at[lax.rem(p, 2)],
            left_sem.at[lax.rem(p, 2)],
        )

    def left_start(p):
        @pl.when(p < first)
        def _():
            left_load(p, 0).start()

        @pl.when(between(p - first, total_p - first))
        def _():
            left_load(p, 1).start()

    def row_loads(j):
        at = lax.rem(j, 2)
        return (
            pltpu.make_async_copy(src_h.at[j], src.at[at], row_sem.at[at, 0]),
            pltpu.make_async_copy(tot_h.at[j], tot.at[at], row_sem.at[at, 1]),
        )

    def resid_store(j):
        at = lax.rem(j, 2)
        return pltpu.make_async_copy(resid.at[at], resid_h.at[j], resid_sem.at[at])

    def sum_store(j):
        at = ring.at(j)
        return pltpu.make_async_copy(chain.inner_in.at[at], sum_h.at[j - per_sum], sum_sem.at[at])

    part_start(0)
    part_start(1)
    left_start(0)
    loads[8].start()
    for one in loads[:8] + loads[9:]:
        one.start()
    barrier = pltpu.get_barrier_semaphore()
    chain.greet(barrier)
    cube.greet(barrier)
    cols[...] = jnp.zeros_like(cols)
    chain.wait_greetings(barrier, 3)
    for one in loads:
        one.wait()

    def produce(p):
        at = lax.rem(p, 2)
        to = cube.slot(p)
        pltpu.make_async_copy(activ_h.at[:, pl.ds(0, piece)], left.at[at], left_sem.at[at]).wait()
        mine, theirs = cube.c, 1 - cube.c
        count = piece // 8

        def product(right):
            for side, store in ((theirs, cube.give.at[to]), (mine, cube.fin.at[to, cube.c])):
                rows_of = left[at, :, pl.ds(pl.multiple_of(side * (piece // 2), piece // 2), piece // 2)]
                for j in range(right.shape[1] // 512):
                    here = pl.ds(j * 512, 512)
                    got = weighted(rows_of, right[:, here])
                    for a in range(2):
                        for b in range(2):
                            lo = (2 * a + b) * count
                            store[a, b, :, here] = got[lo : lo + count]

        @pl.when(p < first)
        def _():
            product(dy)

        @pl.when(p >= first)
        def _():
            product(pre)

        cube.half(p).start()

    def row_sum(x):
        return jnp.sum(x, axis=-1, keepdims=True)

    def rows_back(j):
        for one in row_loads(j):
            one.wait()
        at, got = lax.rem(j, 2), ring.at(j)
        step = 16

        def body(i, carry):
            here = pl.ds(pl.multiple_of(i * step, step), step)
            value = src[at, here, :].astype(F32) + (tot[at, here, :].astype(F32) + vec[0:1, :])
            centred = value - row_sum(value) / width
            spread = lax.rsqrt(row_sum(centred * centred) / width + EPS)
            normal = centred * spread
            down = chain.inner_in[got, here, :].astype(F32)
            scaled = down * vec[1:2, :]
            flat, slope_of = row_sum(scaled) / width, row_sum(scaled * normal) / width
            back = spread * (scaled - flat - normal * slope_of)
            all_rows = pl.ds(pl.multiple_of(j * rows + i * step, step), step)
            low = (back + dy[all_rows, :].astype(F32)).astype(BF16)
            resid[at, here, :] = low
            for c, item in enumerate((down * normal, down, low.astype(F32))):
                cols[c] += item[0:8] + item[8:16]
            return carry

        lax.fori_loop(0, rows // step, body, 0)
        all_rows = pl.ds(pl.multiple_of(j * rows, rows), rows)
        up[all_rows, :] = lax.dot_general(
            resid[at], wo[...], (((1,), (1,)), ((), ())), preferred_element_type=F32
        ).astype(BF16)
        resid_store(j).start()

    def tick(t, carry):
        gone = t - Ring.GONE

        @pl.when(between(gone, total_z))
        def _():
            ring.retire(gone)

            @pl.when(gone >= per_sum)
            def _():
                sum_store(gone).wait()

        part_start(t + 2)

        @pl.when(t < total_z)
        def _():
            part_load(t, 0).wait()
            ring.reduce(t)

        back = t - chain.lag

        @pl.when(between(back, total_z))
        def _():
            ring.spread(back)

            @pl.when(back >= per_sum)
            def _():
                sum_store(back).start()

        cube.tick(t, total_p)

        @pl.when(t < total_p)
        def _():
            left_start(t + 1)
            produce(t)

        chunk = t - 4

        @pl.when(between(chunk + 1, per_sum))
        def _():
            for one in row_loads(chunk + 1):
                one.start()

        @pl.when(between(chunk - 2, per_sum))
        def _():
            resid_store(chunk - 2).wait()

        @pl.when(between(chunk, per_sum))
        def _():
            rows_back(chunk)

        head = t - 4 - per_sum

        @pl.when(between(head, heads))
        def _():
            head_backward(head, q, k, v, up, lse, slope, off, HEAD_TILE, (qg, kg, vg), (k_acc, v_acc))

        return carry

    ticks = max(total_z + Ring.GONE, total_p + Cube.GONE, 4 + per_sum + max(heads, 2))
    lax.fori_loop(0, ticks, tick, 0)
    stores = [
        pltpu.make_async_copy(a, b, load.at[j])
        for j, (a, b) in enumerate(((qg, qg_h), (kg, kg_h), (vg, vg_h), (cols, cols_h)))
    ]
    for one in stores:
        one.start()
    for one in stores:
        one.wait()


def back_call(n, grad, mlp, activ, dy, second, pre, src, tot, vec, wo, q, k, v, lse, slope, off):
    length, width = dy.shape
    chunks = length // BACK_ROWS
    dma = pltpu.SemaphoreType.DMA

    def cut(one):
        return one.reshape(chunks, BACK_ROWS, one.shape[-1])

    smalls = (vec, wo, q, k, v, lse, slope, off)
    inputs = (cut(grad), cut(mlp), activ, dy, second, pre, cut(src), cut(tot), *smalls)
    pieces = (activ.shape[1] + second.shape[1]) // 256
    shapes = [
        ((chunks, BACK_ROWS, width), BF16),
        ((pieces, 2, 2, 2, 32, width), BF16),
        ((chunks, BACK_ROWS, width), BF16),
        *[(q.shape, BF16)] * 3,
        ((3, 8, width), F32),
    ]
    slots = 8
    scratch = [
        pltpu.VMEM((2, length, 256), BF16),
        pltpu.VMEM(dy.shape, BF16),
        pltpu.VMEM(pre.shape, BF16),
        *[pltpu.VMEM((2, BACK_ROWS, width), BF16)] * 3,
        *[pltpu.VMEM(one.shape, one.dtype) for one in smalls],
        *[pltpu.VMEM(q.shape, BF16)] * 4,
        *[pltpu.VMEM((length, 2 * HD), F32)] * 2,
        pltpu.VMEM((3, 8, width), F32),
        dma((10,)),
        dma((2,)),
        dma((slots,)),
        dma((2, 2)),
        dma((2,)),
        dma((slots,)),
        *Chain.scratch(slots, (BACK_ROWS, width)),
        *Cube.scratch((32, width)),
    ]
    return pl.pallas_call(
        functools.partial(back_kernel, n, q.shape[1] // HD),
        out_shape=[jax.ShapeDtypeStruct(*one) for one in shapes],
        in_specs=[pl.BlockSpec(memory_space=pl.ANY)] * len(inputs),
        out_specs=[pl.BlockSpec(memory_space=pl.ANY)] * len(shapes),
        scratch_shapes=scratch,
        compiler_params=pltpu.CompilerParams(
            collective_id=1, has_side_effects=True, vmem_limit_bytes=60 << 20
        ),
    )(*inputs)


def sums_kernel(n, n_z, n_dp, chunks, pieces, *refs):
    z_in, refs = refs[:n_z], refs[n_z:]
    g_in, refs = refs[:n_dp], refs[n_dp:]
    z_out, g_out, load_sem, store_sem, *refs = refs
    chain, refs = Chain(n, refs[:7]), refs[7:]
    fin, c0, r1, r2, gl, c0s, c0r, s1, q1, s2, q2, s3, q3, s4, q4, gstore = refs

    total_z = sum(chunks)
    total_p = sum(pieces)
    d = lax.axis_index("dp")
    c, x, y = d % 2, (d // 2) % 2, d // 4
    to_c, to_x, to_y = d + 1 - 2 * c, d + 2 - 4 * x, d + 4 - 8 * y

    def z_load(j, at):
        return pltpu.make_async_copy(z_in[j], chain.part.at[pl.ds(at, chunks[j])], load_sem.at[j])

    def g_load(j, at):
        return pltpu.make_async_copy(g_in[j].at[:, c], fin.at[pl.ds(at, pieces[j]), c], gl.at[j])

    z_at = [sum(chunks[:k]) for k in range(n_z)]
    p_at = [sum(pieces[:k]) for k in range(n_dp)]
    for j in range(n_z):
        z_load(j, z_at[j]).start()
    for j in range(n_dp):
        g_load(j, p_at[j]).start()

    barrier = pltpu.get_barrier_semaphore()
    chain.greet(barrier)
    for to in (to_c, to_x, to_y):
        pl.semaphore_signal(barrier, inc=1, device_id={"dp": to}, device_id_type=MESH)
    chain.wait_greetings(barrier, 3)

    def store(k):
        return pltpu.make_async_copy(chain.inner_in.at[k], z_out.at[k], store_sem.at[k])

    def core_half(k, j, at):
        return remote(g_in[j].at[k - at, 1 - c], c0.at[k], c0s.at[k], c0r.at[k], "dp", to_c)

    def hop1(k):
        return (
            remote(fin.at[k, c, 0, 1 - x], r1.at[k, 0], s1.at[k, 0], q1.at[k, 0], "dp", to_x),
            remote(fin.at[k, c, 1, 1 - y], r1.at[k, 1], s1.at[k, 1], q1.at[k, 1], "dp", to_y),
        )

    def hop2(k):
        return (
            remote(fin.at[k, c, 0, x], r2.at[k, 0], s2.at[k, 0], q2.at[k, 0], "dp", to_y),
            remote(fin.at[k, c, 1, y], r2.at[k, 1], s2.at[k, 1], q2.at[k, 1], "dp", to_x),
        )

    def hop3(k):
        return (
            remote(fin.at[k, c, 0, x], fin.at[k, c, 0, x], s3.at[k, 0], q3.at[k, 0], "dp", to_x),
            remote(fin.at[k, c, 1, y], fin.at[k, c, 1, y], s3.at[k, 1], q3.at[k, 1], "dp", to_y),
        )

    def hop4(k):
        return remote(fin.at[k, c], fin.at[k, c], s4.at[k], q4.at[k], "dp", to_c)

    def g_store(k):
        return pltpu.make_async_copy(fin.at[k], g_out.at[k], gstore.at[k])

    for j in range(n_dp):

        def send_half(k, carry, j=j):
            core_half(k + p_at[j], j, p_at[j]).start()
            return carry

        lax.fori_loop(0, pieces[j], send_half, 0)

    step = 32 if r1.shape[2] % 32 == 0 else 16

    def stage1(k):
        for j in range(n_dp):

            @pl.when(k == p_at[j])
            def _(j=j):
                g_load(j, p_at[j]).wait()

        core_half(k, 0, k).wait_recv()
        for a in range(2):
            for b in range(2):
                add_rows(fin.at[k, c, a, b], c0.at[k, a, b], step)
        for one in hop1(k):
            one.start()

    def stage2(k):
        for one in hop1(k):
            one.wait()
        add_rows(fin.at[k, c, 0, x], r1.at[k, 0], step)
        add_rows(fin.at[k, c, 1, y], r1.at[k, 1], step)
        for one in hop2(k):
            one.start()

    def stage3(k):
        for one in hop2(k):
            one.wait()
        add_rows(fin.at[k, c, 0, x], r2.at[k, 0], step)
        add_rows(fin.at[k, c, 1, y], r2.at[k, 1], step)
        for one in hop3(k):
            one.start()

    def stage4(k):
        for one in hop3(k):
            one.wait_recv()
        hop4(k).start()

    def stage5(k):
        hop4(k).wait_recv()
        g_store(k).start()

    def tick(t, carry):
        @pl.when(t < total_z)
        def _():
            for j in range(n_z):

                @pl.when(t == z_at[j])
                def _(j=j):
                    z_load(j, z_at[j]).wait()

            chain.reduce(t)

        back = t - chain.lag

        @pl.when(between(back, total_z))
        def _():
            chain.spread(back)
            store(back).start()

        for late, stage in enumerate((stage1, stage2, stage3, stage4, stage5)):
            k = t - late

            @pl.when(between(k, total_p))
            def _(stage=stage, k=k):
                stage(k)

        return carry

    lax.fori_loop(0, max(total_z + chain.most_lag, total_p + 4), tick, 0)

    def drain_z(k, carry):
        chain.drain(k)
        store(k).wait()
        return carry

    lax.fori_loop(0, total_z, drain_z, 0)

    def drain_g(k, carry):
        core_half(k, 0, k).wait_send()
        for one in hop3(k) + (hop4(k),):
            one.wait_send()
        g_store(k).wait()
        return carry

    lax.fori_loop(0, total_p, drain_g, 0)


def device_sums(n, z_parts, g_parts, collective_id):
    chunks = tuple(one.shape[0] for one in z_parts)
    pieces = tuple(one.shape[0] for one in g_parts)
    nz, npc = sum(chunks), sum(pieces)
    z_block = z_parts[0].shape[1:]
    g_block = g_parts[0].shape[4:]
    dma = pltpu.SemaphoreType.DMA
    scratch = [dma((len(chunks),)), dma((nz,))] + Chain.scratch(nz, z_block)
    scratch += [
        pltpu.VMEM((npc, 2, 2, 2, *g_block), BF16),
        pltpu.VMEM((npc, 2, 2, *g_block), BF16),
        pltpu.VMEM((npc, 2, *g_block), BF16),
        pltpu.VMEM((npc, 2, *g_block), BF16),
        dma((len(pieces),)),
        dma((npc,)),
        dma((npc,)),
    ]
    scratch += [dma((npc, 2))] * 6 + [dma((npc,))] * 3
    out_shape = [
        jax.ShapeDtypeStruct((nz, *z_block), BF16),
        jax.ShapeDtypeStruct((npc, 2, 2, 2, *g_block), BF16),
    ]
    vmem = 2 * (3 * nz * math.prod(z_block) + 16 * npc * math.prod(g_block))
    return pl.pallas_call(
        functools.partial(sums_kernel, n, len(z_parts), len(g_parts), chunks, pieces),
        out_shape=out_shape,
        in_specs=[pl.BlockSpec(memory_space=pl.ANY)] * (len(z_parts) + len(g_parts)),
        out_specs=[pl.BlockSpec(memory_space=pl.ANY)] * len(out_shape),
        scratch_shapes=scratch,
        compiler_params=pltpu.CompilerParams(
            collective_id=collective_id, has_side_effects=True, vmem_limit_bytes=vmem + (2 << 20)
        ),
    )(*z_parts, *g_parts)


def on_device(
    fast,
    n_tensor,
    inputs,
    block_ids,
    first_gain,
    first_shift,
    mixing_weight,
    mixing_bias,
    output_weight,
    output_bias,
    second_gain,
    second_shift,
    expand_weight,
    expand_bias,
    shrink_weight,
    shrink_bias,
    cotangent,
):
    source = inputs.astype(F32)
    upstream = cotangent.astype(F32)
    length, width = source.shape
    blocks = block_ids[0]
    local_width = mixing_weight.shape[2]
    local_heads = local_width // HD
    units = expand_weight.shape[1]
    first_head = lax.axis_index("tensor") * local_heads
    rows = 96

    def sums(z_parts, g_parts, collective_id):
        if not fast:
            return (
                [lax.psum(one.astype(BF16), "tensor").astype(F32) for one in z_parts],
                [lax.psum(one, "dp") for one in g_parts],
            )
        z_low = [one.astype(BF16).reshape(length // rows, rows, width) for one in z_parts]
        out = device_sums(n_tensor, z_low, [one.astype(BF16) for one in g_parts], collective_id)
        z_all = out[0].reshape(len(z_parts), length, width)
        z_out = [z_all[k].astype(F32) for k in range(len(z_parts))]
        g_out, at = [], 0
        for one in g_parts:
            g_out.append(out[1][at : at + one.shape[0]].astype(F32))
            at += one.shape[0]
        return z_out, g_out

    weights = mixing_weight.transpose(1, 0, 2)
    normed_low = layer_norm(source, first_gain, first_shift).astype(BF16)

    def project(k):
        return jnp.dot(normed_low, weights[k], preferred_element_type=F32)

    query = (project(0) + mixing_bias[0]).astype(BF16).reshape(length, local_heads, HD)
    keys = project(1).astype(BF16).reshape(length, local_heads, HD)
    vals = (project(2) + mixing_bias[1]).astype(BF16).reshape(length, local_heads, HD)
    masked = biased_scores(query, keys, blocks, first_head)
    row_top = jnp.max(masked, axis=-1, keepdims=True)
    logsum = row_top + jnp.log(jnp.sum(jnp.exp(masked - row_top), axis=-1, keepdims=True))
    probs_low = jnp.exp(masked - logsum).astype(BF16)
    attended = (
        jnp.einsum("hqk,khd->qhd", probs_low, vals, preferred_element_type=F32)
        .reshape(length, local_width)
        .astype(BF16)
    )
    if fast:
        most = max(width, units)
        vectors = jnp.stack(
            [
                jnp.pad(one, (0, most - one.shape[0]))
                for one in (output_bias, second_gain, second_shift, expand_bias)
            ]
        )
        total, second_low, activ_low, pre_grad, partial_mlp, second_part, expand_bias_part = mlp_call(
            n_tensor, attended, output_weight, inputs, cotangent, expand_weight, shrink_weight, vectors
        )
        expand_bias_part = jnp.sum(expand_bias_part, axis=0)
        hidden_state = source + (total.reshape(length, width).astype(F32) + output_bias)
    else:
        partial_out = jnp.dot(attended, output_weight, preferred_element_type=F32)
        resid = lax.psum(partial_out.astype(BF16), "tensor").astype(F32)
        hidden_state = source + (resid + output_bias)
        second_low = layer_norm(hidden_state, second_gain, second_shift).astype(BF16)
        pre_act = jnp.dot(second_low, expand_weight, preferred_element_type=F32) + expand_bias
        activ_low = gelu_exact(pre_act).astype(BF16)
        partial_mlp = jnp.dot(activ_low, shrink_weight, preferred_element_type=F32)
        act_grad = jnp.einsum("td,fd->tf", cotangent, shrink_weight, preferred_element_type=F32)
        _, gelu_pull = jax.vjp(gelu_exact, pre_act)
        pre_grad = gelu_pull(act_grad)[0].astype(BF16)
        expand_bias_part = jnp.sum(pre_grad.astype(F32), axis=0)
        second_part = jnp.einsum("tf,df->td", pre_grad, expand_weight, preferred_element_type=F32)
    shrink_bias_part = jnp.sum(upstream, axis=0)
    if fast:
        places = jnp.arange(length)
        off = jnp.where(
            blocks[:, None] <= blocks[None, :], (places[:, None] - places[None, :]).astype(F32), -1e30
        )
        numbers = (first_head + jnp.arange(local_heads)).astype(F32)
        slope = jnp.broadcast_to((2.0 ** (-8.0 * (numbers + 1.0) / H))[:, None], (local_heads, 128))
        flat = [one.reshape(length, local_width) for one in (query, keys, vals)]
        mlp_sum, weight_sums, resid_low, query_grad, keys_grad, vals_grad, sums_back = back_call(
            n_tensor, second_part, partial_mlp, activ_low, cotangent, second_low, pre_grad, inputs, total,
            vectors[:, :width], output_weight, *flat, logsum.reshape(local_heads, length), slope, off,
        )
        mlp_sum = mlp_sum.reshape(length, width).astype(F32)
        resid_low = resid_low.reshape(length, width)
        hidden_grad = resid_low.astype(F32)
        second_gain_part, second_shift_part, output_bias_part = (
            jnp.sum(sums_back[k], axis=0) for k in range(3)
        )
        pieces = units // 256
        shrink_weight_grad = weight_sums[:pieces].astype(F32).reshape(units, width)
        expand_weight_grad = weight_sums[pieces:].astype(F32).reshape(width, units)
        outputs = (hidden_state + mlp_sum + shrink_bias).astype(BF16)
        output_part = jnp.einsum("tc,td->cd", attended, resid_low, preferred_element_type=F32)
    else:
        shrink_part = jnp.einsum("tf,td->fd", activ_low, cotangent, preferred_element_type=F32)
        expand_part = jnp.einsum("td,tf->df", second_low, pre_grad, preferred_element_type=F32)

        (second_grad, mlp_sum), (shrink_sum, expand_sum) = sums(
            [second_part, partial_mlp],
            [
                shrink_part.reshape(-1, 2, 2, 2, 32, width),
                expand_part.reshape(-1, 2, 2, 2, 32, units),
            ],
            1,
        )
        shrink_weight_grad = shrink_sum.reshape(units, width)
        expand_weight_grad = expand_sum.reshape(width, units)
        outputs = (hidden_state + mlp_sum + shrink_bias).astype(BF16)
        hidden_grad, second_gain_part, second_shift_part = norm_backward(
            hidden_state, second_gain, second_shift, second_grad
        )
        hidden_grad = hidden_grad + upstream
        resid_low = hidden_grad.astype(BF16)
        output_part = jnp.einsum("tc,td->cd", attended, resid_low, preferred_element_type=F32)
        output_bias_part = jnp.sum(resid_low.astype(F32), axis=0)
        attended_grad = (
            jnp.einsum("td,cd->tc", resid_low, output_weight, preferred_element_type=F32)
            .astype(BF16)
            .reshape(length, local_heads, HD)
        )
        probs = jnp.exp(biased_scores(query, keys, blocks, first_head) - logsum)
        probs_low = probs.astype(BF16)
        prob_grad = jnp.einsum("qhd,khd->hqk", attended_grad, vals, preferred_element_type=F32)
        vals_grad = jnp.einsum(
            "hqk,qhd->khd", probs_low, attended_grad, preferred_element_type=F32
        ).astype(BF16)
        row_delta = jnp.sum(probs * prob_grad, axis=-1, keepdims=True)
        score_grad = (probs * (prob_grad - row_delta)).astype(BF16)
        scale_factor = 1.0 / math.sqrt(HD)
        query_grad = (
            jnp.einsum("hqk,khd->qhd", score_grad, keys, preferred_element_type=F32) * scale_factor
        ).astype(BF16)
        keys_grad = (
            jnp.einsum("hqk,qhd->khd", score_grad, query, preferred_element_type=F32) * scale_factor
        ).astype(BF16)
    grads = [one.reshape(length, local_width) for one in (query_grad, keys_grad, vals_grad)]
    mixing_part = jnp.stack(
        [jnp.einsum("td,tc->dc", normed_low, one, preferred_element_type=F32) for one in grads]
    )
    mixing_bias_part = jnp.stack(
        [jnp.sum(grads[0].astype(F32), axis=0), jnp.sum(grads[2].astype(F32), axis=0)]
    )
    normed_part = sum(
        jnp.einsum("tc,dc->td", one, weights[k], preferred_element_type=F32)
        for k, one in enumerate(grads)
    )
    quarters = width // local_width
    (normed_grad,), (mixing_sum, output_sum) = sums(
        [normed_part],
        [
            mixing_part.reshape(-1, 2, 2, 2, 128, local_width),
            output_part.reshape(local_width, quarters, local_width)
            .transpose(1, 0, 2)
            .reshape(-1, 2, 2, 2, 128, local_width),
        ],
        2,
    )
    mixing_weight_grad = mixing_sum.reshape(3, width, local_width).transpose(1, 0, 2)
    output_weight_grad = (
        output_sum.reshape(quarters, local_width, local_width)
        .transpose(1, 0, 2)
        .reshape(local_width, width)
    )
    source_grad, first_gain_part, first_shift_part = norm_backward(
        source, first_gain, first_shift, normed_grad
    )
    input_grad = (source_grad + hidden_grad).astype(BF16)
    small = lax.psum(
        (
            first_gain_part,
            first_shift_part,
            mixing_bias_part,
            output_bias_part,
            second_gain_part,
            second_shift_part,
            expand_bias_part,
            shrink_bias_part,
        ),
        "dp",
    )
    return (
        outputs,
        input_grad,
        small[0],
        small[1],
        mixing_weight_grad,
        small[2],
        output_weight_grad,
        small[3],
        small[4],
        small[5],
        expand_weight_grad,
        small[6],
        shrink_weight_grad,
        small[7],
    )


def solution(mesh):
    in_specs = (
        P("dp", None),
        P("dp", None),
        P(),
        P(),
        P(None, None, "tensor"),
        P(None, "tensor"),
        P("tensor", None),
        P(),
        P(),
        P(),
        P(None, "tensor"),
        P("tensor"),
        P("tensor", None),
        P(),
        P("dp", None),
    )
    out_specs = (
        P("dp", None),
        P("dp", None),
        P(),
        P(),
        P(None, None, "tensor"),
        P(None, "tensor"),
        P("tensor", None),
        P(),
        P(),
        P(),
        P(None, "tensor"),
        P("tensor"),
        P("tensor", None),
        P(),
    )
    n_tensor = mesh.shape["tensor"]
    fast = mesh.shape["dp"] == 8 and n_tensor % 2 == 0
    return jax.shard_map(
        functools.partial(on_device, fast, n_tensor),
        mesh=mesh,
        in_specs=in_specs,
        out_specs=out_specs,
        check_vma=False,
    )
```

```python
import functools
import math

import jax
import jax.numpy as jnp
from jax import lax
from jax.experimental import pallas as pl
from jax.experimental.pallas import tpu as pltpu
from jax.sharding import PartitionSpec as P

H = 32
HD = 64
EPS = 1e-05
F32 = jnp.float32
BF16 = jnp.bfloat16
MESH = pl.DeviceIdType.MESH


def layer_norm(values, scale_gain, shift_bias):
    row_mean = jnp.mean(values, axis=-1, keepdims=True)
    centred = values - row_mean
    row_var = jnp.mean(centred * centred, axis=-1, keepdims=True)
    return centred * lax.rsqrt(row_var + EPS) * scale_gain + shift_bias


def norm_backward(values, scale_gain, shift_bias, upstream):
    _, pull_back = jax.vjp(layer_norm, values, scale_gain, shift_bias)
    return pull_back(upstream)


def gelu_exact(values):
    return jax.nn.gelu(values, approximate=False)


def biased_scores(query, keys, blocks, first_head):
    length, local_heads, head_width = query.shape
    scores = jnp.einsum("qhd,khd->hqk", query, keys, preferred_element_type=F32) * (
        1.0 / math.sqrt(head_width)
    )
    heads_index = (first_head + jnp.arange(local_heads)).astype(F32)
    slopes = 2.0 ** (-8.0 * (heads_index + 1.0) / H)
    places = jnp.arange(length)
    offsets = (places[None, :] - places[:, None]).astype(F32)
    scores = scores + slopes[:, None, None] * offsets[None]
    allowed = blocks[None, :] <= blocks[:, None]
    return jnp.where(allowed[None], scores, -1e30)


def add_rows(dst, src, step):
    rows = dst.shape[0]

    def body(i, carry):
        at = pl.ds(pl.multiple_of(i * step, step), step)
        dst[at, :] = (dst[at, :].astype(F32) + src[at, :].astype(F32)).astype(BF16)
        return carry

    lax.fori_loop(0, rows // step, body, 0)


def remote(src, dst, send, recv, axis, to):
    return pltpu.make_async_remote_copy(
        src_ref=src,
        dst_ref=dst,
        send_sem=send,
        recv_sem=recv,
        device_id={axis: to},
        device_id_type=MESH,
    )


class Chain:
    def __init__(self, n, refs, slack=1):
        self.part, self.outer_in, self.inner_in, self.s_in, self.s_out, self.r_outer, self.r_inner = refs
        i = lax.axis_index("tensor")
        left = i < n // 2
        depth = jnp.where(left, i, n - 1 - i)
        self.inner = jnp.where(left, i + 1, i - 1)
        self.has_outer = depth > 0
        self.outer = jnp.where(self.has_outer, jnp.where(left, i - 1, i + 1), self.inner)
        self.is_mid = depth == n // 2 - 1
        self.first = slack * depth
        self.lag = slack * (n - 1 - depth)
        self.most_lag = slack * (n - 1)

    @staticmethod
    def scratch(count, block):
        dma = pltpu.SemaphoreType.DMA
        return [pltpu.VMEM((count, *block), BF16)] * 3 + [dma((count,))] * 4

    def to_mid(self, k):
        return remote(
            self.part.at[k], self.inner_in.at[k], self.s_in.at[k], self.r_inner.at[k], "tensor", self.inner
        )

    def to_inner(self, k):
        return remote(
            self.part.at[k], self.outer_in.at[k], self.s_in.at[k], self.r_outer.at[k], "tensor", self.inner
        )

    def to_outer(self, k):
        return remote(
            self.inner_in.at[k], self.inner_in.at[k], self.s_out.at[k], self.r_inner.at[k], "tensor", self.outer
        )

    def greet(self, barrier):
        pl.semaphore_signal(barrier, inc=1, device_id={"tensor": self.inner}, device_id_type=MESH)

        @pl.when(self.has_outer)
        def _():
            pl.semaphore_signal(barrier, inc=1, device_id={"tensor": self.outer}, device_id_type=MESH)

    def wait_greetings(self, barrier, others):
        @pl.when(self.has_outer)
        def _():
            pl.semaphore_wait(barrier, others + 2)

        @pl.when(jnp.logical_not(self.has_outer))
        def _():
            pl.semaphore_wait(barrier, others + 1)

    def reduce(self, k):
        @pl.when(self.has_outer)
        def _():
            self.to_inner(k).wait_recv()
            add_rows(self.part.at[k], self.outer_in.at[k], 16)

        @pl.when(self.is_mid)
        def _():
            self.to_mid(k).start()

        @pl.when(jnp.logical_not(self.is_mid))
        def _():
            self.to_inner(k).start()

    def spread(self, k):
        self.to_mid(k).wait_recv()

        @pl.when(self.is_mid)
        def _():
            add_rows(self.inner_in.at[k], self.part.at[k], 16)

        @pl.when(self.has_outer)
        def _():
            self.to_outer(k).start()

    def drain(self, k):
        self.to_mid(k).wait_send()

        @pl.when(self.has_outer)
        def _():
            self.to_outer(k).wait_send()


def between(k, count):
    return jnp.logical_and(k >= 0, k < count)


def head_forward(head, q, k, v, slope, off, tile, attended, lse):
    length = q.shape[0]
    odd = lax.rem(head, 2)
    mask = lane_half(odd).astype(BF16)
    lanes = pl.ds(pl.multiple_of((head // 2) * 2 * HD, 2 * HD), 2 * HD)
    gain = slope[pl.ds(head, 1), 0:1]
    for j in range(length // tile):
        rows = slice(j * tile, (j + 1) * tile)
        most = min(length, (j + 2) * tile)
        scores = lax.dot_general(
            k[0:most, lanes] * mask, q[rows, lanes], (((1,), (1,)), ((), ())), preferred_element_type=F32
        )
        scores = scores * (1.0 / math.sqrt(HD)) + gain * off[0:most, rows]
        top = jnp.max(scores, axis=0, keepdims=True)
        raised = jnp.exp(scores - top)
        total = jnp.sum(raised, axis=0, keepdims=True)
        lse[pl.ds(head, 1), rows] = top + jnp.log(total)
        probs = (raised * (1.0 / total)).astype(BF16)
        got = lax.dot_general(
            v[0:most, lanes] * mask, probs, (((0,), (0,)), ((), ())), preferred_element_type=F32
        )
        mine = got.T.astype(BF16)

        @pl.when(odd == 0)
        def _(rows=rows, mine=mine):
            attended[rows, lanes] = mine

        @pl.when(odd == 1)
        def _(rows=rows, mine=mine):
            attended[rows, lanes] += mine


def head_kernel(heads, *refs):
    (src_h, w_h, vec_h, bias_h, slope_h, blocks_h), refs = refs[:6], refs[6:]
    (normed_h, q_h, k_h, v_h, att_h, lse_h, off_h), refs = refs[:7], refs[7:]
    (src, w, vec, bias, slope, blocks), refs = refs[:6], refs[6:]
    (normed, q, k, v, att, lse, off), refs = refs[:7], refs[7:]
    load, w_load, store = refs
    length, width = src.shape
    loads = [
        pltpu.make_async_copy(a, b, load.at[j])
        for j, (a, b) in enumerate(
            ((src_h, src), (vec_h, vec), (blocks_h, blocks), (bias_h, bias), (slope_h, slope))
        )
    ]
    w_loads = [pltpu.make_async_copy(w_h.at[m], w.at[m], w_load.at[m]) for m in range(3)]
    for one in loads + w_loads:
        one.start()
    for one in loads:
        one.wait()
    step = 16

    def normalize(i, carry):
        at = pl.ds(pl.multiple_of(i * step, step), step)
        value = src[at, :].astype(F32)
        centred = value - jnp.sum(value, axis=-1, keepdims=True) / width
        var = jnp.sum(centred * centred, axis=-1, keepdims=True) / width
        normed[at, :] = (centred * lax.rsqrt(var + EPS) * vec[0:1, :] + vec[1:2, :]).astype(BF16)
        return carry

    lax.fori_loop(0, length // step, normalize, 0)

    here = blocks[...].astype(F32)
    there = jnp.broadcast_to(here, (8, length)).T[:, 0:1]
    for j in range(length // 256):
        cols = slice(j * 256, (j + 1) * 256)
        distance = (
            lax.broadcasted_iota(jnp.int32, (length, 256), 0)
            - lax.broadcasted_iota(jnp.int32, (length, 256), 1)
            - j * 256
        ).astype(F32)
        off[:, cols] = jnp.where(there <= here[:, cols], distance, -1e30)

    for m, to in enumerate((q, k, v)):
        w_loads[m].wait()

        def project(i, carry, m=m, to=to):
            at = pl.ds(pl.multiple_of(i * 256, 256), 256)
            to[at, :] = (
                jnp.dot(normed[at, :], w[m], preferred_element_type=F32) + bias[m : m + 1, :]
            ).astype(BF16)
            return carry

        lax.fori_loop(0, length // 256, project, 0)

    stores = [
        pltpu.make_async_copy(a, b, store.at[j])
        for j, (a, b) in enumerate(
            ((normed, normed_h), (off, off_h), (q, q_h), (k, k_h), (v, v_h), (att, att_h), (lse, lse_h))
        )
    ]
    for one in stores[:5]:
        one.start()

    def attend(head, carry):
        head_forward(head, q, k, v, slope, off, HEAD_TILE, att, lse)
        return carry

    lax.fori_loop(0, heads, attend, 0)
    for one in stores[5:]:
        one.start()
    for one in stores:
        one.wait()


def head_call(src, w, vec, bias, slope, blocks):
    length, width = src.shape
    local = w.shape[2]
    heads = local // HD
    inputs = (src, w, vec, bias, slope, blocks)
    shapes = [
        ((length, width), BF16),
        *[((length, local), BF16)] * 4,
        ((heads, length), F32),
        ((length, length), F32),
    ]
    dma = pltpu.SemaphoreType.DMA
    return pl.pallas_call(
        functools.partial(head_kernel, heads),
        out_shape=[jax.ShapeDtypeStruct(*one) for one in shapes],
        in_specs=[pl.BlockSpec(memory_space=pl.ANY)] * len(inputs),
        out_specs=[pl.BlockSpec(memory_space=pl.ANY)] * len(shapes),
        scratch_shapes=[
            *[pltpu.VMEM(one.shape, one.dtype) for one in inputs],
            *[pltpu.VMEM(*one) for one in shapes],
            dma((5,)),
            dma((3,)),
            dma((7,)),
        ],
        compiler_params=pltpu.CompilerParams(vmem_limit_bytes=60 << 20),
    )(*inputs)


ROWS = 32
SLACK = 2
BLOCK_ROWS = 256
TILE = 512


def mlp_kernel(n, length, *refs):
    (att_h, wo_h, src_h, dy_h, wu_h, wd_h, vec_h), refs = refs[:7], refs[7:]
    (tot_h, second_h, activ_h, pre_h, mlp_h, grad_h, bias_h), refs = refs[:7], refs[7:]
    (att, wo, src, dy, wu, wd, vec, second, activ, pre, mlp, grad, bias), refs = refs[:13], refs[13:]
    load, store, tot_store, *refs = refs
    chain = Chain(n, refs, SLACK)
    width = wo.shape[1]
    units = wu.shape[1]
    chunks = length // ROWS
    blocks = length // BLOCK_ROWS
    per_block = BLOCK_ROWS // ROWS
    group = 4

    loads = [
        pltpu.make_async_copy(a, b, load.at[k])
        for k, (a, b) in enumerate(
            ((att_h, att), (wo_h, wo), (vec_h, vec), (src_h, src), (wu_h, wu), (dy_h, dy), (wd_h, wd))
        )
    ]
    for one in loads:
        one.start()
    barrier = pltpu.get_barrier_semaphore()
    chain.greet(barrier)
    bias[...] = jnp.zeros_like(bias)
    chain.wait_greetings(barrier, 0)
    for one in loads[:3]:
        one.wait()

    def tot_copy(k):
        return pltpu.make_async_copy(chain.inner_in.at[k], tot_h.at[k], tot_store.at[k])

    def block_copies(b):
        at = pl.ds(pl.multiple_of(b * BLOCK_ROWS, BLOCK_ROWS), BLOCK_ROWS)
        pairs = ((second, second_h), (activ, activ_h), (pre, pre_h), (mlp, mlp_h), (grad, grad_h))
        return [
            pltpu.make_async_copy(a.at[at], h.at[at], store.at[b, j]) for j, (a, h) in enumerate(pairs)
        ]

    def produce(g):
        rows = group * ROWS
        left = att[pl.ds(pl.multiple_of(g * rows, rows), rows), :]
        for j in range(width // 512):
            cols = pl.ds(j * 512, 512)
            got = jnp.dot(left, wo[:, cols], preferred_element_type=F32).astype(BF16)
            for q in range(group):
                chain.part[g * group + q, :, cols] = got[q * ROWS : (q + 1) * ROWS]

    def normalize(b):
        step = 16

        def body(i, carry):
            at = pl.ds(pl.multiple_of(b * BLOCK_ROWS + i * step, step), step)
            k = b * per_block + i // (ROWS // step)
            inside = pl.ds(pl.multiple_of((i % (ROWS // step)) * step, step), step)
            value = src[at, :].astype(F32) + (chain.inner_in[k, inside, :].astype(F32) + vec[0:1, :width])
            centred = value - jnp.mean(value, axis=-1, keepdims=True)
            var = jnp.mean(centred * centred, axis=-1, keepdims=True)
            second[at, :] = (
                centred * lax.rsqrt(var + EPS) * vec[1:2, :width] + vec[2:3, :width]
            ).astype(BF16)
            return carry

        lax.fori_loop(0, BLOCK_ROWS // step, body, 0)

    def hidden_tile(b, j):
        at = pl.ds(pl.multiple_of(b * BLOCK_ROWS, BLOCK_ROWS), BLOCK_ROWS)
        cols = pl.ds(pl.multiple_of(j * TILE, TILE), TILE)
        value = jnp.dot(second[at, :], wu[:, cols], preferred_element_type=F32) + vec[3:4, cols]
        back = lax.dot_general(
            dy[at, :], wd[cols, :], (((1,), (1,)), ((), ())), preferred_element_type=F32
        )
        below = 0.5 + 0.5 * lax.erf(value * math.sqrt(0.5))
        density = jnp.exp(-0.5 * value * value) * (1.0 / math.sqrt(2.0 * math.pi))
        activ[at, cols] = (value * below).astype(BF16)
        low = (back * (below + value * density)).astype(BF16)
        pre[at, cols] = low
        bias[:, cols] += jnp.sum(low.astype(F32).reshape(BLOCK_ROWS // 8, 8, TILE), axis=0)

    def out_tile(b, j):
        at = pl.ds(pl.multiple_of(b * BLOCK_ROWS, BLOCK_ROWS), BLOCK_ROWS)
        cols = pl.ds(pl.multiple_of(j * TILE, TILE), TILE)
        mlp[at, cols] = jnp.dot(activ[at, :], wd[:, cols], preferred_element_type=F32).astype(BF16)
        grad[at, cols] = lax.dot_general(
            pre[at, :], wu[cols, :], (((1,), (1,)), ((), ())), preferred_element_type=F32
        ).astype(BF16)

    ahead = units // TILE
    steps = ahead + width // TILE
    per_tick = -(-steps // per_block)
    first_tick = per_block + chain.most_lag

    def tick(t, carry):
        @pl.when(jnp.logical_and(t % group == 0, t < chunks))
        def _():
            produce(t // group)

        ready = t - chain.first

        @pl.when(between(ready, chunks))
        def _():
            chain.reduce(ready)

        back = t - chain.lag

        @pl.when(between(back, chunks))
        def _():
            chain.spread(back)
            tot_copy(back).start()

        late = t - first_tick

        @pl.when(late == 0)
        def _():
            for one in loads[3:]:
                one.wait()

        @pl.when(between(late, blocks * per_block))
        def _():
            b = late // per_block
            for q in range(per_tick):
                s = (late % per_block) * per_tick + q

                @pl.when(s == 0)
                def _():
                    normalize(b)

                @pl.when(s < ahead)
                def _():
                    hidden_tile(b, s)

                @pl.when(between(s - ahead, width // TILE))
                def _():
                    out_tile(b, s - ahead)

                @pl.when(s == steps - 1)
                def _():
                    for one in block_copies(b):
                        one.start()

        return carry

    lax.fori_loop(0, chunks + first_tick, tick, 0)
    bias_copy = pltpu.make_async_copy(bias, bias_h, load.at[0])
    bias_copy.start()

    def drain(k, carry):
        chain.drain(k)
        tot_copy(k).wait()
        return carry

    lax.fori_loop(0, chunks, drain, 0)
    for b in range(blocks):
        for one in block_copies(b):
            one.wait()
    bias_copy.wait()


def mlp_call(n, att, wo, src, dy, wu, wd, vec):
    length, width = src.shape
    units = wu.shape[1]
    chunks = length // ROWS
    dma = pltpu.SemaphoreType.DMA
    inputs = (att, wo, src, dy, wu, wd, vec)
    outs = [(chunks, ROWS, width), (length, width), (length, units), (length, units)]
    outs += [(length, width), (length, width)]
    out_shape = [jax.ShapeDtypeStruct(one, BF16) for one in outs] + [jax.ShapeDtypeStruct((8, units), F32)]
    scratch = [pltpu.VMEM(one.shape, one.dtype) for one in inputs]
    scratch += [pltpu.VMEM(one.shape, one.dtype) for one in out_shape[1:]]
    scratch += [dma((7,)), dma((length // BLOCK_ROWS, 5)), dma((chunks,))]
    scratch += Chain.scratch(chunks, (ROWS, width))
    return pl.pallas_call(
        functools.partial(mlp_kernel, n, length),
        out_shape=out_shape,
        in_specs=[pl.BlockSpec(memory_space=pl.ANY)] * len(inputs),
        out_specs=[pl.BlockSpec(memory_space=pl.ANY)] * len(out_shape),
        scratch_shapes=scratch,
        compiler_params=pltpu.CompilerParams(
            collective_id=0, has_side_effects=True, vmem_limit_bytes=60 << 20
        ),
    )(*inputs)


class Ring:
    def __init__(self, n, refs, slots, slack):
        self.chain = Chain(n, refs, slack)
        self.slots = slots
        self.gone = self.chain.most_lag + 2

    def at(self, k):
        return lax.rem(k, self.slots)

    def reduce(self, k):
        self.chain.reduce(self.at(k))

    def spread(self, k):
        self.chain.spread(self.at(k))

    def retire(self, k):
        self.chain.drain(self.at(k))


class Cube:
    def __init__(self, refs, keep, step, apart=1):
        (self.fin, self.give, self.c0, self.r1, self.r2), refs = refs[:5], refs[5:]
        self.s0, self.q0, self.s1, self.q1, self.s2, self.q2, self.s3, self.q3, self.s4, self.q4, self.kept = refs
        self.keep_of, self.step, self.apart = keep, step, apart
        self.gone = 6 * apart
        self.slots = self.gone + 1
        d = lax.axis_index("dp")
        self.c, self.x, self.y = d % 2, (d // 2) % 2, d // 4
        self.to_c, self.to_x, self.to_y = d + 1 - 2 * self.c, d + 2 - 4 * self.x, d + 4 - 8 * self.y
        self.stages = (self.stage1, self.stage2, self.stage3, self.stage4, self.stage5, self.retire)

    @classmethod
    def scratch(cls, block, apart=1):
        dma, n = pltpu.SemaphoreType.DMA, 6 * apart + 1
        return [
            pltpu.VMEM((n, 2, 2, 2, *block), BF16),
            pltpu.VMEM((n, 2, 2, *block), BF16),
            pltpu.VMEM((n, 2, 2, *block), BF16),
            pltpu.VMEM((n, 2, *block), BF16),
            pltpu.VMEM((n, 2, *block), BF16),
            *[dma((n,))] * 2,
            *[dma((n, 2))] * 6,
            *[dma((n,))] * 3,
        ]

    def greet(self, barrier):
        for to in (self.to_c, self.to_x, self.to_y):
            pl.semaphore_signal(barrier, inc=1, device_id={"dp": to}, device_id_type=MESH)

    def slot(self, k):
        return lax.rem(k, self.slots)

    def half(self, k):
        p = self.slot(k)
        return remote(self.give.at[p], self.c0.at[p], self.s0.at[p], self.q0.at[p], "dp", self.to_c)

    def quarters(self, p):
        return self.fin.at[p, self.c, 0, self.x], self.fin.at[p, self.c, 1, self.y]

    def hop1(self, k):
        p, fin, c = self.slot(k), self.fin, self.c
        return (
            remote(fin.at[p, c, 0, 1 - self.x], self.r1.at[p, 0], self.s1.at[p, 0], self.q1.at[p, 0], "dp", self.to_x),
            remote(fin.at[p, c, 1, 1 - self.y], self.r1.at[p, 1], self.s1.at[p, 1], self.q1.at[p, 1], "dp", self.to_y),
        )

    def hop2(self, k):
        p = self.slot(k)
        a, b = self.quarters(p)
        return (
            remote(a, self.r2.at[p, 0], self.s2.at[p, 0], self.q2.at[p, 0], "dp", self.to_y),
            remote(b, self.r2.at[p, 1], self.s2.at[p, 1], self.q2.at[p, 1], "dp", self.to_x),
        )

    def hop3(self, k):
        p = self.slot(k)
        a, b = self.quarters(p)
        return (
            remote(a, a, self.s3.at[p, 0], self.q3.at[p, 0], "dp", self.to_x),
            remote(b, b, self.s3.at[p, 1], self.q3.at[p, 1], "dp", self.to_y),
        )

    def hop4(self, k):
        p = self.slot(k)
        mine = self.fin.at[p, self.c]
        return remote(mine, mine, self.s4.at[p], self.q4.at[p], "dp", self.to_c)

    def kept_wait(self, k):
        p = self.slot(k)
        pltpu.make_async_copy(self.fin.at[p], self.fin.at[p], self.kept.at[p]).wait()

    def add_quarters(self, k, got):
        p = self.slot(k)
        for j, quarter in enumerate(self.quarters(p)):
            add_rows(quarter, got.at[p, j], self.step)

    def stage1(self, k):
        self.half(k).wait()
        p = self.slot(k)
        for a in range(2):
            for b in range(2):
                add_rows(self.fin.at[p, self.c, a, b], self.c0.at[p, a, b], self.step)
        for one in self.hop1(k):
            one.start()

    def stage2(self, k):
        for one in self.hop1(k):
            one.wait()
        self.add_quarters(k, self.r1)
        for one in self.hop2(k):
            one.start()

    def stage3(self, k):
        for one in self.hop2(k):
            one.wait()
        self.add_quarters(k, self.r2)
        for one in self.hop3(k):
            one.start()

    def stage4(self, k):
        for one in self.hop3(k):
            one.wait_recv()
        self.hop4(k).start()

    def stage5(self, k):
        self.hop4(k).wait_recv()
        p = self.slot(k)
        self.keep_of(k, self.fin.at[p], self.kept.at[p])

    def retire(self, k):
        for one in self.hop3(k) + (self.hop4(k),):
            one.wait_send()
        self.kept_wait(k)

    def tick(self, t, count):
        for late, stage in reversed(tuple(enumerate(self.stages, 1))):
            k = t - late * self.apart

            @pl.when(between(k, count))
            def _(stage=stage, k=k):
                stage(k)


def weighted(left, right):
    return lax.dot_general(left, right, (((0,), (0,)), ((), ())), preferred_element_type=F32).astype(BF16)


def lane_half(odd):
    return (lax.broadcasted_iota(jnp.int32, (1, 2 * HD), 1) // HD == odd).astype(F32)


def head_backward(head, q, k, v, up, lse, slope, off, tile, grads, acc):
    q_grad, k_grad, v_grad = grads
    k_acc, v_acc = acc
    length = q.shape[0]
    odd = lax.rem(head, 2)
    mask = lane_half(odd).astype(BF16)
    lanes = pl.ds(pl.multiple_of((head // 2) * 2 * HD, 2 * HD), 2 * HD)
    scale = 1.0 / math.sqrt(HD)
    gain = slope[pl.ds(head, 1), 0:1]
    nt = (((1,), (1,)), ((), ()))
    for j in range(length // tile):
        rows = slice(j * tile, (j + 1) * tile)
        most = min(length, (j + 2) * tile)
        q_here = q[rows, lanes]
        up_here = up[rows, lanes] * mask
        k_here = k[0:most, lanes] * mask
        scores = lax.dot_general(k_here, q_here, nt, preferred_element_type=F32)
        probs = jnp.exp(scores * scale + gain * off[0:most, rows] - lse[pl.ds(head, 1), rows])
        back = lax.dot_general(v[0:most, lanes], up_here, nt, preferred_element_type=F32)
        delta = jnp.sum(probs * back, axis=0, keepdims=True)
        score_grad = (probs * (back - delta)).astype(BF16)
        v_part = jnp.dot(probs.astype(BF16), up_here, preferred_element_type=F32)
        k_part = jnp.dot(score_grad, q_here * mask, preferred_element_type=F32)
        if j == 0:
            v_acc[0:most, :] = v_part
            k_acc[0:most, :] = k_part
            if most < length:
                v_acc[most:length, :] = jnp.zeros((length - most, 2 * HD), F32)
                k_acc[most:length, :] = jnp.zeros((length - most, 2 * HD), F32)
        else:
            v_acc[0:most, :] += v_part
            k_acc[0:most, :] += k_part
        q_part = lax.dot_general(k_here, score_grad, (((0,), (0,)), ((), ())), preferred_element_type=F32)
        mine = (q_part.T * scale).astype(BF16)

        @pl.when(odd == 0)
        def _(rows=rows, mine=mine):
            q_grad[rows, lanes] = mine

        @pl.when(odd == 1)
        def _(rows=rows, mine=mine):
            q_grad[rows, lanes] += mine

    for to, got, factor in ((k_grad, k_acc, scale), (v_grad, v_acc, 1.0)):

        @pl.when(odd == 0)
        def _(to=to, got=got, factor=factor):
            to[:, lanes] = (got[...] * factor).astype(BF16)

        @pl.when(odd == 1)
        def _(to=to, got=got, factor=factor):
            to[:, lanes] += (got[...] * factor).astype(BF16)


BACK_ROWS = 48
BACK_SLOTS = 12
BACK_SLACK = 2
BACK_APART = 2
BACK_COLUMNS = 1024
HEAD_TILE = 256


def back_kernel(n, heads, *refs):
    (grad_h, mlp_h, activ_h, dy_h, second_h, pre_h, src_h, tot_h), refs = refs[:8], refs[8:]
    smalls_h, refs = refs[:8], refs[8:]
    (sum_h, g_out, resid_h, grads_h, cols_h), refs = refs[:5], refs[5:]
    (left, dy, pre, src, tot, resid), refs = refs[:6], refs[6:]
    smalls, refs = refs[:8], refs[8:]
    vec, wo, q, k, v, lse, slope, off = smalls
    (up, qg, kg, vg, k_acc, v_acc, cols), refs = refs[:7], refs[7:]
    (load, left_sem, part_sem, row_sem, resid_sem, sum_sem), refs = refs[:6], refs[6:]
    ring, refs = Ring(n, refs[:7], BACK_SLOTS, BACK_SLACK), refs[7:]
    chain = ring.chain

    per_row = dy_h.shape[1] // BACK_COLUMNS

    def keep(k, piece_ref, sem):
        here = pl.ds(pl.multiple_of(lax.rem(k, per_row) * BACK_COLUMNS, BACK_COLUMNS), BACK_COLUMNS)
        pltpu.make_async_copy(piece_ref, g_out.at[k // per_row, :, :, :, :, here], sem).start()

    cube = Cube(refs, keep, 32, BACK_APART)
    width, units = dy.shape[1], pre.shape[1]
    rows, per_sum = BACK_ROWS, grad_h.shape[0]
    total_z = 2 * per_sum
    piece = 256
    first = activ_h.shape[1] // piece
    total_left = first + second_h.shape[1] // piece
    total_p = total_left * per_row

    loads = [pltpu.make_async_copy(a, b, load.at[j]) for j, (a, b) in enumerate(zip(smalls_h, smalls))]
    loads += [pltpu.make_async_copy(dy_h, dy, load.at[8]), pltpu.make_async_copy(pre_h, pre, load.at[9])]

    def part_load(j, which):
        return pltpu.make_async_copy(
            (grad_h, mlp_h)[which].at[lax.rem(j, per_sum)], chain.part.at[ring.at(j)], part_sem.at[ring.at(j)]
        )

    def part_start(j):
        @pl.when(j < per_sum)
        def _():
            part_load(j, 0).start()

        @pl.when(between(j - per_sum, per_sum))
        def _():
            part_load(j, 1).start()

    def left_load(p, which):
        at = (p - which * first) * piece
        return pltpu.make_async_copy(
            (activ_h, second_h)[which].at[:, pl.ds(pl.multiple_of(at, piece), piece)],
            left.at[lax.rem(p, 2)],
            left_sem.at[lax.rem(p, 2)],
        )

    def left_start(p):
        @pl.when(p < first)
        def _():
            left_load(p, 0).start()

        @pl.when(between(p - first, total_left - first))
        def _():
            left_load(p, 1).start()

    def row_loads(j):
        at = lax.rem(j, 2)
        return (
            pltpu.make_async_copy(src_h.at[j], src.at[at], row_sem.at[at, 0]),
            pltpu.make_async_copy(tot_h.at[j], tot.at[at], row_sem.at[at, 1]),
        )

    def resid_store(j):
        at = lax.rem(j, 2)
        return pltpu.make_async_copy(resid.at[at], resid_h.at[j], resid_sem.at[at])

    def sum_store(j):
        at = ring.at(j)
        return pltpu.make_async_copy(chain.inner_in.at[at], sum_h.at[j - per_sum], sum_sem.at[at])

    part_start(0)
    left_start(0)
    loads[8].start()
    part_start(1)
    for one in loads[:8] + loads[9:]:
        one.start()
    barrier = pltpu.get_barrier_semaphore()
    chain.greet(barrier)
    cube.greet(barrier)
    cols[...] = jnp.zeros_like(cols)
    chain.wait_greetings(barrier, 3)
    loads[8].wait()

    def produce(p):
        r, part = p // per_row, lax.rem(p, per_row)
        at = lax.rem(r, 2)
        to = cube.slot(p)

        @pl.when(part == 0)
        def _():
            left_start(r + 1)
            pltpu.make_async_copy(activ_h.at[:, pl.ds(0, piece)], left.at[at], left_sem.at[at]).wait()

        mine, theirs = cube.c, 1 - cube.c
        count = piece // 8

        def product(right):
            for side, store in ((theirs, cube.give.at[to]), (mine, cube.fin.at[to, cube.c])):
                rows_of = left[at, :, pl.ds(pl.multiple_of(side * (piece // 2), piece // 2), piece // 2)]
                for j in range(BACK_COLUMNS // 512):
                    from_here = pl.ds(pl.multiple_of(part * BACK_COLUMNS + j * 512, 512), 512)
                    got = weighted(rows_of, right[:, from_here])
                    for a in range(2):
                        for b in range(2):
                            lo = (2 * a + b) * count
                            store[a, b, :, j * 512 : (j + 1) * 512] = got[lo : lo + count]

        @pl.when(r < first)
        def _():
            product(dy)

        @pl.when(r >= first)
        def _():
            product(pre)

        cube.half(p).start()

    def row_sum(x):
        return jnp.sum(x, axis=-1, keepdims=True)

    def rows_back(j):
        for one in row_loads(j):
            one.wait()
        at, got = lax.rem(j, 2), ring.at(j)
        step = 16

        def body(i, carry):
            here = pl.ds(pl.multiple_of(i * step, step), step)
            value = src[at, here, :].astype(F32) + (tot[at, here, :].astype(F32) + vec[0:1, :])
            centred = value - row_sum(value) / width
            spread = lax.rsqrt(row_sum(centred * centred) / width + EPS)
            normal = centred * spread
            down = chain.inner_in[got, here, :].astype(F32)
            scaled = down * vec[1:2, :]
            flat, slope_of = row_sum(scaled) / width, row_sum(scaled * normal) / width
            back = spread * (scaled - flat - normal * slope_of)
            all_rows = pl.ds(pl.multiple_of(j * rows + i * step, step), step)
            low = (back + dy[all_rows, :].astype(F32)).astype(BF16)
            resid[at, here, :] = low
            for c, item in enumerate((down * normal, down, low.astype(F32))):
                cols[c] += item[0:8] + item[8:16]
            return carry

        lax.fori_loop(0, rows // step, body, 0)
        all_rows = pl.ds(pl.multiple_of(j * rows, rows), rows)
        up[all_rows, :] = lax.dot_general(
            resid[at], wo[...], (((1,), (1,)), ((), ())), preferred_element_type=F32
        ).astype(BF16)
        resid_store(j).start()

    def tick(t, carry):
        gone = t - ring.gone

        @pl.when(between(gone, total_z))
        def _():
            ring.retire(gone)

            @pl.when(gone >= per_sum)
            def _():
                sum_store(gone).wait()

        part_start(t + 2)
        ready = t - chain.first

        @pl.when(between(ready, total_z))
        def _():
            part_load(ready, 0).wait()
            ring.reduce(ready)

        back = t - chain.lag

        @pl.when(between(back, total_z))
        def _():
            ring.spread(back)

            @pl.when(back >= per_sum)
            def _():
                sum_store(back).start()

        cube.tick(t, total_p)

        @pl.when(t == 2)
        def _():
            for one in loads[:8] + loads[9:]:
                one.wait()

        @pl.when(t < total_p)
        def _():
            produce(t)

        chunk = t - chain.most_lag - 1

        @pl.when(between(chunk + 1, per_sum))
        def _():
            for one in row_loads(chunk + 1):
                one.start()

        @pl.when(between(chunk - 2, per_sum))
        def _():
            resid_store(chunk - 2).wait()

        @pl.when(between(chunk, per_sum))
        def _():
            rows_back(chunk)

        head = t - chain.most_lag - 1 - per_sum

        @pl.when(between(head, heads))
        def _():
            head_backward(head, q, k, v, up, lse, slope, off, HEAD_TILE, (qg, kg, vg), (k_acc, v_acc))

        return carry

    ticks = max(total_z + ring.gone, total_p + cube.gone, chain.most_lag + 1 + per_sum + max(heads, 2))
    lax.fori_loop(0, ticks, tick, 0)
    stores = [
        pltpu.make_async_copy(a, b, load.at[j])
        for j, (a, b) in enumerate(((qg, grads_h.at[0]), (kg, grads_h.at[1]), (vg, grads_h.at[2]), (cols, cols_h)))
    ]
    for one in stores:
        one.start()
    for one in stores:
        one.wait()


def back_call(n, grad, mlp, activ, dy, second, pre, src, tot, vec, wo, q, k, v, lse, slope, off):
    length, width = dy.shape
    chunks = length // BACK_ROWS
    dma = pltpu.SemaphoreType.DMA

    def cut(one):
        return one.reshape(chunks, BACK_ROWS, one.shape[-1])

    smalls = (vec, wo, q, k, v, lse, slope, off)
    inputs = (cut(grad), cut(mlp), activ, dy, second, pre, cut(src), cut(tot), *smalls)
    tiles = (activ.shape[1] + second.shape[1]) // 256
    shapes = [
        ((chunks, BACK_ROWS, width), BF16),
        ((tiles, 2, 2, 2, 32, width), BF16),
        ((chunks, BACK_ROWS, width), BF16),
        ((3, *q.shape), BF16),
        ((3, 8, width), F32),
    ]
    slots = BACK_SLOTS
    scratch = [
        pltpu.VMEM((2, length, 256), BF16),
        pltpu.VMEM(dy.shape, BF16),
        pltpu.VMEM(pre.shape, BF16),
        *[pltpu.VMEM((2, BACK_ROWS, width), BF16)] * 3,
        *[pltpu.VMEM(one.shape, one.dtype) for one in smalls],
        *[pltpu.VMEM(q.shape, BF16)] * 4,
        *[pltpu.VMEM((length, 2 * HD), F32)] * 2,
        pltpu.VMEM((3, 8, width), F32),
        dma((10,)),
        dma((2,)),
        dma((slots,)),
        dma((2, 2)),
        dma((2,)),
        dma((slots,)),
        *Chain.scratch(slots, (BACK_ROWS, width)),
        *Cube.scratch((32, BACK_COLUMNS), BACK_APART),
    ]
    return pl.pallas_call(
        functools.partial(back_kernel, n, q.shape[1] // HD),
        out_shape=[jax.ShapeDtypeStruct(*one) for one in shapes],
        in_specs=[pl.BlockSpec(memory_space=pl.ANY)] * len(inputs),
        out_specs=[pl.BlockSpec(memory_space=pl.ANY)] * len(shapes),
        scratch_shapes=scratch,
        compiler_params=pltpu.CompilerParams(
            collective_id=1, has_side_effects=True, vmem_limit_bytes=60 << 20
        ),
    )(*inputs)


FRONT_ROWS = 48


def front_kernel(n, *refs):
    (grads_h, w_h, normed_h, att_h, resid_h, src_h, gain_h, small_h), refs = refs[:8], refs[8:]
    (mix_out, wo_out, input_h, small_out), refs = refs[:4], refs[4:]
    (grads, w, normed, att, resid, src, gain, cols, buf, got), refs = refs[:10], refs[10:]
    (load, row_sem, ss, sq), refs = refs[:4], refs[4:]
    chain, refs = Chain(n, refs[:7], FRONT_SLACK), refs[7:]
    length, width = src.shape
    local = att.shape[1]
    blocks = width // local
    rows = FRONT_ROWS
    chunks = length // rows
    group = 4
    total_p = 4 * blocks

    def keep(k, piece_ref, sem):
        @pl.when(k < blocks)
        def _():
            at = pl.ds(pl.multiple_of(k * local, local), local)
            pltpu.make_async_copy(piece_ref, wo_out.at[:, :, :, :, at], sem).start()

        @pl.when(k >= blocks)
        def _():
            pltpu.make_async_copy(piece_ref, mix_out.at[k - blocks], sem).start()

    cube = Cube(refs, keep, 32, FRONT_APART)

    pairs = (
        (grads_h, grads), (w_h, w), (att_h, att), (resid_h, resid), (normed_h, normed), (src_h, src),
        (gain_h, gain), (small_h, buf.at[0]),
    )
    loads = [pltpu.make_async_copy(a, b, load.at[j]) for j, (a, b) in enumerate(pairs)]
    for one in loads:
        one.start()
    barrier = pltpu.get_barrier_semaphore()
    chain.greet(barrier)
    cube.greet(barrier)
    cols[...] = jnp.zeros_like(cols)
    chain.wait_greetings(barrier, 3)
    for one in loads[:2]:
        one.wait()

    def produce_rows(g):
        at = pl.ds(pl.multiple_of(g * group * rows, group * rows), group * rows)
        for j in range(width // 512):
            here = pl.ds(j * 512, 512)
            total = sum(
                lax.dot_general(
                    grads[m, at, :], w[m, here, :], (((1,), (1,)), ((), ())), preferred_element_type=F32
                )
                for m in range(3)
            ).astype(BF16)
            for q in range(group):
                chain.part[g * group + q, :, here] = total[q * rows : (q + 1) * rows]

    half = local // 2
    count = half // 4

    def put(to, side, value):
        for a in range(2):
            for b in range(2):
                lo = (2 * a + b) * count
                to[a, b] = value[lo : lo + count]

    def produce(p):
        slot = cube.slot(p)
        for side, to in ((1 - cube.c, cube.give.at[slot]), (cube.c, cube.fin.at[slot, cube.c])):

            @pl.when(p < blocks)
            def _(side=side, to=to):
                left = att[:, pl.ds(pl.multiple_of(side * half, half), half)]
                right = resid[:, pl.ds(pl.multiple_of(p * local, local), local)]
                put(to, side, weighted(left, right))

            @pl.when(p >= blocks)
            def _(side=side, to=to):
                m, r = p // blocks - 1, lax.rem(p, blocks)
                left = normed[:, pl.ds(pl.multiple_of(r * local + side * half, half), half)]
                put(to, side, weighted(left, grads[m]))

        cube.half(p).start()

    def row_sum(x):
        return jnp.sum(x, axis=-1, keepdims=True)

    def row_store(j):
        at = pl.ds(pl.multiple_of(j * rows, rows), rows)
        return pltpu.make_async_copy(src.at[at], input_h.at[at], row_sem.at[j])

    def rows_back(j):
        step = 16

        def body(i, carry):
            here = pl.ds(pl.multiple_of(i * step, step), step)
            at = pl.ds(pl.multiple_of(j * rows + i * step, step), step)
            value = src[at, :].astype(F32)
            centred = value - row_sum(value) / width
            spread = lax.rsqrt(row_sum(centred * centred) / width + EPS)
            normal = centred * spread
            down = chain.inner_in[j, here, :].astype(F32)
            scaled = down * gain[0:1, :]
            flat, slope_of = row_sum(scaled) / width, row_sum(scaled * normal) / width
            back = spread * (scaled - flat - normal * slope_of)
            src[at, :] = (back + resid[at, :].astype(F32)).astype(BF16)
            for c, item in enumerate((down * normal, down)):
                cols[c] += item[0:8] + item[8:16]
            return carry

        lax.fori_loop(0, rows // step, body, 0)
        row_store(j).start()

    def swap(j):
        to = (cube.to_c, cube.to_x, cube.to_y)[j]
        return remote(buf.at[j], got.at[j], ss.at[j], sq.at[j], "dp", to)

    def small_step(j):
        if j == 0:
            for c in range(2):
                buf[0, c : c + 1, :] = jnp.sum(cols[c], axis=0, keepdims=True)
        else:
            swap(j - 1).wait()
            buf[j] = buf[j - 1] + got[j - 1]
        if j < 3:
            swap(j).start()

    late = chain.most_lag + 1

    def tick(t, carry):
        @pl.when(jnp.logical_and(lax.rem(t, group) == 0, t < chunks))
        def _():
            produce_rows(t // group)

        ready = t - chain.first

        @pl.when(between(ready, chunks))
        def _():
            chain.reduce(ready)

        back = t - chain.lag

        @pl.when(between(back, chunks))
        def _():
            chain.spread(back)

        cube.tick(t, total_p)

        @pl.when(t == 0)
        def _():
            for one in loads[2:4]:
                one.wait()

        @pl.when(t == 2)
        def _():
            for one in loads[4:]:
                one.wait()

        @pl.when(t < total_p)
        def _():
            produce(t)

        @pl.when(between(t - late, chunks))
        def _():
            rows_back(t - late)

        for j in range(4):

            @pl.when(t == late + chunks + j)
            def _(j=j):
                small_step(j)

        return carry

    lax.fori_loop(0, max(chunks + late + 4, total_p + cube.gone), tick, 0)
    small_store = pltpu.make_async_copy(buf.at[3], small_out, load.at[0])
    small_store.start()

    def drain(k, carry):
        chain.drain(k)
        row_store(k).wait()
        return carry

    lax.fori_loop(0, chunks, drain, 0)
    small_store.wait()


FRONT_SLACK = 2
FRONT_APART = 2


def front_call(n, grads, w, normed, att, resid, src, gain, small):
    length, width = src.shape
    local = att.shape[1]
    blocks = width // local
    chunks = length // FRONT_ROWS
    block = (local // 8, local)
    dma = pltpu.SemaphoreType.DMA
    inputs = (grads, w, normed, att, resid, src, gain, small)
    shapes = [
        ((3 * blocks, 2, 2, 2, *block), BF16),
        ((2, 2, 2, local // 8, width), BF16),
        ((length, width), BF16),
        (small.shape, F32),
    ]
    order = (grads, w, normed, att, resid, src, gain)
    scratch = [
        *[pltpu.VMEM(one.shape, one.dtype) for one in order],
        pltpu.VMEM((2, 8, width), F32),
        pltpu.VMEM((4, *small.shape), F32),
        pltpu.VMEM((3, *small.shape), F32),
        dma((8,)),
        dma((chunks,)),
        dma((3,)),
        dma((3,)),
        *Chain.scratch(chunks, (FRONT_ROWS, width)),
        *Cube.scratch(block, FRONT_APART),
    ]
    return pl.pallas_call(
        functools.partial(front_kernel, n),
        out_shape=[jax.ShapeDtypeStruct(*one) for one in shapes],
        in_specs=[pl.BlockSpec(memory_space=pl.ANY)] * len(inputs),
        out_specs=[pl.BlockSpec(memory_space=pl.ANY)] * len(shapes),
        scratch_shapes=scratch,
        compiler_params=pltpu.CompilerParams(
            collective_id=2, has_side_effects=True, vmem_limit_bytes=60 << 20
        ),
    )(*inputs)


def on_device(
    fast,
    n_tensor,
    inputs,
    block_ids,
    first_gain,
    first_shift,
    mixing_weight,
    mixing_bias,
    output_weight,
    output_bias,
    second_gain,
    second_shift,
    expand_weight,
    expand_bias,
    shrink_weight,
    shrink_bias,
    cotangent,
):
    source = inputs.astype(F32)
    upstream = cotangent.astype(F32)
    length, width = source.shape
    blocks = block_ids[0]
    local_width = mixing_weight.shape[2]
    local_heads = local_width // HD
    units = expand_weight.shape[1]
    first_head = lax.axis_index("tensor") * local_heads
    weights = mixing_weight.transpose(1, 0, 2)
    if fast:
        numbers = (first_head + jnp.arange(local_heads)).astype(F32)
        slope = jnp.broadcast_to((2.0 ** (-8.0 * (numbers + 1.0) / H))[:, None], (local_heads, 128))
        bias = jnp.stack([mixing_bias[0], jnp.zeros_like(mixing_bias[0]), mixing_bias[1]])
        normed_low, query, keys, vals, attended, logsum, off = head_call(
            inputs, weights, jnp.stack([first_gain, first_shift]), bias, slope, block_ids
        )
    else:
        normed_low = layer_norm(source, first_gain, first_shift).astype(BF16)

        def project(k):
            return jnp.dot(normed_low, weights[k], preferred_element_type=F32)

        query = (project(0) + mixing_bias[0]).astype(BF16).reshape(length, local_heads, HD)
        keys = project(1).astype(BF16).reshape(length, local_heads, HD)
        vals = (project(2) + mixing_bias[1]).astype(BF16).reshape(length, local_heads, HD)
        masked = biased_scores(query, keys, blocks, first_head)
        row_top = jnp.max(masked, axis=-1, keepdims=True)
        logsum = row_top + jnp.log(jnp.sum(jnp.exp(masked - row_top), axis=-1, keepdims=True))
        probs_low = jnp.exp(masked - logsum).astype(BF16)
        attended = (
            jnp.einsum("hqk,khd->qhd", probs_low, vals, preferred_element_type=F32)
            .reshape(length, local_width)
            .astype(BF16)
        )
    if fast:
        most = max(width, units)
        vectors = jnp.stack(
            [
                jnp.pad(one, (0, most - one.shape[0]))
                for one in (output_bias, second_gain, second_shift, expand_bias)
            ]
        )
        total, second_low, activ_low, pre_grad, partial_mlp, second_part, expand_bias_part = mlp_call(
            n_tensor, attended, output_weight, inputs, cotangent, expand_weight, shrink_weight, vectors
        )
        expand_bias_part = jnp.sum(expand_bias_part, axis=0)
        hidden_state = source + (total.reshape(length, width).astype(F32) + output_bias)
    else:
        partial_out = jnp.dot(attended, output_weight, preferred_element_type=F32)
        resid = lax.psum(partial_out.astype(BF16), "tensor").astype(F32)
        hidden_state = source + (resid + output_bias)
        second_low = layer_norm(hidden_state, second_gain, second_shift).astype(BF16)
        pre_act = jnp.dot(second_low, expand_weight, preferred_element_type=F32) + expand_bias
        activ_low = gelu_exact(pre_act).astype(BF16)
        partial_mlp = jnp.dot(activ_low, shrink_weight, preferred_element_type=F32)
        act_grad = jnp.einsum("td,fd->tf", cotangent, shrink_weight, preferred_element_type=F32)
        _, gelu_pull = jax.vjp(gelu_exact, pre_act)
        pre_grad = gelu_pull(act_grad)[0].astype(BF16)
        expand_bias_part = jnp.sum(pre_grad.astype(F32), axis=0)
        second_part = jnp.einsum("tf,df->td", pre_grad, expand_weight, preferred_element_type=F32)
    shrink_bias_part = jnp.sum(upstream, axis=0)
    if fast:
        mlp_sum, weight_sums, resid_low, grads, sums_back = back_call(
            n_tensor, second_part, partial_mlp, activ_low, cotangent, second_low, pre_grad, inputs, total,
            vectors[:, :width], output_weight, query, keys, vals, logsum, slope, off,
        )
        mlp_sum = mlp_sum.reshape(length, width).astype(F32)
        resid_low = resid_low.reshape(length, width)
        hidden_grad = resid_low.astype(F32)
        second_gain_part, second_shift_part, output_bias_part = (
            jnp.sum(sums_back[k], axis=0) for k in range(3)
        )
        pieces = units // 256
        shrink_weight_grad = weight_sums[:pieces].astype(F32).reshape(units, width)
        expand_weight_grad = weight_sums[pieces:].astype(F32).reshape(width, units)
        outputs = (hidden_state + mlp_sum + shrink_bias).astype(BF16)
    else:
        shrink_part = jnp.einsum("tf,td->fd", activ_low, cotangent, preferred_element_type=F32)
        expand_part = jnp.einsum("td,tf->df", second_low, pre_grad, preferred_element_type=F32)

        mlp_sum = lax.psum(partial_mlp.astype(BF16), "tensor").astype(F32)
        second_grad = lax.psum(second_part.astype(BF16), "tensor").astype(F32)
        outputs = (hidden_state + mlp_sum + shrink_bias).astype(BF16)
        hidden_grad, second_gain_part, second_shift_part = norm_backward(
            hidden_state, second_gain, second_shift, second_grad
        )
        hidden_grad = hidden_grad + upstream
        resid_low = hidden_grad.astype(BF16)
        output_part = jnp.einsum("tc,td->cd", attended, resid_low, preferred_element_type=F32)
        output_bias_part = jnp.sum(resid_low.astype(F32), axis=0)
        attended_grad = (
            jnp.einsum("td,cd->tc", resid_low, output_weight, preferred_element_type=F32)
            .astype(BF16)
            .reshape(length, local_heads, HD)
        )
        probs = jnp.exp(biased_scores(query, keys, blocks, first_head) - logsum)
        probs_low = probs.astype(BF16)
        prob_grad = jnp.einsum("qhd,khd->hqk", attended_grad, vals, preferred_element_type=F32)
        vals_grad = jnp.einsum(
            "hqk,qhd->khd", probs_low, attended_grad, preferred_element_type=F32
        ).astype(BF16)
        row_delta = jnp.sum(probs * prob_grad, axis=-1, keepdims=True)
        score_grad = (probs * (prob_grad - row_delta)).astype(BF16)
        scale_factor = 1.0 / math.sqrt(HD)
        query_grad = (
            jnp.einsum("hqk,khd->qhd", score_grad, keys, preferred_element_type=F32) * scale_factor
        ).astype(BF16)
        keys_grad = (
            jnp.einsum("hqk,qhd->khd", score_grad, query, preferred_element_type=F32) * scale_factor
        ).astype(BF16)
        grads = [one.reshape(length, local_width) for one in (query_grad, keys_grad, vals_grad)]
    mixing_bias_part = jnp.stack(
        [jnp.sum(grads[0].astype(F32), axis=0), jnp.sum(grads[2].astype(F32), axis=0)]
    )
    if fast:
        small = jnp.stack(
            [
                jnp.zeros_like(second_gain_part),
                jnp.zeros_like(second_gain_part),
                second_gain_part,
                second_shift_part,
                output_bias_part,
                expand_bias_part,
                shrink_bias_part,
                jnp.pad(mixing_bias_part.reshape(-1), (0, width - 2 * local_width)),
            ]
        )
        mixing_sum, output_sum, input_grad, small = front_call(
            n_tensor, grads, weights, normed_low, attended, resid_low, inputs,
            first_gain.reshape(1, width), small,
        )
        mixing_weight_grad = mixing_sum.reshape(3, width, local_width).astype(F32).transpose(1, 0, 2)
        output_weight_grad = output_sum.reshape(local_width, width).astype(F32)
        first_gain_grad, first_shift_grad, second_gain_grad, second_shift_grad = small[0], small[1], small[2], small[3]
        output_bias_grad, expand_bias_grad, shrink_bias_grad = small[4], small[5], small[6]
        mixing_bias_grad = small[7, : 2 * local_width].reshape(2, local_width)
    else:
        mixing_part = jnp.stack(
            [jnp.einsum("td,tc->dc", normed_low, one, preferred_element_type=F32) for one in grads]
        )
        normed_part = sum(
            jnp.einsum("tc,dc->td", one, weights[k], preferred_element_type=F32)
            for k, one in enumerate(grads)
        )
        normed_grad = lax.psum(normed_part.astype(BF16), "tensor").astype(F32)
        source_grad, first_gain_part, first_shift_part = norm_backward(
            source, first_gain, first_shift, normed_grad
        )
        input_grad = (source_grad + hidden_grad).astype(BF16)
        summed = lax.psum(
            (
                first_gain_part, first_shift_part, mixing_part, mixing_bias_part, output_part, output_bias_part,
                second_gain_part, second_shift_part, expand_part, expand_bias_part, shrink_part, shrink_bias_part,
            ),
            "dp",
        )
        first_gain_grad, first_shift_grad, mixing_weight_grad, mixing_bias_grad = summed[:4]
        mixing_weight_grad = mixing_weight_grad.transpose(1, 0, 2)
        output_weight_grad, output_bias_grad, second_gain_grad, second_shift_grad = summed[4:8]
        expand_weight_grad, expand_bias_grad, shrink_weight_grad, shrink_bias_grad = summed[8:]
    return (
        outputs,
        input_grad,
        first_gain_grad,
        first_shift_grad,
        mixing_weight_grad,
        mixing_bias_grad,
        output_weight_grad,
        output_bias_grad,
        second_gain_grad,
        second_shift_grad,
        expand_weight_grad,
        expand_bias_grad,
        shrink_weight_grad,
        shrink_bias_grad,
    )


def solution(mesh):
    in_specs = (
        P("dp", None),
        P("dp", None),
        P(),
        P(),
        P(None, None, "tensor"),
        P(None, "tensor"),
        P("tensor", None),
        P(),
        P(),
        P(),
        P(None, "tensor"),
        P("tensor"),
        P("tensor", None),
        P(),
        P("dp", None),
    )
    out_specs = (
        P("dp", None),
        P("dp", None),
        P(),
        P(),
        P(None, None, "tensor"),
        P(None, "tensor"),
        P("tensor", None),
        P(),
        P(),
        P(),
        P(None, "tensor"),
        P("tensor"),
        P("tensor", None),
        P(),
    )
    n_tensor = mesh.shape["tensor"]
    fast = mesh.shape["dp"] == 8 and n_tensor in (2, 4)
    return jax.shard_map(
        functools.partial(on_device, fast, n_tensor),
        mesh=mesh,
        in_specs=in_specs,
        out_specs=out_specs,
        check_vma=False,
    )
```

```python
import functools
import math

import jax
import jax.numpy as jnp
from jax import lax
from jax.experimental import pallas as pl
from jax.experimental.pallas import tpu as pltpu
from jax.sharding import PartitionSpec as P

H = 32
HD = 64
EPS = 1e-05
F32 = jnp.float32
BF16 = jnp.bfloat16
MESH = pl.DeviceIdType.MESH


def layer_norm(values, scale_gain, shift_bias):
    row_mean = jnp.mean(values, axis=-1, keepdims=True)
    centred = values - row_mean
    row_var = jnp.mean(centred * centred, axis=-1, keepdims=True)
    return centred * lax.rsqrt(row_var + EPS) * scale_gain + shift_bias


def norm_backward(values, scale_gain, shift_bias, upstream):
    _, pull_back = jax.vjp(layer_norm, values, scale_gain, shift_bias)
    return pull_back(upstream)


def gelu_exact(values):
    return jax.nn.gelu(values, approximate=False)


def biased_scores(query, keys, blocks, first_head):
    length, local_heads, head_width = query.shape
    scores = jnp.einsum("qhd,khd->hqk", query, keys, preferred_element_type=F32) * (
        1.0 / math.sqrt(head_width)
    )
    heads_index = (first_head + jnp.arange(local_heads)).astype(F32)
    slopes = 2.0 ** (-8.0 * (heads_index + 1.0) / H)
    places = jnp.arange(length)
    offsets = (places[None, :] - places[:, None]).astype(F32)
    scores = scores + slopes[:, None, None] * offsets[None]
    allowed = blocks[None, :] <= blocks[:, None]
    return jnp.where(allowed[None], scores, -1e30)


def add_rows(dst, src, step):
    rows = dst.shape[0]

    def body(i, carry):
        at = pl.ds(pl.multiple_of(i * step, step), step)
        dst[at, :] = (dst[at, :].astype(F32) + src[at, :].astype(F32)).astype(BF16)
        return carry

    lax.fori_loop(0, rows // step, body, 0)


def remote(src, dst, send, recv, axis, to):
    return pltpu.make_async_remote_copy(
        src_ref=src,
        dst_ref=dst,
        send_sem=send,
        recv_sem=recv,
        device_id={axis: to},
        device_id_type=MESH,
    )


class Chain:
    def __init__(self, n, refs, slack=1):
        self.part, self.outer_in, self.inner_in, self.s_in, self.s_out, self.r_outer, self.r_inner = refs
        i = lax.axis_index("tensor")
        left = i < n // 2
        depth = jnp.where(left, i, n - 1 - i)
        self.inner = jnp.where(left, i + 1, i - 1)
        self.has_outer = depth > 0
        self.outer = jnp.where(self.has_outer, jnp.where(left, i - 1, i + 1), self.inner)
        self.is_mid = depth == n // 2 - 1
        self.first = slack * depth
        self.lag = slack * (n - 1 - depth)
        self.most_lag = slack * (n - 1)

    @staticmethod
    def scratch(count, block):
        dma = pltpu.SemaphoreType.DMA
        return [pltpu.VMEM((count, *block), BF16)] * 3 + [dma((count,))] * 4

    def to_mid(self, k):
        return remote(
            self.part.at[k], self.inner_in.at[k], self.s_in.at[k], self.r_inner.at[k], "tensor", self.inner
        )

    def to_inner(self, k):
        return remote(
            self.part.at[k], self.outer_in.at[k], self.s_in.at[k], self.r_outer.at[k], "tensor", self.inner
        )

    def to_outer(self, k):
        return remote(
            self.inner_in.at[k], self.inner_in.at[k], self.s_out.at[k], self.r_inner.at[k], "tensor", self.outer
        )

    def greet(self, barrier):
        pl.semaphore_signal(barrier, inc=1, device_id={"tensor": self.inner}, device_id_type=MESH)

        @pl.when(self.has_outer)
        def _():
            pl.semaphore_signal(barrier, inc=1, device_id={"tensor": self.outer}, device_id_type=MESH)

    def wait_greetings(self, barrier, others):
        @pl.when(self.has_outer)
        def _():
            pl.semaphore_wait(barrier, others + 2)

        @pl.when(jnp.logical_not(self.has_outer))
        def _():
            pl.semaphore_wait(barrier, others + 1)

    def reduce(self, k):
        @pl.when(self.has_outer)
        def _():
            self.to_inner(k).wait_recv()
            add_rows(self.part.at[k], self.outer_in.at[k], 16)

        @pl.when(self.is_mid)
        def _():
            self.to_mid(k).start()

        @pl.when(jnp.logical_not(self.is_mid))
        def _():
            self.to_inner(k).start()

    def spread(self, k):
        self.to_mid(k).wait_recv()

        @pl.when(self.is_mid)
        def _():
            add_rows(self.inner_in.at[k], self.part.at[k], 16)

        @pl.when(self.has_outer)
        def _():
            self.to_outer(k).start()

    def drain(self, k):
        self.to_mid(k).wait_send()

        @pl.when(self.has_outer)
        def _():
            self.to_outer(k).wait_send()


def between(k, count):
    return jnp.logical_and(k >= 0, k < count)


def head_forward(head, q, k, v, slope, off, tile, attended, lse):
    length = q.shape[0]
    odd = lax.rem(head, 2)
    mask = lane_half(odd).astype(BF16)
    lanes = pl.ds(pl.multiple_of((head // 2) * 2 * HD, 2 * HD), 2 * HD)
    gain = slope[pl.ds(head, 1), 0:1]
    for j in range(length // tile):
        rows = slice(j * tile, (j + 1) * tile)
        most = min(length, (j + 2) * tile)
        scores = lax.dot_general(
            k[0:most, lanes] * mask, q[rows, lanes], (((1,), (1,)), ((), ())), preferred_element_type=F32
        )
        scores = scores * (1.0 / math.sqrt(HD)) + gain * off[0:most, rows]
        top = jnp.max(scores, axis=0, keepdims=True)
        raised = jnp.exp(scores - top)
        total = jnp.sum(raised, axis=0, keepdims=True)
        lse[pl.ds(head, 1), rows] = top + jnp.log(total)
        probs = (raised * (1.0 / total)).astype(BF16)
        got = lax.dot_general(
            v[0:most, lanes] * mask, probs, (((0,), (0,)), ((), ())), preferred_element_type=F32
        )
        mine = got.T.astype(BF16)

        @pl.when(odd == 0)
        def _(rows=rows, mine=mine):
            attended[rows, lanes] = mine

        @pl.when(odd == 1)
        def _(rows=rows, mine=mine):
            attended[rows, lanes] += mine


def head_kernel(heads, *refs):
    (src_h, w_h, vec_h, bias_h, slope_h, blocks_h), refs = refs[:6], refs[6:]
    (normed_h, q_h, k_h, v_h, att_h, lse_h, off_h), refs = refs[:7], refs[7:]
    (src, w, vec, bias, slope, blocks), refs = refs[:6], refs[6:]
    (normed, q, k, v, att, lse, off), refs = refs[:7], refs[7:]
    load, w_load, store = refs
    length, width = src.shape
    loads = [
        pltpu.make_async_copy(a, b, load.at[j])
        for j, (a, b) in enumerate(
            ((src_h, src), (vec_h, vec), (blocks_h, blocks), (bias_h, bias), (slope_h, slope))
        )
    ]
    w_loads = [pltpu.make_async_copy(w_h.at[m], w.at[m], w_load.at[m]) for m in range(3)]
    for one in loads + w_loads:
        one.start()
    for one in loads:
        one.wait()
    step = 16

    def normalize(i, carry):
        at = pl.ds(pl.multiple_of(i * step, step), step)
        value = src[at, :].astype(F32)
        centred = value - jnp.sum(value, axis=-1, keepdims=True) / width
        var = jnp.sum(centred * centred, axis=-1, keepdims=True) / width
        normed[at, :] = (centred * lax.rsqrt(var + EPS) * vec[0:1, :] + vec[1:2, :]).astype(BF16)
        return carry

    lax.fori_loop(0, length // step, normalize, 0)

    here = blocks[...].astype(F32)
    there = jnp.broadcast_to(here, (8, length)).T[:, 0:1]
    for j in range(length // 256):
        cols = slice(j * 256, (j + 1) * 256)
        distance = (
            lax.broadcasted_iota(jnp.int32, (length, 256), 0)
            - lax.broadcasted_iota(jnp.int32, (length, 256), 1)
            - j * 256
        ).astype(F32)
        off[:, cols] = jnp.where(there <= here[:, cols], distance, -1e30)

    for m, to in enumerate((q, k, v)):
        w_loads[m].wait()

        def project(i, carry, m=m, to=to):
            at = pl.ds(pl.multiple_of(i * 256, 256), 256)
            to[at, :] = (
                jnp.dot(normed[at, :], w[m], preferred_element_type=F32) + bias[m : m + 1, :]
            ).astype(BF16)
            return carry

        lax.fori_loop(0, length // 256, project, 0)

    stores = [
        pltpu.make_async_copy(a, b, store.at[j])
        for j, (a, b) in enumerate(
            ((normed, normed_h), (off, off_h), (q, q_h), (k, k_h), (v, v_h), (att, att_h), (lse, lse_h))
        )
    ]
    for one in stores[:5]:
        one.start()

    def attend(head, carry):
        head_forward(head, q, k, v, slope, off, HEAD_TILE, att, lse)
        return carry

    lax.fori_loop(0, heads, attend, 0)
    for one in stores[5:]:
        one.start()
    for one in stores:
        one.wait()


def head_call(src, w, vec, bias, slope, blocks):
    length, width = src.shape
    local = w.shape[2]
    heads = local // HD
    inputs = (src, w, vec, bias, slope, blocks)
    shapes = [
        ((length, width), BF16),
        *[((length, local), BF16)] * 4,
        ((heads, length), F32),
        ((length, length), F32),
    ]
    dma = pltpu.SemaphoreType.DMA
    return pl.pallas_call(
        functools.partial(head_kernel, heads),
        out_shape=[jax.ShapeDtypeStruct(*one) for one in shapes],
        in_specs=[pl.BlockSpec(memory_space=pl.ANY)] * len(inputs),
        out_specs=[pl.BlockSpec(memory_space=pl.ANY)] * len(shapes),
        scratch_shapes=[
            *[pltpu.VMEM(one.shape, one.dtype) for one in inputs],
            *[pltpu.VMEM(*one) for one in shapes],
            dma((5,)),
            dma((3,)),
            dma((7,)),
        ],
        compiler_params=pltpu.CompilerParams(vmem_limit_bytes=60 << 20),
    )(*inputs)


ROWS = 32
SLACK = 2
BLOCK_ROWS = 256
TILE = 512


def mlp_kernel(n, length, *refs):
    (att_h, wo_h, src_h, dy_h, wu_h, wd_h, vec_h), refs = refs[:7], refs[7:]
    (tot_h, second_h, activ_h, pre_h, mlp_h, grad_h, bias_h), refs = refs[:7], refs[7:]
    (att, wo, src, dy, wu, wd, vec, second, activ, pre, mlp, grad, bias), refs = refs[:13], refs[13:]
    load, store, tot_store, *refs = refs
    chain = Chain(n, refs, SLACK)
    width = wo.shape[1]
    units = wu.shape[1]
    chunks = length // ROWS
    blocks = length // BLOCK_ROWS
    per_block = BLOCK_ROWS // ROWS
    group = 4

    loads = [
        pltpu.make_async_copy(a, b, load.at[k])
        for k, (a, b) in enumerate(
            ((att_h, att), (wo_h, wo), (vec_h, vec), (src_h, src), (wu_h, wu), (dy_h, dy), (wd_h, wd))
        )
    ]
    for one in loads:
        one.start()
    barrier = pltpu.get_barrier_semaphore()
    chain.greet(barrier)
    bias[...] = jnp.zeros_like(bias)
    chain.wait_greetings(barrier, 0)
    for one in loads[:3]:
        one.wait()

    def tot_copy(k):
        return pltpu.make_async_copy(chain.inner_in.at[k], tot_h.at[k], tot_store.at[k])

    def block_copies(b):
        at = pl.ds(pl.multiple_of(b * BLOCK_ROWS, BLOCK_ROWS), BLOCK_ROWS)
        pairs = ((second, second_h), (activ, activ_h), (pre, pre_h), (mlp, mlp_h), (grad, grad_h))
        return [
            pltpu.make_async_copy(a.at[at], h.at[at], store.at[b, j]) for j, (a, h) in enumerate(pairs)
        ]

    def produce(g):
        rows = group * ROWS
        left = att[pl.ds(pl.multiple_of(g * rows, rows), rows), :]
        for j in range(width // 512):
            cols = pl.ds(j * 512, 512)
            got = jnp.dot(left, wo[:, cols], preferred_element_type=F32).astype(BF16)
            for q in range(group):
                chain.part[g * group + q, :, cols] = got[q * ROWS : (q + 1) * ROWS]

    def normalize(b):
        step = 16

        def body(i, carry):
            at = pl.ds(pl.multiple_of(b * BLOCK_ROWS + i * step, step), step)
            k = b * per_block + i // (ROWS // step)
            inside = pl.ds(pl.multiple_of((i % (ROWS // step)) * step, step), step)
            value = src[at, :].astype(F32) + (chain.inner_in[k, inside, :].astype(F32) + vec[0:1, :width])
            centred = value - jnp.mean(value, axis=-1, keepdims=True)
            var = jnp.mean(centred * centred, axis=-1, keepdims=True)
            second[at, :] = (
                centred * lax.rsqrt(var + EPS) * vec[1:2, :width] + vec[2:3, :width]
            ).astype(BF16)
            return carry

        lax.fori_loop(0, BLOCK_ROWS // step, body, 0)

    def hidden_tile(b, j):
        at = pl.ds(pl.multiple_of(b * BLOCK_ROWS, BLOCK_ROWS), BLOCK_ROWS)
        cols = pl.ds(pl.multiple_of(j * TILE, TILE), TILE)
        value = jnp.dot(second[at, :], wu[:, cols], preferred_element_type=F32) + vec[3:4, cols]
        back = lax.dot_general(
            dy[at, :], wd[cols, :], (((1,), (1,)), ((), ())), preferred_element_type=F32
        )
        below = 0.5 + 0.5 * lax.erf(value * math.sqrt(0.5))
        density = jnp.exp(-0.5 * value * value) * (1.0 / math.sqrt(2.0 * math.pi))
        activ[at, cols] = (value * below).astype(BF16)
        low = (back * (below + value * density)).astype(BF16)
        pre[at, cols] = low
        bias[:, cols] += jnp.sum(low.astype(F32).reshape(BLOCK_ROWS // 8, 8, TILE), axis=0)

    def out_tile(b, j):
        at = pl.ds(pl.multiple_of(b * BLOCK_ROWS, BLOCK_ROWS), BLOCK_ROWS)
        cols = pl.ds(pl.multiple_of(j * TILE, TILE), TILE)
        mlp[at, cols] = jnp.dot(activ[at, :], wd[:, cols], preferred_element_type=F32).astype(BF16)
        grad[at, cols] = lax.dot_general(
            pre[at, :], wu[cols, :], (((1,), (1,)), ((), ())), preferred_element_type=F32
        ).astype(BF16)

    ahead = units // TILE
    steps = ahead + width // TILE
    per_tick = -(-steps // per_block)
    first_tick = per_block + chain.most_lag

    def tick(t, carry):
        @pl.when(jnp.logical_and(t % group == 0, t < chunks))
        def _():
            produce(t // group)

        ready = t - chain.first

        @pl.when(between(ready, chunks))
        def _():
            chain.reduce(ready)

        back = t - chain.lag

        @pl.when(between(back, chunks))
        def _():
            chain.spread(back)
            tot_copy(back).start()

        late = t - first_tick

        @pl.when(late == 0)
        def _():
            for one in loads[3:]:
                one.wait()

        @pl.when(between(late, blocks * per_block))
        def _():
            b = late // per_block
            for q in range(per_tick):
                s = (late % per_block) * per_tick + q

                @pl.when(s == 0)
                def _():
                    normalize(b)

                @pl.when(s < ahead)
                def _():
                    hidden_tile(b, s)

                @pl.when(between(s - ahead, width // TILE))
                def _():
                    out_tile(b, s - ahead)

                @pl.when(s == steps - 1)
                def _():
                    for one in block_copies(b):
                        one.start()

        return carry

    lax.fori_loop(0, chunks + first_tick, tick, 0)
    bias_copy = pltpu.make_async_copy(bias, bias_h, load.at[0])
    bias_copy.start()

    def drain(k, carry):
        chain.drain(k)
        tot_copy(k).wait()
        return carry

    lax.fori_loop(0, chunks, drain, 0)
    for b in range(blocks):
        for one in block_copies(b):
            one.wait()
    bias_copy.wait()


def mlp_call(n, att, wo, src, dy, wu, wd, vec):
    length, width = src.shape
    units = wu.shape[1]
    chunks = length // ROWS
    dma = pltpu.SemaphoreType.DMA
    inputs = (att, wo, src, dy, wu, wd, vec)
    outs = [(chunks, ROWS, width), (length, width), (length, units), (length, units)]
    outs += [(length, width), (length, width)]
    out_shape = [jax.ShapeDtypeStruct(one, BF16) for one in outs] + [jax.ShapeDtypeStruct((8, units), F32)]
    scratch = [pltpu.VMEM(one.shape, one.dtype) for one in inputs]
    scratch += [pltpu.VMEM(one.shape, one.dtype) for one in out_shape[1:]]
    scratch += [dma((7,)), dma((length // BLOCK_ROWS, 5)), dma((chunks,))]
    scratch += Chain.scratch(chunks, (ROWS, width))
    return pl.pallas_call(
        functools.partial(mlp_kernel, n, length),
        out_shape=out_shape,
        in_specs=[pl.BlockSpec(memory_space=pl.ANY)] * len(inputs),
        out_specs=[pl.BlockSpec(memory_space=pl.ANY)] * len(out_shape),
        scratch_shapes=scratch,
        compiler_params=pltpu.CompilerParams(
            collective_id=0, has_side_effects=True, vmem_limit_bytes=60 << 20
        ),
    )(*inputs)


class Ring:
    def __init__(self, n, refs, slots, slack):
        self.chain = Chain(n, refs, slack)
        self.slots = slots
        self.gone = self.chain.most_lag + 2

    def at(self, k):
        return lax.rem(k, self.slots)

    def reduce(self, k):
        self.chain.reduce(self.at(k))

    def spread(self, k):
        self.chain.spread(self.at(k))

    def retire(self, k):
        self.chain.drain(self.at(k))


class Cube:
    def __init__(self, refs, keep, step, apart=1):
        (self.fin, self.give, self.c0, self.r1, self.r2), refs = refs[:5], refs[5:]
        self.s0, self.q0, self.s1, self.q1, self.s2, self.q2, self.s3, self.q3, self.s4, self.q4, self.kept = refs
        self.keep_of, self.step, self.apart = keep, step, apart
        self.gone = 6 * apart
        self.slots = self.gone + 1
        d = lax.axis_index("dp")
        self.c, self.x, self.y = d % 2, (d // 2) % 2, d // 4
        self.to_c, self.to_x, self.to_y = d + 1 - 2 * self.c, d + 2 - 4 * self.x, d + 4 - 8 * self.y
        self.stages = (self.stage1, self.stage2, self.stage3, self.stage4, self.stage5, self.retire)

    @classmethod
    def scratch(cls, block, apart=1):
        dma, n = pltpu.SemaphoreType.DMA, 6 * apart + 1
        return [
            pltpu.VMEM((n, 2, 2, 2, *block), BF16),
            pltpu.VMEM((n, 2, 2, *block), BF16),
            pltpu.VMEM((n, 2, 2, *block), BF16),
            pltpu.VMEM((n, 2, *block), BF16),
            pltpu.VMEM((n, 2, *block), BF16),
            *[dma((n,))] * 2,
            *[dma((n, 2))] * 6,
            *[dma((n,))] * 3,
        ]

    def greet(self, barrier):
        for to in (self.to_c, self.to_x, self.to_y):
            pl.semaphore_signal(barrier, inc=1, device_id={"dp": to}, device_id_type=MESH)

    def slot(self, k):
        return lax.rem(k, self.slots)

    def half(self, k):
        p = self.slot(k)
        return remote(self.give.at[p], self.c0.at[p], self.s0.at[p], self.q0.at[p], "dp", self.to_c)

    def quarters(self, p):
        return self.fin.at[p, self.c, 0, self.x], self.fin.at[p, self.c, 1, self.y]

    def hop1(self, k):
        p, fin, c = self.slot(k), self.fin, self.c
        return (
            remote(fin.at[p, c, 0, 1 - self.x], self.r1.at[p, 0], self.s1.at[p, 0], self.q1.at[p, 0], "dp", self.to_x),
            remote(fin.at[p, c, 1, 1 - self.y], self.r1.at[p, 1], self.s1.at[p, 1], self.q1.at[p, 1], "dp", self.to_y),
        )

    def hop2(self, k):
        p = self.slot(k)
        a, b = self.quarters(p)
        return (
            remote(a, self.r2.at[p, 0], self.s2.at[p, 0], self.q2.at[p, 0], "dp", self.to_y),
            remote(b, self.r2.at[p, 1], self.s2.at[p, 1], self.q2.at[p, 1], "dp", self.to_x),
        )

    def hop3(self, k):
        p = self.slot(k)
        a, b = self.quarters(p)
        return (
            remote(a, a, self.s3.at[p, 0], self.q3.at[p, 0], "dp", self.to_x),
            remote(b, b, self.s3.at[p, 1], self.q3.at[p, 1], "dp", self.to_y),
        )

    def hop4(self, k):
        p = self.slot(k)
        mine = self.fin.at[p, self.c]
        return remote(mine, mine, self.s4.at[p], self.q4.at[p], "dp", self.to_c)

    def kept_wait(self, k):
        p = self.slot(k)
        pltpu.make_async_copy(self.fin.at[p], self.fin.at[p], self.kept.at[p]).wait()

    def add_quarters(self, k, got):
        p = self.slot(k)
        for j, quarter in enumerate(self.quarters(p)):
            add_rows(quarter, got.at[p, j], self.step)

    def stage1(self, k):
        self.half(k).wait()
        p = self.slot(k)
        for a in range(2):
            for b in range(2):
                add_rows(self.fin.at[p, self.c, a, b], self.c0.at[p, a, b], self.step)
        for one in self.hop1(k):
            one.start()

    def stage2(self, k):
        for one in self.hop1(k):
            one.wait()
        self.add_quarters(k, self.r1)
        for one in self.hop2(k):
            one.start()

    def stage3(self, k):
        for one in self.hop2(k):
            one.wait()
        self.add_quarters(k, self.r2)
        for one in self.hop3(k):
            one.start()

    def stage4(self, k):
        for one in self.hop3(k):
            one.wait_recv()
        self.hop4(k).start()

    def stage5(self, k):
        self.hop4(k).wait_recv()
        p = self.slot(k)
        self.keep_of(k, self.fin.at[p], self.kept.at[p])

    def retire(self, k):
        for one in self.hop3(k) + (self.hop4(k),):
            one.wait_send()
        self.kept_wait(k)

    def tick(self, t, count):
        for late, stage in reversed(tuple(enumerate(self.stages, 1))):
            k = t - late * self.apart

            @pl.when(between(k, count))
            def _(stage=stage, k=k):
                stage(k)


def weighted(left, right):
    return lax.dot_general(left, right, (((0,), (0,)), ((), ())), preferred_element_type=F32).astype(BF16)


def lane_half(odd):
    return (lax.broadcasted_iota(jnp.int32, (1, 2 * HD), 1) // HD == odd).astype(F32)


def head_backward(head, q, k, v, up, lse, slope, off, tile, grads, acc):
    q_grad, k_grad, v_grad = grads
    k_acc, v_acc = acc
    length = q.shape[0]
    odd = lax.rem(head, 2)
    mask = lane_half(odd).astype(BF16)
    lanes = pl.ds(pl.multiple_of((head // 2) * 2 * HD, 2 * HD), 2 * HD)
    scale = 1.0 / math.sqrt(HD)
    gain = slope[pl.ds(head, 1), 0:1]
    nt = (((1,), (1,)), ((), ()))
    for j in range(length // tile):
        rows = slice(j * tile, (j + 1) * tile)
        most = min(length, (j + 2) * tile)
        q_here = q[rows, lanes]
        up_here = up[rows, lanes] * mask
        k_here = k[0:most, lanes] * mask
        scores = lax.dot_general(k_here, q_here, nt, preferred_element_type=F32)
        probs = jnp.exp(scores * scale + gain * off[0:most, rows] - lse[pl.ds(head, 1), rows])
        back = lax.dot_general(v[0:most, lanes], up_here, nt, preferred_element_type=F32)
        delta = jnp.sum(probs * back, axis=0, keepdims=True)
        score_grad = (probs * (back - delta)).astype(BF16)
        v_part = jnp.dot(probs.astype(BF16), up_here, preferred_element_type=F32)
        k_part = jnp.dot(score_grad, q_here * mask, preferred_element_type=F32)
        if j == 0:
            v_acc[0:most, :] = v_part
            k_acc[0:most, :] = k_part
            if most < length:
                v_acc[most:length, :] = jnp.zeros((length - most, 2 * HD), F32)
                k_acc[most:length, :] = jnp.zeros((length - most, 2 * HD), F32)
        else:
            v_acc[0:most, :] += v_part
            k_acc[0:most, :] += k_part
        q_part = lax.dot_general(k_here, score_grad, (((0,), (0,)), ((), ())), preferred_element_type=F32)
        mine = (q_part.T * scale).astype(BF16)

        @pl.when(odd == 0)
        def _(rows=rows, mine=mine):
            q_grad[rows, lanes] = mine

        @pl.when(odd == 1)
        def _(rows=rows, mine=mine):
            q_grad[rows, lanes] += mine

    for to, got, factor in ((k_grad, k_acc, scale), (v_grad, v_acc, 1.0)):

        @pl.when(odd == 0)
        def _(to=to, got=got, factor=factor):
            to[:, lanes] = (got[...] * factor).astype(BF16)

        @pl.when(odd == 1)
        def _(to=to, got=got, factor=factor):
            to[:, lanes] += (got[...] * factor).astype(BF16)


ROWS_BACK = 48
BACK_SLOTS = 12
BACK_SLACK = 2
BACK_APART = 2
BACK_COLUMNS = 1024
HEAD_TILE = 256
PIECE = 256
GROUP = 4


def back_kernel(n, heads, *refs):
    (grad_h, mlp_h, activ_h, dy_h, second_h, pre_h, src_h, tot_h, w_h, normed_h, att_h, eb_h), refs = refs[:12], refs[12:]
    smalls_h, refs = refs[:8], refs[8:]
    (out_h, shrink_out, expand_out, wo_out, mix_out, input_h, small_out), refs = refs[:7], refs[7:]
    (left, dy, pre, src, tot, out, resid, w, att, eb), refs = refs[:10], refs[10:]
    smalls, refs = refs[:8], refs[8:]
    vec, wo, q, k, v, lse, slope, off = smalls
    (up, grads, k_acc, v_acc, cols, buf, got_small), refs = refs[:7], refs[7:]
    (load, left_sem, part_sem, row_sem, out_sem, ss, sq), refs = refs[:7], refs[7:]
    ring, refs = Ring(n, refs[:7], BACK_SLOTS, BACK_SLACK), refs[7:]
    chain = ring.chain
    width, local = dy.shape[1], q.shape[1]
    rows, per_sum = ROWS_BACK, grad_h.shape[0]
    loaded_z, total_z = 2 * per_sum, 3 * per_sum
    per_row = width // BACK_COLUMNS
    first = activ_h.shape[1] // PIECE
    total_left = first + second_h.shape[1] // PIECE
    to_output = total_left * per_row
    to_mixing = to_output + local // PIECE * per_row
    pair = BACK_COLUMNS // local
    per_matrix = width // PIECE // pair
    total_p = to_mixing + 3 * per_matrix

    def keep(p, piece_ref, sem):
        here = pl.ds(pl.multiple_of(lax.rem(p, per_row) * BACK_COLUMNS, BACK_COLUMNS), BACK_COLUMNS)
        for lo, hi, to in (
            (0, first * per_row, shrink_out),
            (first * per_row, to_output, expand_out),
            (to_output, to_mixing, wo_out),
        ):

            @pl.when(jnp.logical_and(p >= lo, p < hi))
            def _(lo=lo, to=to):
                pltpu.make_async_copy(piece_ref, to.at[(p - lo) // per_row, :, :, :, :, here], sem).start()

        @pl.when(p >= to_mixing)
        def _():
            i = p - to_mixing
            for j in range(pair):
                pltpu.make_async_copy(
                    piece_ref.at[:, :, :, :, pl.ds(j * local, local)],
                    mix_out.at[i // per_matrix, lax.rem(i, per_matrix) * pair + j],
                    sem,
                ).start()

    cube = Cube(refs, keep, PIECE // 8, BACK_APART)

    loads = [pltpu.make_async_copy(a, b, load.at[j]) for j, (a, b) in enumerate(zip(smalls_h, smalls))]
    pairs = ((dy_h, dy), (pre_h, pre), (w_h, w), (att_h, att), (eb_h, eb), (normed_h, dy))
    loads += [pltpu.make_async_copy(a, b, load.at[8 + j]) for j, (a, b) in enumerate(pairs)]

    def part_load(j, which):
        return pltpu.make_async_copy(
            (grad_h, mlp_h)[which].at[lax.rem(j, per_sum)], chain.part.at[ring.at(j)], part_sem.at[ring.at(j)]
        )

    def part_start(j):
        @pl.when(j < per_sum)
        def _():
            part_load(j, 0).start()

        @pl.when(between(j - per_sum, per_sum))
        def _():
            part_load(j, 1).start()

    def left_load(r, which):
        at = (r - which * first) * PIECE
        return pltpu.make_async_copy(
            (activ_h, second_h)[which].at[:, pl.ds(pl.multiple_of(at, PIECE), PIECE)],
            left.at[lax.rem(r, 2)],
            left_sem.at[lax.rem(r, 2)],
        )

    def left_start(r):
        @pl.when(r < first)
        def _():
            left_load(r, 0).start()

        @pl.when(between(r - first, total_left - first))
        def _():
            left_load(r, 1).start()

    def row_loads(j):
        at, chunk = lax.rem(j, 2), lax.rem(j, per_sum)
        return (
            pltpu.make_async_copy(src_h.at[chunk], src.at[at], row_sem.at[at, 0]),
            pltpu.make_async_copy(tot_h.at[chunk], tot.at[at], row_sem.at[at, 1]),
        )

    def out_store(j, to):
        at = lax.rem(j, 2)
        return pltpu.make_async_copy(out.at[at], to.at[lax.rem(j, per_sum)], out_sem.at[at])

    part_start(0)
    left_start(0)
    loads[8].start()
    part_start(1)
    for one in loads[:8] + [loads[9]]:
        one.start()
    barrier = pltpu.get_barrier_semaphore()
    chain.greet(barrier)
    cube.greet(barrier)
    cols[...] = jnp.zeros_like(cols)
    buf[...] = jnp.zeros_like(buf)
    chain.wait_greetings(barrier, 3)
    loads[8].wait()

    def product(p, columns, right):
        to = cube.slot(p)
        count = PIECE // 8
        for side, store in ((1 - cube.c, cube.give.at[to]), (cube.c, cube.fin.at[to, cube.c])):
            for j in range(BACK_COLUMNS // 512):
                got = weighted(columns(j, side), right(j))
                for a in range(2):
                    for b in range(2):
                        lo = (2 * a + b) * count
                        store[a, b, :, j * 512 : (j + 1) * 512] = got[lo : lo + count]

    half = PIECE // 2

    def produce(p):
        r, part = p // per_row, lax.rem(p, per_row)

        @pl.when(r < total_left)
        def _():
            at = lax.rem(r, 2)

            @pl.when(part == 0)
            def _():
                left_start(r + 1)
                pltpu.make_async_copy(activ_h.at[:, pl.ds(0, PIECE)], left.at[at], left_sem.at[at]).wait()

            def columns(j, side):
                return left[at, :, pl.ds(pl.multiple_of(side * half, half), half)]

            for which, ref in enumerate((dy, pre)):

                def right(j, ref=ref):
                    return ref[:, pl.ds(pl.multiple_of(part * BACK_COLUMNS + j * 512, 512), 512)]

                @pl.when((r >= first) == bool(which))
                def _(right=right):
                    product(p, columns, right)

        @pl.when(between(p - to_output, to_mixing - to_output))
        def _():
            tile = r - total_left

            def columns(j, side):
                return att[:, pl.ds(pl.multiple_of(tile * PIECE + side * half, half), half)]

            def right(j):
                return resid[:, pl.ds(pl.multiple_of(part * BACK_COLUMNS + j * 512, 512), 512)]

            product(p, columns, right)

        @pl.when(p >= to_mixing)
        def _():
            i = p - to_mixing
            tile = lax.rem(i, per_matrix) * pair

            def columns(j, side):
                return dy[:, pl.ds(pl.multiple_of((tile + j) * PIECE + side * half, half), half)]

            def right(j):
                return grads[i // per_matrix]

            product(p, columns, right)

        cube.half(p).start()

    def produce_rows(g):
        at = pl.ds(pl.multiple_of(g * GROUP * rows, GROUP * rows), GROUP * rows)
        for j in range(width // 512):
            here = pl.ds(j * 512, 512)
            total = sum(
                lax.dot_general(
                    grads[m, at, :], w[m, here, :], (((1,), (1,)), ((), ())), preferred_element_type=F32
                )
                for m in range(3)
            ).astype(BF16)
            for i in range(GROUP):
                chain.part[ring.at(loaded_z + g * GROUP + i), :, here] = total[i * rows : (i + 1) * rows]

    def row_sum(x):
        return jnp.sum(x, axis=-1, keepdims=True)

    def norm_back(value, down, gain):
        centred = value - row_sum(value) / width
        spread = lax.rsqrt(row_sum(centred * centred) / width + EPS)
        normal = centred * spread
        scaled = down * gain
        flat, slope_of = row_sum(scaled) / width, row_sum(scaled * normal) / width
        return normal, spread * (scaled - flat - normal * slope_of)

    def each_rows(j, what):
        step = 16

        def body(i, carry):
            what(
                pl.ds(pl.multiple_of(i * step, step), step),
                pl.ds(pl.multiple_of(lax.rem(j, per_sum) * rows + i * step, step), step),
            )
            return carry

        lax.fori_loop(0, rows // step, body, 0)

    def gather(start, *items):
        for c, item in enumerate(items):
            cols[start + c] += item[0:8] + item[8:16]

    def hidden_rows(at, here):
        return src[at, here, :].astype(F32) + (tot[at, here, :].astype(F32) + vec[0:1, :])

    def rows_back(j):
        at, slot = lax.rem(j, 2), ring.at(j)

        def what(here, there):
            down = chain.inner_in[slot, here, :].astype(F32)
            normal, back = norm_back(hidden_rows(at, here), down, vec[1:2, :])
            given = dy[there, :].astype(F32)
            low = (back + given).astype(BF16)
            resid[there, :] = low
            gather(0, down * normal, down, low.astype(F32))
            gather(5, given)

        each_rows(j, what)
        there = pl.ds(pl.multiple_of(j * rows, rows), rows)
        up[there, :] = lax.dot_general(
            resid[there, :], wo[...], (((1,), (1,)), ((), ())), preferred_element_type=F32
        ).astype(BF16)

    def rows_out(j):
        at, slot = lax.rem(j, 2), ring.at(j)

        def what(here, there):
            out[at, here, :] = (
                hidden_rows(at, here) + chain.inner_in[slot, here, :].astype(F32) + vec[5:6, :]
            ).astype(BF16)

        each_rows(j, what)
        out_store(j, out_h).start()

    def rows_front(j):
        at, slot = lax.rem(j, 2), ring.at(j)

        def what(here, there):
            down = chain.inner_in[slot, here, :].astype(F32)
            normal, back = norm_back(src[at, here, :].astype(F32), down, vec[4:5, :])
            out[at, here, :] = (back + resid[there, :].astype(F32)).astype(BF16)
            gather(3, down * normal, down)

        each_rows(j, what)
        out_store(j, input_h).start()

    def swap(j):
        to = (cube.to_c, cube.to_x, cube.to_y)[j]
        return remote(buf.at[j], got_small.at[j], ss.at[j], sq.at[j], "dp", to)

    def small_step(j):
        if j == 0:
            for row, item in ((0, cols[3]), (1, cols[4]), (2, cols[0]), (3, cols[1]), (4, cols[2]), (5, eb[...]), (6, cols[5])):
                buf[0, row : row + 1, :] = jnp.sum(item, axis=0, keepdims=True)
        else:
            swap(j - 1).wait()
            buf[j] = buf[j - 1] + got_small[j - 1]
        if j < 3:
            swap(j).start()

    late = chain.most_lag + 1
    heads_at = late + per_sum

    def tick(t, carry):
        gone = t - ring.gone

        @pl.when(between(gone, total_z))
        def _():
            ring.retire(gone)

        part_start(t + 2)

        @pl.when(jnp.logical_and(between(t - loaded_z, per_sum), lax.rem(t - loaded_z, GROUP) == 0))
        def _():
            produce_rows((t - loaded_z) // GROUP)

        ready = t - chain.first

        @pl.when(between(ready, total_z))
        def _():
            @pl.when(ready < loaded_z)
            def _():
                part_load(ready, 0).wait()

            ring.reduce(ready)

        back = t - chain.lag

        @pl.when(between(back, total_z))
        def _():
            ring.spread(back)

        cube.tick(t, total_p)

        @pl.when(t == 2)
        def _():
            for one in loads[:8] + [loads[9]]:
                one.wait()
            for one in loads[10:13]:
                one.start()

        @pl.when(t == heads_at)
        def _():
            for one in loads[10:13]:
                one.wait()
            loads[13].start()

        @pl.when(t == to_mixing)
        def _():
            loads[13].wait()

        @pl.when(t < total_p)
        def _():
            produce(t)

        chunk = t - late

        @pl.when(between(chunk + 1, total_z))
        def _():
            for one in row_loads(chunk + 1):
                one.start()

        @pl.when(between(chunk - 2 - per_sum, total_z - per_sum))
        def _():
            out_store(chunk - 2, out_h).wait()

        @pl.when(between(chunk, total_z))
        def _():
            for one in row_loads(chunk):
                one.wait()

            for which, what in enumerate((rows_back, rows_out, rows_front)):

                @pl.when(between(chunk - which * per_sum, per_sum))
                def _(what=what):
                    what(chunk)

        head = t - heads_at

        @pl.when(between(head, heads))
        def _():
            head_backward(
                head, q, k, v, up, lse, slope, off, HEAD_TILE, (grads.at[0], grads.at[1], grads.at[2]), (k_acc, v_acc)
            )

        @pl.when(head == heads)
        def _():
            for j, m in enumerate((0, 2)):
                buf[0, 7:8, j * local : (j + 1) * local] = jnp.sum(
                    grads[m].astype(F32), axis=0, keepdims=True
                )

        for j in range(4):

            @pl.when(t == late + total_z + j)
            def _(j=j):
                small_step(j)

        return carry

    assert heads_at + heads <= loaded_z and heads_at + 1 < to_output
    lax.fori_loop(0, max(total_z + late + 4, total_p + cube.gone), tick, 0)
    small_store = pltpu.make_async_copy(buf.at[3], small_out, load.at[0])
    small_store.start()
    small_store.wait()


def back_call(n, grad, mlp, activ, dy, second, pre, src, tot, w, normed, att, eb, vec, wo, q, k, v, lse, slope, off):
    length, width = dy.shape
    local = q.shape[1]
    chunks = length // ROWS_BACK
    dma = pltpu.SemaphoreType.DMA

    def cut(one):
        return one.reshape(chunks, ROWS_BACK, one.shape[-1])

    smalls = (vec, wo, q, k, v, lse, slope, off)
    inputs = (cut(grad), cut(mlp), activ, dy, second, pre, cut(src), cut(tot), w, normed, att, eb, *smalls)
    piece = (2, 2, 2, PIECE // 8)
    shapes = [
        ((chunks, ROWS_BACK, width), BF16),
        ((activ.shape[1] // PIECE, *piece, width), BF16),
        ((second.shape[1] // PIECE, *piece, width), BF16),
        ((local // PIECE, *piece, width), BF16),
        ((3, width // PIECE, *piece, local), BF16),
        ((chunks, ROWS_BACK, width), BF16),
        ((8, width), F32),
    ]
    slots = BACK_SLOTS
    scratch = [
        pltpu.VMEM((2, length, PIECE), BF16),
        pltpu.VMEM(dy.shape, BF16),
        pltpu.VMEM(pre.shape, BF16),
        *[pltpu.VMEM((2, ROWS_BACK, width), BF16)] * 3,
        pltpu.VMEM(dy.shape, BF16),
        *[pltpu.VMEM(one.shape, one.dtype) for one in (w, att, eb)],
        *[pltpu.VMEM(one.shape, one.dtype) for one in smalls],
        pltpu.VMEM(q.shape, BF16),
        pltpu.VMEM((3, *q.shape), BF16),
        *[pltpu.VMEM((length, 2 * HD), F32)] * 2,
        pltpu.VMEM((6, 8, width), F32),
        pltpu.VMEM((4, 8, width), F32),
        pltpu.VMEM((3, 8, width), F32),
        dma((14,)),
        dma((2,)),
        dma((slots,)),
        dma((2, 2)),
        dma((2,)),
        dma((3,)),
        dma((3,)),
        *Chain.scratch(slots, (ROWS_BACK, width)),
        *Cube.scratch((PIECE // 8, BACK_COLUMNS), BACK_APART),
    ]
    return pl.pallas_call(
        functools.partial(back_kernel, n, local // HD),
        out_shape=[jax.ShapeDtypeStruct(*one) for one in shapes],
        in_specs=[pl.BlockSpec(memory_space=pl.ANY)] * len(inputs),
        out_specs=[pl.BlockSpec(memory_space=pl.ANY)] * len(shapes),
        scratch_shapes=scratch,
        compiler_params=pltpu.CompilerParams(
            collective_id=1, has_side_effects=True, vmem_limit_bytes=61 << 20
        ),
    )(*inputs)


def on_device(
    fast,
    n_tensor,
    inputs,
    block_ids,
    first_gain,
    first_shift,
    mixing_weight,
    mixing_bias,
    output_weight,
    output_bias,
    second_gain,
    second_shift,
    expand_weight,
    expand_bias,
    shrink_weight,
    shrink_bias,
    cotangent,
):
    source = inputs.astype(F32)
    upstream = cotangent.astype(F32)
    length, width = source.shape
    blocks = block_ids[0]
    local_width = mixing_weight.shape[2]
    local_heads = local_width // HD
    units = expand_weight.shape[1]
    first_head = lax.axis_index("tensor") * local_heads
    weights = mixing_weight.transpose(1, 0, 2)
    if fast:
        numbers = (first_head + jnp.arange(local_heads)).astype(F32)
        slope = jnp.broadcast_to((2.0 ** (-8.0 * (numbers + 1.0) / H))[:, None], (local_heads, 128))
        bias = jnp.stack([mixing_bias[0], jnp.zeros_like(mixing_bias[0]), mixing_bias[1]])
        normed_low, query, keys, vals, attended, logsum, off = head_call(
            inputs, weights, jnp.stack([first_gain, first_shift]), bias, slope, block_ids
        )
    else:
        normed_low = layer_norm(source, first_gain, first_shift).astype(BF16)

        def project(k):
            return jnp.dot(normed_low, weights[k], preferred_element_type=F32)

        query = (project(0) + mixing_bias[0]).astype(BF16).reshape(length, local_heads, HD)
        keys = project(1).astype(BF16).reshape(length, local_heads, HD)
        vals = (project(2) + mixing_bias[1]).astype(BF16).reshape(length, local_heads, HD)
        masked = biased_scores(query, keys, blocks, first_head)
        row_top = jnp.max(masked, axis=-1, keepdims=True)
        logsum = row_top + jnp.log(jnp.sum(jnp.exp(masked - row_top), axis=-1, keepdims=True))
        probs_low = jnp.exp(masked - logsum).astype(BF16)
        attended = (
            jnp.einsum("hqk,khd->qhd", probs_low, vals, preferred_element_type=F32)
            .reshape(length, local_width)
            .astype(BF16)
        )
    if fast:
        most = max(width, units)
        vectors = jnp.stack(
            [
                jnp.pad(one, (0, most - one.shape[0]))
                for one in (output_bias, second_gain, second_shift, expand_bias, first_gain, shrink_bias)
            ]
        )
        total, second_low, activ_low, pre_grad, partial_mlp, second_part, expand_bias_part = mlp_call(
            n_tensor, attended, output_weight, inputs, cotangent, expand_weight, shrink_weight, vectors
        )
    else:
        partial_out = jnp.dot(attended, output_weight, preferred_element_type=F32)
        resid = lax.psum(partial_out.astype(BF16), "tensor").astype(F32)
        hidden_state = source + (resid + output_bias)
        second_low = layer_norm(hidden_state, second_gain, second_shift).astype(BF16)
        pre_act = jnp.dot(second_low, expand_weight, preferred_element_type=F32) + expand_bias
        activ_low = gelu_exact(pre_act).astype(BF16)
        partial_mlp = jnp.dot(activ_low, shrink_weight, preferred_element_type=F32)
        act_grad = jnp.einsum("td,fd->tf", cotangent, shrink_weight, preferred_element_type=F32)
        _, gelu_pull = jax.vjp(gelu_exact, pre_act)
        pre_grad = gelu_pull(act_grad)[0].astype(BF16)
        expand_bias_part = jnp.sum(pre_grad.astype(F32), axis=0)
        second_part = jnp.einsum("tf,df->td", pre_grad, expand_weight, preferred_element_type=F32)
    if fast:
        outputs, shrink_sum, expand_sum, output_sum, mixing_sum, input_grad, small = back_call(
            n_tensor, second_part, partial_mlp, activ_low, cotangent, second_low, pre_grad, inputs, total,
            weights, normed_low, attended, expand_bias_part, vectors[:, :width], output_weight, query, keys, vals,
            logsum, slope, off,
        )
        outputs, input_grad = outputs.reshape(length, width), input_grad.reshape(length, width)
        shrink_weight_grad = shrink_sum.astype(F32).reshape(units, width)
        expand_weight_grad = expand_sum.astype(F32).reshape(width, units)
        mixing_weight_grad = mixing_sum.astype(F32).reshape(3, width, local_width).transpose(1, 0, 2)
        output_weight_grad = output_sum.astype(F32).reshape(local_width, width)
        first_gain_grad, first_shift_grad, second_gain_grad, second_shift_grad = small[0], small[1], small[2], small[3]
        output_bias_grad, expand_bias_grad, shrink_bias_grad = small[4], small[5], small[6]
        mixing_bias_grad = small[7, : 2 * local_width].reshape(2, local_width)
    else:
        shrink_bias_part = jnp.sum(upstream, axis=0)
        shrink_part = jnp.einsum("tf,td->fd", activ_low, cotangent, preferred_element_type=F32)
        expand_part = jnp.einsum("td,tf->df", second_low, pre_grad, preferred_element_type=F32)

        mlp_sum = lax.psum(partial_mlp.astype(BF16), "tensor").astype(F32)
        second_grad = lax.psum(second_part.astype(BF16), "tensor").astype(F32)
        outputs = (hidden_state + mlp_sum + shrink_bias).astype(BF16)
        hidden_grad, second_gain_part, second_shift_part = norm_backward(
            hidden_state, second_gain, second_shift, second_grad
        )
        hidden_grad = hidden_grad + upstream
        resid_low = hidden_grad.astype(BF16)
        output_part = jnp.einsum("tc,td->cd", attended, resid_low, preferred_element_type=F32)
        output_bias_part = jnp.sum(resid_low.astype(F32), axis=0)
        attended_grad = (
            jnp.einsum("td,cd->tc", resid_low, output_weight, preferred_element_type=F32)
            .astype(BF16)
            .reshape(length, local_heads, HD)
        )
        probs = jnp.exp(biased_scores(query, keys, blocks, first_head) - logsum)
        probs_low = probs.astype(BF16)
        prob_grad = jnp.einsum("qhd,khd->hqk", attended_grad, vals, preferred_element_type=F32)
        vals_grad = jnp.einsum(
            "hqk,qhd->khd", probs_low, attended_grad, preferred_element_type=F32
        ).astype(BF16)
        row_delta = jnp.sum(probs * prob_grad, axis=-1, keepdims=True)
        score_grad = (probs * (prob_grad - row_delta)).astype(BF16)
        scale_factor = 1.0 / math.sqrt(HD)
        query_grad = (
            jnp.einsum("hqk,khd->qhd", score_grad, keys, preferred_element_type=F32) * scale_factor
        ).astype(BF16)
        keys_grad = (
            jnp.einsum("hqk,qhd->khd", score_grad, query, preferred_element_type=F32) * scale_factor
        ).astype(BF16)
        grads = [one.reshape(length, local_width) for one in (query_grad, keys_grad, vals_grad)]
        mixing_bias_part = jnp.stack(
            [jnp.sum(grads[0].astype(F32), axis=0), jnp.sum(grads[2].astype(F32), axis=0)]
        )
        mixing_part = jnp.stack(
            [jnp.einsum("td,tc->dc", normed_low, one, preferred_element_type=F32) for one in grads]
        )
        normed_part = sum(
            jnp.einsum("tc,dc->td", one, weights[k], preferred_element_type=F32)
            for k, one in enumerate(grads)
        )
        normed_grad = lax.psum(normed_part.astype(BF16), "tensor").astype(F32)
        source_grad, first_gain_part, first_shift_part = norm_backward(
            source, first_gain, first_shift, normed_grad
        )
        input_grad = (source_grad + hidden_grad).astype(BF16)
        summed = lax.psum(
            (
                first_gain_part, first_shift_part, mixing_part, mixing_bias_part, output_part, output_bias_part,
                second_gain_part, second_shift_part, expand_part, expand_bias_part, shrink_part, shrink_bias_part,
            ),
            "dp",
        )
        first_gain_grad, first_shift_grad, mixing_weight_grad, mixing_bias_grad = summed[:4]
        mixing_weight_grad = mixing_weight_grad.transpose(1, 0, 2)
        output_weight_grad, output_bias_grad, second_gain_grad, second_shift_grad = summed[4:8]
        expand_weight_grad, expand_bias_grad, shrink_weight_grad, shrink_bias_grad = summed[8:]
    return (
        outputs,
        input_grad,
        first_gain_grad,
        first_shift_grad,
        mixing_weight_grad,
        mixing_bias_grad,
        output_weight_grad,
        output_bias_grad,
        second_gain_grad,
        second_shift_grad,
        expand_weight_grad,
        expand_bias_grad,
        shrink_weight_grad,
        shrink_bias_grad,
    )


def solution(mesh):
    in_specs = (
        P("dp", None),
        P("dp", None),
        P(),
        P(),
        P(None, None, "tensor"),
        P(None, "tensor"),
        P("tensor", None),
        P(),
        P(),
        P(),
        P(None, "tensor"),
        P("tensor"),
        P("tensor", None),
        P(),
        P("dp", None),
    )
    out_specs = (
        P("dp", None),
        P("dp", None),
        P(),
        P(),
        P(None, None, "tensor"),
        P(None, "tensor"),
        P("tensor", None),
        P(),
        P(),
        P(),
        P(None, "tensor"),
        P("tensor"),
        P("tensor", None),
        P(),
    )
    n_tensor = mesh.shape["tensor"]
    fast = mesh.shape["dp"] == 8 and n_tensor in (2, 4)
    return jax.shard_map(
        functools.partial(on_device, fast, n_tensor),
        mesh=mesh,
        in_specs=in_specs,
        out_specs=out_specs,
        check_vma=False,
    )
```

```python
import functools
import math

import jax
import jax.numpy as jnp
from jax import lax
from jax.experimental import pallas as pl
from jax.experimental.pallas import tpu as pltpu
from jax.sharding import PartitionSpec as P

H = 32
HD = 64
EPS = 1e-05
F32 = jnp.float32
BF16 = jnp.bfloat16
MESH = pl.DeviceIdType.MESH


def layer_norm(values, scale_gain, shift_bias):
    row_mean = jnp.mean(values, axis=-1, keepdims=True)
    centred = values - row_mean
    row_var = jnp.mean(centred * centred, axis=-1, keepdims=True)
    return centred * lax.rsqrt(row_var + EPS) * scale_gain + shift_bias


def norm_backward(values, scale_gain, shift_bias, upstream):
    _, pull_back = jax.vjp(layer_norm, values, scale_gain, shift_bias)
    return pull_back(upstream)


def gelu_exact(values):
    return jax.nn.gelu(values, approximate=False)


def biased_scores(query, keys, blocks, first_head):
    length, local_heads, head_width = query.shape
    scores = jnp.einsum("qhd,khd->hqk", query, keys, preferred_element_type=F32) * (
        1.0 / math.sqrt(head_width)
    )
    heads_index = (first_head + jnp.arange(local_heads)).astype(F32)
    slopes = 2.0 ** (-8.0 * (heads_index + 1.0) / H)
    places = jnp.arange(length)
    offsets = (places[None, :] - places[:, None]).astype(F32)
    scores = scores + slopes[:, None, None] * offsets[None]
    allowed = blocks[None, :] <= blocks[:, None]
    return jnp.where(allowed[None], scores, -1e30)


def add_rows(dst, src, step):
    rows = dst.shape[0]

    def body(i, carry):
        at = pl.ds(pl.multiple_of(i * step, step), step)
        dst[at, :] = (dst[at, :].astype(F32) + src[at, :].astype(F32)).astype(BF16)
        return carry

    lax.fori_loop(0, rows // step, body, 0)


def remote(src, dst, send, recv, axis, to):
    return pltpu.make_async_remote_copy(
        src_ref=src,
        dst_ref=dst,
        send_sem=send,
        recv_sem=recv,
        device_id={axis: to},
        device_id_type=MESH,
    )


class Chain:
    def __init__(self, n, refs, slack=1):
        self.part, self.outer_in, self.inner_in, self.s_in, self.s_out, self.r_outer, self.r_inner = refs
        i = lax.axis_index("tensor")
        left = i < n // 2
        depth = jnp.where(left, i, n - 1 - i)
        self.inner = jnp.where(left, i + 1, i - 1)
        self.has_outer = depth > 0
        self.outer = jnp.where(self.has_outer, jnp.where(left, i - 1, i + 1), self.inner)
        self.is_mid = depth == n // 2 - 1
        self.first = slack * depth
        self.lag = slack * (n - 1 - depth)
        self.most_lag = slack * (n - 1)

    @staticmethod
    def scratch(count, block):
        dma = pltpu.SemaphoreType.DMA
        return [pltpu.VMEM((count, *block), BF16)] * 3 + [dma((count,))] * 4

    def to_mid(self, k):
        return remote(
            self.part.at[k], self.inner_in.at[k], self.s_in.at[k], self.r_inner.at[k], "tensor", self.inner
        )

    def to_inner(self, k):
        return remote(
            self.part.at[k], self.outer_in.at[k], self.s_in.at[k], self.r_outer.at[k], "tensor", self.inner
        )

    def to_outer(self, k):
        return remote(
            self.inner_in.at[k], self.inner_in.at[k], self.s_out.at[k], self.r_inner.at[k], "tensor", self.outer
        )

    def greet(self, barrier):
        pl.semaphore_signal(barrier, inc=1, device_id={"tensor": self.inner}, device_id_type=MESH)

        @pl.when(self.has_outer)
        def _():
            pl.semaphore_signal(barrier, inc=1, device_id={"tensor": self.outer}, device_id_type=MESH)

    def wait_greetings(self, barrier, others):
        @pl.when(self.has_outer)
        def _():
            pl.semaphore_wait(barrier, others + 2)

        @pl.when(jnp.logical_not(self.has_outer))
        def _():
            pl.semaphore_wait(barrier, others + 1)

    def reduce(self, k):
        @pl.when(self.has_outer)
        def _():
            self.to_inner(k).wait_recv()
            add_rows(self.part.at[k], self.outer_in.at[k], 16)

        @pl.when(self.is_mid)
        def _():
            self.to_mid(k).start()

        @pl.when(jnp.logical_not(self.is_mid))
        def _():
            self.to_inner(k).start()

    def spread(self, k):
        self.to_mid(k).wait_recv()

        @pl.when(self.is_mid)
        def _():
            add_rows(self.inner_in.at[k], self.part.at[k], 16)

        @pl.when(self.has_outer)
        def _():
            self.to_outer(k).start()

    def drain(self, k):
        self.to_mid(k).wait_send()

        @pl.when(self.has_outer)
        def _():
            self.to_outer(k).wait_send()


def between(k, count):
    return jnp.logical_and(k >= 0, k < count)


def pair_forward(pair, q, k, v, slope, off, tile, attended, lse):
    length = q.shape[0]
    lanes = pl.ds(pl.multiple_of(pair * 2 * HD, 2 * HD), 2 * HD)
    masks = [lane_half(odd).astype(BF16) for odd in range(2)]
    gains = [slope[pl.ds(2 * pair + odd, 1), 0:1] for odd in range(2)]
    for j in range(length // tile):
        rows = slice(j * tile, (j + 1) * tile)
        most = min(length, (j + 2) * tile)
        here = q[rows, lanes]
        scores = [
            lax.dot_general(
                k[0:most, lanes], here * masks[odd], (((1,), (1,)), ((), ())), preferred_element_type=F32
            )
            for odd in range(2)
        ]
        got = []
        for odd in range(2):
            raised = scores[odd] * (1.0 / math.sqrt(HD)) + gains[odd] * off[0:most, rows]
            top = jnp.max(raised, axis=0, keepdims=True)
            raised = jnp.exp(raised - top)
            total = jnp.sum(raised, axis=0, keepdims=True)
            lse[pl.ds(2 * pair + odd, 1), rows] = top + jnp.log(total)
            probs = (raised * (1.0 / total)).astype(BF16)
            got.append(
                lax.dot_general(
                    v[0:most, lanes], probs, (((0,), (0,)), ((), ())), preferred_element_type=F32
                )
            )
        both = jnp.concatenate([got[0][:HD], got[1][HD:]], axis=0)
        attended[rows, lanes] = both.T.astype(BF16)


def head_kernel(heads, *refs):
    (src_h, w_h, vec_h, bias_h, slope_h, blocks_h), refs = refs[:6], refs[6:]
    (normed_h, q_h, k_h, v_h, att_h, lse_h, off_h), refs = refs[:7], refs[7:]
    (src, w, vec, bias, slope, blocks), refs = refs[:6], refs[6:]
    (normed, q, k, v, att, lse, off), refs = refs[:7], refs[7:]
    load, w_load, store = refs
    length, width = src.shape
    loads = [
        pltpu.make_async_copy(a, b, load.at[j])
        for j, (a, b) in enumerate(
            ((src_h, src), (vec_h, vec), (blocks_h, blocks), (bias_h, bias), (slope_h, slope))
        )
    ]
    w_loads = [pltpu.make_async_copy(w_h.at[m], w.at[m], w_load.at[m]) for m in range(3)]
    for one in loads + w_loads:
        one.start()
    for one in loads:
        one.wait()
    step, groups = 16, 4

    def normalize(i, carry):
        ats = [pl.ds(pl.multiple_of((i * groups + g) * step, step), step) for g in range(groups)]
        values = [src[at, :].astype(F32) for at in ats]
        centred = [one - jnp.sum(one, axis=-1, keepdims=True) / width for one in values]
        spread = [lax.rsqrt(jnp.sum(one * one, axis=-1, keepdims=True) / width + EPS) for one in centred]
        for at, one, by in zip(ats, centred, spread):
            normed[at, :] = (one * by * vec[0:1, :] + vec[1:2, :]).astype(BF16)
        return carry

    lax.fori_loop(0, length // (step * groups), normalize, 0)

    here = blocks[...].astype(F32)
    there = jnp.broadcast_to(here, (8, length)).T[:, 0:1]
    for j in range(length // 256):
        cols = slice(j * 256, (j + 1) * 256)
        distance = (
            lax.broadcasted_iota(jnp.int32, (length, 256), 0)
            - lax.broadcasted_iota(jnp.int32, (length, 256), 1)
            - j * 256
        ).astype(F32)
        off[:, cols] = jnp.where(there <= here[:, cols], distance, -1e30)

    for m, to in enumerate((q, k, v)):
        w_loads[m].wait()

        def project(i, carry, m=m, to=to):
            at = pl.ds(pl.multiple_of(i * 256, 256), 256)
            to[at, :] = (
                jnp.dot(normed[at, :], w[m], preferred_element_type=F32) + bias[m : m + 1, :]
            ).astype(BF16)
            return carry

        lax.fori_loop(0, length // 256, project, 0)

    stores = [
        pltpu.make_async_copy(a, b, store.at[j])
        for j, (a, b) in enumerate(
            ((normed, normed_h), (off, off_h), (q, q_h), (k, k_h), (v, v_h), (att, att_h), (lse, lse_h))
        )
    ]
    for one in stores[:5]:
        one.start()

    def attend(pair, carry):
        pair_forward(pair, q, k, v, slope, off, HEAD_TILE, att, lse)
        return carry

    lax.fori_loop(0, heads // 2, attend, 0)
    for one in stores[5:]:
        one.start()
    for one in stores:
        one.wait()


def head_call(src, w, vec, bias, slope, blocks):
    length, width = src.shape
    local = w.shape[2]
    heads = local // HD
    inputs = (src, w, vec, bias, slope, blocks)
    shapes = [
        ((length, width), BF16),
        *[((length, local), BF16)] * 4,
        ((heads, length), F32),
        ((length, length), F32),
    ]
    dma = pltpu.SemaphoreType.DMA
    return pl.pallas_call(
        functools.partial(head_kernel, heads),
        out_shape=[jax.ShapeDtypeStruct(*one) for one in shapes],
        in_specs=[pl.BlockSpec(memory_space=pl.ANY)] * len(inputs),
        out_specs=[pl.BlockSpec(memory_space=pl.ANY)] * len(shapes),
        scratch_shapes=[
            *[pltpu.VMEM(one.shape, one.dtype) for one in inputs],
            *[pltpu.VMEM(*one) for one in shapes],
            dma((5,)),
            dma((3,)),
            dma((7,)),
        ],
        compiler_params=pltpu.CompilerParams(vmem_limit_bytes=60 << 20),
    )(*inputs)


ROWS = 32
SLACK = 2
BLOCK_ROWS = 256
TILE = 512


def mlp_kernel(n, length, *refs):
    (att_h, wo_h, src_h, dy_h, wu_h, wd_h, vec_h), refs = refs[:7], refs[7:]
    (tot_h, second_h, activ_h, pre_h, mlp_h, grad_h, bias_h), refs = refs[:7], refs[7:]
    (att, wo, src, dy, wu, wd, vec, second, activ, pre, mlp, grad, bias), refs = refs[:13], refs[13:]
    load, store, tot_store, *refs = refs
    chain = Chain(n, refs, SLACK)
    width = wo.shape[1]
    units = wu.shape[1]
    chunks = length // ROWS
    blocks = length // BLOCK_ROWS
    per_block = BLOCK_ROWS // ROWS
    group = 4

    loads = [
        pltpu.make_async_copy(a, b, load.at[k])
        for k, (a, b) in enumerate(
            ((att_h, att), (wo_h, wo), (vec_h, vec), (src_h, src), (wu_h, wu), (dy_h, dy), (wd_h, wd))
        )
    ]
    for one in loads:
        one.start()
    barrier = pltpu.get_barrier_semaphore()
    chain.greet(barrier)
    bias[...] = jnp.zeros_like(bias)
    chain.wait_greetings(barrier, 0)
    for one in loads[:3]:
        one.wait()

    def tot_copy(k):
        return pltpu.make_async_copy(chain.inner_in.at[k], tot_h.at[k], tot_store.at[k])

    def block_copies(b):
        at = pl.ds(pl.multiple_of(b * BLOCK_ROWS, BLOCK_ROWS), BLOCK_ROWS)
        pairs = ((second, second_h), (activ, activ_h), (pre, pre_h), (mlp, mlp_h), (grad, grad_h))
        return [
            pltpu.make_async_copy(a.at[at], h.at[at], store.at[b, j]) for j, (a, h) in enumerate(pairs)
        ]

    def produce(g):
        rows = group * ROWS
        left = att[pl.ds(pl.multiple_of(g * rows, rows), rows), :]
        for j in range(width // 512):
            cols = pl.ds(j * 512, 512)
            got = jnp.dot(left, wo[:, cols], preferred_element_type=F32).astype(BF16)
            for q in range(group):
                chain.part[g * group + q, :, cols] = got[q * ROWS : (q + 1) * ROWS]

    def normalize(b):
        step, groups = 16, 4

        def body(i, carry):
            ats, values = [], []
            for g in range(groups):
                r = i * groups + g
                at = pl.ds(pl.multiple_of(b * BLOCK_ROWS + r * step, step), step)
                k = b * per_block + r // (ROWS // step)
                inside = pl.ds(pl.multiple_of((r % (ROWS // step)) * step, step), step)
                ats.append(at)
                values.append(
                    src[at, :].astype(F32) + (chain.inner_in[k, inside, :].astype(F32) + vec[0:1, :width])
                )
            centred = [one - jnp.mean(one, axis=-1, keepdims=True) for one in values]
            spread = [lax.rsqrt(jnp.mean(one * one, axis=-1, keepdims=True) + EPS) for one in centred]
            for at, one, by in zip(ats, centred, spread):
                second[at, :] = (one * by * vec[1:2, :width] + vec[2:3, :width]).astype(BF16)
            return carry

        lax.fori_loop(0, BLOCK_ROWS // (step * groups), body, 0)

    def hidden_tile(b, j):
        at = pl.ds(pl.multiple_of(b * BLOCK_ROWS, BLOCK_ROWS), BLOCK_ROWS)
        cols = pl.ds(pl.multiple_of(j * TILE, TILE), TILE)
        value = jnp.dot(second[at, :], wu[:, cols], preferred_element_type=F32) + vec[3:4, cols]
        back = lax.dot_general(
            dy[at, :], wd[cols, :], (((1,), (1,)), ((), ())), preferred_element_type=F32
        )
        below = 0.5 + 0.5 * lax.erf(value * math.sqrt(0.5))
        density = jnp.exp(-0.5 * value * value) * (1.0 / math.sqrt(2.0 * math.pi))
        activ[at, cols] = (value * below).astype(BF16)
        low = (back * (below + value * density)).astype(BF16)
        pre[at, cols] = low
        bias[:, cols] += jnp.sum(low.astype(F32).reshape(BLOCK_ROWS // 8, 8, TILE), axis=0)

    def out_tile(b, j):
        at = pl.ds(pl.multiple_of(b * BLOCK_ROWS, BLOCK_ROWS), BLOCK_ROWS)
        cols = pl.ds(pl.multiple_of(j * TILE, TILE), TILE)
        mlp[at, cols] = jnp.dot(activ[at, :], wd[:, cols], preferred_element_type=F32).astype(BF16)
        grad[at, cols] = lax.dot_general(
            pre[at, :], wu[cols, :], (((1,), (1,)), ((), ())), preferred_element_type=F32
        ).astype(BF16)

    ahead = units // TILE
    steps = ahead + width // TILE
    per_tick = -(-steps // per_block)
    first_tick = per_block + chain.most_lag

    def tick(t, carry):
        @pl.when(jnp.logical_and(t % group == 0, t < chunks))
        def _():
            produce(t // group)

        ready = t - chain.first

        @pl.when(between(ready, chunks))
        def _():
            chain.reduce(ready)

        back = t - chain.lag

        @pl.when(between(back, chunks))
        def _():
            chain.spread(back)
            tot_copy(back).start()

        late = t - first_tick

        @pl.when(late == 0)
        def _():
            for one in loads[3:]:
                one.wait()

        @pl.when(between(late, blocks * per_block))
        def _():
            b = late // per_block
            for q in range(per_tick):
                s = (late % per_block) * per_tick + q

                @pl.when(s == 0)
                def _():
                    normalize(b)

                @pl.when(s < ahead)
                def _():
                    hidden_tile(b, s)

                @pl.when(between(s - ahead, width // TILE))
                def _():
                    out_tile(b, s - ahead)

                @pl.when(s == steps - 1)
                def _():
                    for one in block_copies(b):
                        one.start()

        return carry

    lax.fori_loop(0, chunks + first_tick, tick, 0)
    bias_copy = pltpu.make_async_copy(bias, bias_h, load.at[0])
    bias_copy.start()

    def drain(k, carry):
        chain.drain(k)
        tot_copy(k).wait()
        return carry

    lax.fori_loop(0, chunks, drain, 0)
    for b in range(blocks):
        for one in block_copies(b):
            one.wait()
    bias_copy.wait()


def mlp_call(n, att, wo, src, dy, wu, wd, vec):
    length, width = src.shape
    units = wu.shape[1]
    chunks = length // ROWS
    dma = pltpu.SemaphoreType.DMA
    inputs = (att, wo, src, dy, wu, wd, vec)
    outs = [(chunks, ROWS, width), (length, width), (length, units), (length, units)]
    outs += [(length, width), (length, width)]
    out_shape = [jax.ShapeDtypeStruct(one, BF16) for one in outs] + [jax.ShapeDtypeStruct((8, units), F32)]
    scratch = [pltpu.VMEM(one.shape, one.dtype) for one in inputs]
    scratch += [pltpu.VMEM(one.shape, one.dtype) for one in out_shape[1:]]
    scratch += [dma((7,)), dma((length // BLOCK_ROWS, 5)), dma((chunks,))]
    scratch += Chain.scratch(chunks, (ROWS, width))
    return pl.pallas_call(
        functools.partial(mlp_kernel, n, length),
        out_shape=out_shape,
        in_specs=[pl.BlockSpec(memory_space=pl.ANY)] * len(inputs),
        out_specs=[pl.BlockSpec(memory_space=pl.ANY)] * len(out_shape),
        scratch_shapes=scratch,
        compiler_params=pltpu.CompilerParams(
            collective_id=0, has_side_effects=True, vmem_limit_bytes=60 << 20
        ),
    )(*inputs)


class Ring:
    def __init__(self, n, refs, slots, slack):
        self.chain = Chain(n, refs, slack)
        self.slots = slots
        self.gone = self.chain.most_lag + 2

    def at(self, k):
        return lax.rem(k, self.slots)

    def reduce(self, k):
        self.chain.reduce(self.at(k))

    def spread(self, k):
        self.chain.spread(self.at(k))

    def retire(self, k):
        self.chain.drain(self.at(k))


class Cube:
    def __init__(self, refs, keep, step, apart=1):
        (self.fin, self.give, self.c0, self.r1, self.r2), refs = refs[:5], refs[5:]
        self.s0, self.q0, self.s1, self.q1, self.s2, self.q2, self.s3, self.q3, self.s4, self.q4, self.kept = refs
        self.keep_of, self.step, self.apart = keep, step, apart
        self.gone = 6 * apart
        self.slots = self.gone + 1
        d = lax.axis_index("dp")
        self.c, self.x, self.y = d % 2, (d // 2) % 2, d // 4
        self.to_c, self.to_x, self.to_y = d + 1 - 2 * self.c, d + 2 - 4 * self.x, d + 4 - 8 * self.y
        self.stages = (self.stage1, self.stage2, self.stage3, self.stage4, self.stage5, self.retire)

    @classmethod
    def scratch(cls, block, apart=1):
        dma, n = pltpu.SemaphoreType.DMA, 6 * apart + 1
        return [
            pltpu.VMEM((n, 2, 2, 2, *block), BF16),
            pltpu.VMEM((n, 2, 2, *block), BF16),
            pltpu.VMEM((n, 2, 2, *block), BF16),
            pltpu.VMEM((n, 2, *block), BF16),
            pltpu.VMEM((n, 2, *block), BF16),
            *[dma((n,))] * 2,
            *[dma((n, 2))] * 6,
            *[dma((n,))] * 3,
        ]

    def greet(self, barrier):
        for to in (self.to_c, self.to_x, self.to_y):
            pl.semaphore_signal(barrier, inc=1, device_id={"dp": to}, device_id_type=MESH)

    def slot(self, k):
        return lax.rem(k, self.slots)

    def half(self, k):
        p = self.slot(k)
        return remote(self.give.at[p], self.c0.at[p], self.s0.at[p], self.q0.at[p], "dp", self.to_c)

    def quarters(self, p):
        return self.fin.at[p, self.c, 0, self.x], self.fin.at[p, self.c, 1, self.y]

    def hop1(self, k):
        p, fin, c = self.slot(k), self.fin, self.c
        return (
            remote(fin.at[p, c, 0, 1 - self.x], self.r1.at[p, 0], self.s1.at[p, 0], self.q1.at[p, 0], "dp", self.to_x),
            remote(fin.at[p, c, 1, 1 - self.y], self.r1.at[p, 1], self.s1.at[p, 1], self.q1.at[p, 1], "dp", self.to_y),
        )

    def hop2(self, k):
        p = self.slot(k)
        a, b = self.quarters(p)
        return (
            remote(a, self.r2.at[p, 0], self.s2.at[p, 0], self.q2.at[p, 0], "dp", self.to_y),
            remote(b, self.r2.at[p, 1], self.s2.at[p, 1], self.q2.at[p, 1], "dp", self.to_x),
        )

    def hop3(self, k):
        p = self.slot(k)
        a, b = self.quarters(p)
        return (
            remote(a, a, self.s3.at[p, 0], self.q3.at[p, 0], "dp", self.to_x),
            remote(b, b, self.s3.at[p, 1], self.q3.at[p, 1], "dp", self.to_y),
        )

    def hop4(self, k):
        p = self.slot(k)
        mine = self.fin.at[p, self.c]
        return remote(mine, mine, self.s4.at[p], self.q4.at[p], "dp", self.to_c)

    def kept_wait(self, k):
        p = self.slot(k)
        pltpu.make_async_copy(self.fin.at[p], self.fin.at[p], self.kept.at[p]).wait()

    def add_quarters(self, k, got):
        p = self.slot(k)
        for j, quarter in enumerate(self.quarters(p)):
            add_rows(quarter, got.at[p, j], self.step)

    def stage1(self, k):
        self.half(k).wait()
        p = self.slot(k)
        for a in range(2):
            for b in range(2):
                add_rows(self.fin.at[p, self.c, a, b], self.c0.at[p, a, b], self.step)
        for one in self.hop1(k):
            one.start()

    def stage2(self, k):
        for one in self.hop1(k):
            one.wait()
        self.add_quarters(k, self.r1)
        for one in self.hop2(k):
            one.start()

    def stage3(self, k):
        for one in self.hop2(k):
            one.wait()
        self.add_quarters(k, self.r2)
        for one in self.hop3(k):
            one.start()

    def stage4(self, k):
        for one in self.hop3(k):
            one.wait_recv()
        self.hop4(k).start()

    def stage5(self, k):
        self.hop4(k).wait_recv()
        p = self.slot(k)
        self.keep_of(k, self.fin.at[p], self.kept.at[p])

    def retire(self, k):
        for one in self.hop3(k) + (self.hop4(k),):
            one.wait_send()
        self.kept_wait(k)

    def tick(self, t, count):
        for late, stage in reversed(tuple(enumerate(self.stages, 1))):
            k = t - late * self.apart

            @pl.when(between(k, count))
            def _(stage=stage, k=k):
                stage(k)


def weighted(left, right):
    return lax.dot_general(left, right, (((0,), (0,)), ((), ())), preferred_element_type=F32).astype(BF16)


def lane_half(odd):
    return (lax.broadcasted_iota(jnp.int32, (1, 2 * HD), 1) // HD == odd).astype(F32)


def head_backward(head, q, k, v, up, lse, slope, off, tile, grads, acc):
    q_grad, k_grad, v_grad = grads
    k_acc, v_acc = acc
    length = q.shape[0]
    odd = lax.rem(head, 2)
    mask = lane_half(odd).astype(BF16)
    lanes = pl.ds(pl.multiple_of((head // 2) * 2 * HD, 2 * HD), 2 * HD)
    scale = 1.0 / math.sqrt(HD)
    gain = slope[pl.ds(head, 1), 0:1]
    nt = (((1,), (1,)), ((), ()))
    for j in range(length // tile):
        rows = slice(j * tile, (j + 1) * tile)
        most = min(length, (j + 2) * tile)
        q_here = q[rows, lanes]
        up_here = up[rows, lanes] * mask
        k_here = k[0:most, lanes] * mask
        scores = lax.dot_general(k_here, q_here, nt, preferred_element_type=F32)
        probs = jnp.exp(scores * scale + gain * off[0:most, rows] - lse[pl.ds(head, 1), rows])
        back = lax.dot_general(v[0:most, lanes], up_here, nt, preferred_element_type=F32)
        delta = jnp.sum(probs * back, axis=0, keepdims=True)
        score_grad = (probs * (back - delta)).astype(BF16)
        v_part = jnp.dot(probs.astype(BF16), up_here, preferred_element_type=F32)
        k_part = jnp.dot(score_grad, q_here * mask, preferred_element_type=F32)
        if j == 0:
            v_acc[0:most, :] = v_part
            k_acc[0:most, :] = k_part
            if most < length:
                v_acc[most:length, :] = jnp.zeros((length - most, 2 * HD), F32)
                k_acc[most:length, :] = jnp.zeros((length - most, 2 * HD), F32)
        else:
            v_acc[0:most, :] += v_part
            k_acc[0:most, :] += k_part
        q_part = lax.dot_general(k_here, score_grad, (((0,), (0,)), ((), ())), preferred_element_type=F32)
        mine = (q_part.T * scale).astype(BF16)

        @pl.when(odd == 0)
        def _(rows=rows, mine=mine):
            q_grad[rows, lanes] = mine

        @pl.when(odd == 1)
        def _(rows=rows, mine=mine):
            q_grad[rows, lanes] += mine

    for to, got, factor in ((k_grad, k_acc, scale), (v_grad, v_acc, 1.0)):

        @pl.when(odd == 0)
        def _(to=to, got=got, factor=factor):
            to[:, lanes] = (got[...] * factor).astype(BF16)

        @pl.when(odd == 1)
        def _(to=to, got=got, factor=factor):
            to[:, lanes] += (got[...] * factor).astype(BF16)


ROWS_BACK = 48
BACK_SLOTS = 12
BACK_SLACK = 2
BACK_APART = 2
BACK_COLUMNS = 1024
HEAD_TILE = 256
PIECE = 256
GROUP = 4


def back_kernel(n, heads, *refs):
    (grad_h, mlp_h, activ_h, dy_h, second_h, pre_h, src_h, tot_h, w_h, normed_h, att_h, eb_h), refs = refs[:12], refs[12:]
    smalls_h, refs = refs[:8], refs[8:]
    (out_h, shrink_out, expand_out, wo_out, mix_out, input_h, small_out), refs = refs[:7], refs[7:]
    (left, dy, pre, src, tot, out, resid, w, att, eb), refs = refs[:10], refs[10:]
    smalls, refs = refs[:8], refs[8:]
    vec, wo, q, k, v, lse, slope, off = smalls
    (up, grads, k_acc, v_acc, cols, buf, got_small), refs = refs[:7], refs[7:]
    (load, left_sem, part_sem, row_sem, out_sem, ss, sq), refs = refs[:7], refs[7:]
    ring, refs = Ring(n, refs[:7], BACK_SLOTS, BACK_SLACK), refs[7:]
    chain = ring.chain
    width, local = dy.shape[1], q.shape[1]
    rows, per_sum = ROWS_BACK, grad_h.shape[0]
    loaded_z, total_z = 2 * per_sum, 3 * per_sum
    per_row = width // BACK_COLUMNS
    first = activ_h.shape[1] // PIECE
    total_left = first + second_h.shape[1] // PIECE
    to_output = total_left * per_row
    to_mixing = to_output + local // PIECE * per_row
    pair = BACK_COLUMNS // local
    per_matrix = width // PIECE // pair
    total_p = to_mixing + 3 * per_matrix

    def keep(p, piece_ref, sem):
        here = pl.ds(pl.multiple_of(lax.rem(p, per_row) * BACK_COLUMNS, BACK_COLUMNS), BACK_COLUMNS)
        for lo, hi, to in (
            (0, first * per_row, shrink_out),
            (first * per_row, to_output, expand_out),
            (to_output, to_mixing, wo_out),
        ):

            @pl.when(jnp.logical_and(p >= lo, p < hi))
            def _(lo=lo, to=to):
                pltpu.make_async_copy(piece_ref, to.at[(p - lo) // per_row, :, :, :, :, here], sem).start()

        @pl.when(p >= to_mixing)
        def _():
            i = p - to_mixing
            for j in range(pair):
                pltpu.make_async_copy(
                    piece_ref.at[:, :, :, :, pl.ds(j * local, local)],
                    mix_out.at[i // per_matrix, lax.rem(i, per_matrix) * pair + j],
                    sem,
                ).start()

    cube = Cube(refs, keep, PIECE // 8, BACK_APART)

    loads = [pltpu.make_async_copy(a, b, load.at[j]) for j, (a, b) in enumerate(zip(smalls_h, smalls))]
    pairs = ((dy_h, dy), (pre_h, pre), (w_h, w), (att_h, att), (eb_h, eb), (normed_h, dy))
    loads += [pltpu.make_async_copy(a, b, load.at[8 + j]) for j, (a, b) in enumerate(pairs)]

    def part_load(j, which):
        return pltpu.make_async_copy(
            (grad_h, mlp_h)[which].at[lax.rem(j, per_sum)], chain.part.at[ring.at(j)], part_sem.at[ring.at(j)]
        )

    def part_start(j):
        @pl.when(j < per_sum)
        def _():
            part_load(j, 0).start()

        @pl.when(between(j - per_sum, per_sum))
        def _():
            part_load(j, 1).start()

    def left_load(r, which):
        at = (r - which * first) * PIECE
        return pltpu.make_async_copy(
            (activ_h, second_h)[which].at[:, pl.ds(pl.multiple_of(at, PIECE), PIECE)],
            left.at[lax.rem(r, 2)],
            left_sem.at[lax.rem(r, 2)],
        )

    def left_start(r):
        @pl.when(r < first)
        def _():
            left_load(r, 0).start()

        @pl.when(between(r - first, total_left - first))
        def _():
            left_load(r, 1).start()

    def row_loads(j):
        at, chunk = lax.rem(j, 2), lax.rem(j, per_sum)
        return (
            pltpu.make_async_copy(src_h.at[chunk], src.at[at], row_sem.at[at, 0]),
            pltpu.make_async_copy(tot_h.at[chunk], tot.at[at], row_sem.at[at, 1]),
        )

    def out_store(j, to):
        at = lax.rem(j, 2)
        return pltpu.make_async_copy(out.at[at], to.at[lax.rem(j, per_sum)], out_sem.at[at])

    part_start(0)
    left_start(0)
    loads[8].start()
    part_start(1)
    for one in loads[:8] + [loads[9]]:
        one.start()
    barrier = pltpu.get_barrier_semaphore()
    chain.greet(barrier)
    cube.greet(barrier)
    cols[...] = jnp.zeros_like(cols)
    buf[...] = jnp.zeros_like(buf)
    chain.wait_greetings(barrier, 3)
    loads[8].wait()

    def product(p, columns, right):
        to = cube.slot(p)
        count = PIECE // 8
        for side, store in ((1 - cube.c, cube.give.at[to]), (cube.c, cube.fin.at[to, cube.c])):
            for j in range(BACK_COLUMNS // 512):
                got = weighted(columns(j, side), right(j))
                for a in range(2):
                    for b in range(2):
                        lo = (2 * a + b) * count
                        store[a, b, :, j * 512 : (j + 1) * 512] = got[lo : lo + count]

    half = PIECE // 2

    def produce(p):
        r, part = p // per_row, lax.rem(p, per_row)

        @pl.when(r < total_left)
        def _():
            at = lax.rem(r, 2)

            @pl.when(part == 0)
            def _():
                left_start(r + 1)
                pltpu.make_async_copy(activ_h.at[:, pl.ds(0, PIECE)], left.at[at], left_sem.at[at]).wait()

            def columns(j, side):
                return left[at, :, pl.ds(pl.multiple_of(side * half, half), half)]

            for which, ref in enumerate((dy, pre)):

                def right(j, ref=ref):
                    return ref[:, pl.ds(pl.multiple_of(part * BACK_COLUMNS + j * 512, 512), 512)]

                @pl.when((r >= first) == bool(which))
                def _(right=right):
                    product(p, columns, right)

        @pl.when(between(p - to_output, to_mixing - to_output))
        def _():
            tile = r - total_left

            def columns(j, side):
                return att[:, pl.ds(pl.multiple_of(tile * PIECE + side * half, half), half)]

            def right(j):
                return resid[:, pl.ds(pl.multiple_of(part * BACK_COLUMNS + j * 512, 512), 512)]

            product(p, columns, right)

        @pl.when(p >= to_mixing)
        def _():
            i = p - to_mixing
            tile = lax.rem(i, per_matrix) * pair

            def columns(j, side):
                return dy[:, pl.ds(pl.multiple_of((tile + j) * PIECE + side * half, half), half)]

            def right(j):
                return grads[i // per_matrix]

            product(p, columns, right)

        cube.half(p).start()

    def produce_rows(g):
        at = pl.ds(pl.multiple_of(g * GROUP * rows, GROUP * rows), GROUP * rows)
        for j in range(width // 512):
            here = pl.ds(j * 512, 512)
            total = sum(
                lax.dot_general(
                    grads[m, at, :], w[m, here, :], (((1,), (1,)), ((), ())), preferred_element_type=F32
                )
                for m in range(3)
            ).astype(BF16)
            for i in range(GROUP):
                chain.part[ring.at(loaded_z + g * GROUP + i), :, here] = total[i * rows : (i + 1) * rows]

    def row_sum(x):
        return jnp.sum(x, axis=-1, keepdims=True)

    def norm_back(value, down, gain):
        centred = value - row_sum(value) / width
        spread = lax.rsqrt(row_sum(centred * centred) / width + EPS)
        normal = centred * spread
        scaled = down * gain
        flat, slope_of = row_sum(scaled) / width, row_sum(scaled * normal) / width
        return normal, spread * (scaled - flat - normal * slope_of)

    def each_rows(j, what):
        step = 16

        def body(i, carry):
            what(
                pl.ds(pl.multiple_of(i * step, step), step),
                pl.ds(pl.multiple_of(lax.rem(j, per_sum) * rows + i * step, step), step),
            )
            return carry

        lax.fori_loop(0, rows // step, body, 0)

    def gather(start, *items):
        for c, item in enumerate(items):
            cols[start + c] += item[0:8] + item[8:16]

    def hidden_rows(at, here):
        return src[at, here, :].astype(F32) + (tot[at, here, :].astype(F32) + vec[0:1, :])

    def rows_back(j):
        at, slot = lax.rem(j, 2), ring.at(j)

        def what(here, there):
            down = chain.inner_in[slot, here, :].astype(F32)
            normal, back = norm_back(hidden_rows(at, here), down, vec[1:2, :])
            given = dy[there, :].astype(F32)
            low = (back + given).astype(BF16)
            resid[there, :] = low
            gather(0, down * normal, down, low.astype(F32))
            gather(5, given)

        each_rows(j, what)
        there = pl.ds(pl.multiple_of(j * rows, rows), rows)
        up[there, :] = lax.dot_general(
            resid[there, :], wo[...], (((1,), (1,)), ((), ())), preferred_element_type=F32
        ).astype(BF16)

    def rows_out(j):
        at, slot = lax.rem(j, 2), ring.at(j)

        def what(here, there):
            out[at, here, :] = (
                hidden_rows(at, here) + chain.inner_in[slot, here, :].astype(F32) + vec[5:6, :]
            ).astype(BF16)

        each_rows(j, what)
        out_store(j, out_h).start()

    def rows_front(j):
        at, slot = lax.rem(j, 2), ring.at(j)

        def what(here, there):
            down = chain.inner_in[slot, here, :].astype(F32)
            normal, back = norm_back(src[at, here, :].astype(F32), down, vec[4:5, :])
            out[at, here, :] = (back + resid[there, :].astype(F32)).astype(BF16)
            gather(3, down * normal, down)

        each_rows(j, what)
        out_store(j, input_h).start()

    def swap(j):
        to = (cube.to_c, cube.to_x, cube.to_y)[j]
        return remote(buf.at[j], got_small.at[j], ss.at[j], sq.at[j], "dp", to)

    def small_step(j):
        if j == 0:
            for row, item in ((0, cols[3]), (1, cols[4]), (2, cols[0]), (3, cols[1]), (4, cols[2]), (5, eb[...]), (6, cols[5])):
                buf[0, row : row + 1, :] = jnp.sum(item, axis=0, keepdims=True)
        else:
            swap(j - 1).wait()
            buf[j] = buf[j - 1] + got_small[j - 1]
        if j < 3:
            swap(j).start()

    late = chain.most_lag + 1
    heads_at = late + per_sum

    def tick(t, carry):
        gone = t - ring.gone

        @pl.when(between(gone, total_z))
        def _():
            ring.retire(gone)

        part_start(t + 2)

        @pl.when(jnp.logical_and(between(t - loaded_z, per_sum), lax.rem(t - loaded_z, GROUP) == 0))
        def _():
            produce_rows((t - loaded_z) // GROUP)

        ready = t - chain.first

        @pl.when(between(ready, total_z))
        def _():
            @pl.when(ready < loaded_z)
            def _():
                part_load(ready, 0).wait()

            ring.reduce(ready)

        back = t - chain.lag

        @pl.when(between(back, total_z))
        def _():
            ring.spread(back)

        cube.tick(t, total_p)

        @pl.when(t == 2)
        def _():
            for one in loads[:8] + [loads[9]]:
                one.wait()
            for one in loads[10:13]:
                one.start()

        @pl.when(t == heads_at)
        def _():
            for one in loads[10:13]:
                one.wait()
            loads[13].start()

        @pl.when(t == to_mixing)
        def _():
            loads[13].wait()

        @pl.when(t < total_p)
        def _():
            produce(t)

        chunk = t - late

        @pl.when(between(chunk + 1, total_z))
        def _():
            for one in row_loads(chunk + 1):
                one.start()

        @pl.when(between(chunk - 2 - per_sum, total_z - per_sum))
        def _():
            out_store(chunk - 2, out_h).wait()

        @pl.when(between(chunk, total_z))
        def _():
            for one in row_loads(chunk):
                one.wait()

            for which, what in enumerate((rows_back, rows_out, rows_front)):

                @pl.when(between(chunk - which * per_sum, per_sum))
                def _(what=what):
                    what(chunk)

        head = t - heads_at

        @pl.when(between(head, heads))
        def _():
            head_backward(
                head, q, k, v, up, lse, slope, off, HEAD_TILE, (grads.at[0], grads.at[1], grads.at[2]), (k_acc, v_acc)
            )

        @pl.when(head == heads)
        def _():
            for j, m in enumerate((0, 2)):
                buf[0, 7:8, j * local : (j + 1) * local] = jnp.sum(
                    grads[m].astype(F32), axis=0, keepdims=True
                )

        for j in range(4):

            @pl.when(t == late + total_z + j)
            def _(j=j):
                small_step(j)

        return carry

    assert heads_at + heads <= loaded_z and heads_at + 1 < to_output
    lax.fori_loop(0, max(total_z + late + 4, total_p + cube.gone), tick, 0)
    small_store = pltpu.make_async_copy(buf.at[3], small_out, load.at[0])
    small_store.start()
    small_store.wait()


def back_call(n, grad, mlp, activ, dy, second, pre, src, tot, w, normed, att, eb, vec, wo, q, k, v, lse, slope, off):
    length, width = dy.shape
    local = q.shape[1]
    chunks = length // ROWS_BACK
    dma = pltpu.SemaphoreType.DMA

    def cut(one):
        return one.reshape(chunks, ROWS_BACK, one.shape[-1])

    smalls = (vec, wo, q, k, v, lse, slope, off)
    inputs = (cut(grad), cut(mlp), activ, dy, second, pre, cut(src), cut(tot), w, normed, att, eb, *smalls)
    piece = (2, 2, 2, PIECE // 8)
    shapes = [
        ((chunks, ROWS_BACK, width), BF16),
        ((activ.shape[1] // PIECE, *piece, width), BF16),
        ((second.shape[1] // PIECE, *piece, width), BF16),
        ((local // PIECE, *piece, width), BF16),
        ((3, width // PIECE, *piece, local), BF16),
        ((chunks, ROWS_BACK, width), BF16),
        ((8, width), F32),
    ]
    slots = BACK_SLOTS
    scratch = [
        pltpu.VMEM((2, length, PIECE), BF16),
        pltpu.VMEM(dy.shape, BF16),
        pltpu.VMEM(pre.shape, BF16),
        *[pltpu.VMEM((2, ROWS_BACK, width), BF16)] * 3,
        pltpu.VMEM(dy.shape, BF16),
        *[pltpu.VMEM(one.shape, one.dtype) for one in (w, att, eb)],
        *[pltpu.VMEM(one.shape, one.dtype) for one in smalls],
        pltpu.VMEM(q.shape, BF16),
        pltpu.VMEM((3, *q.shape), BF16),
        *[pltpu.VMEM((length, 2 * HD), F32)] * 2,
        pltpu.VMEM((6, 8, width), F32),
        pltpu.VMEM((4, 8, width), F32),
        pltpu.VMEM((3, 8, width), F32),
        dma((14,)),
        dma((2,)),
        dma((slots,)),
        dma((2, 2)),
        dma((2,)),
        dma((3,)),
        dma((3,)),
        *Chain.scratch(slots, (ROWS_BACK, width)),
        *Cube.scratch((PIECE // 8, BACK_COLUMNS), BACK_APART),
    ]
    return pl.pallas_call(
        functools.partial(back_kernel, n, local // HD),
        out_shape=[jax.ShapeDtypeStruct(*one) for one in shapes],
        in_specs=[pl.BlockSpec(memory_space=pl.ANY)] * len(inputs),
        out_specs=[pl.BlockSpec(memory_space=pl.ANY)] * len(shapes),
        scratch_shapes=scratch,
        compiler_params=pltpu.CompilerParams(
            collective_id=1, has_side_effects=True, vmem_limit_bytes=61 << 20
        ),
    )(*inputs)


def on_device(
    fast,
    n_tensor,
    inputs,
    block_ids,
    first_gain,
    first_shift,
    mixing_weight,
    mixing_bias,
    output_weight,
    output_bias,
    second_gain,
    second_shift,
    expand_weight,
    expand_bias,
    shrink_weight,
    shrink_bias,
    cotangent,
):
    source = inputs.astype(F32)
    upstream = cotangent.astype(F32)
    length, width = source.shape
    blocks = block_ids[0]
    local_width = mixing_weight.shape[2]
    local_heads = local_width // HD
    units = expand_weight.shape[1]
    first_head = lax.axis_index("tensor") * local_heads
    weights = mixing_weight.transpose(1, 0, 2)
    if fast:
        numbers = (first_head + jnp.arange(local_heads)).astype(F32)
        slope = jnp.broadcast_to((2.0 ** (-8.0 * (numbers + 1.0) / H))[:, None], (local_heads, 128))
        bias = jnp.stack([mixing_bias[0], jnp.zeros_like(mixing_bias[0]), mixing_bias[1]])
        normed_low, query, keys, vals, attended, logsum, off = head_call(
            inputs, weights, jnp.stack([first_gain, first_shift]), bias, slope, block_ids
        )
    else:
        normed_low = layer_norm(source, first_gain, first_shift).astype(BF16)

        def project(k):
            return jnp.dot(normed_low, weights[k], preferred_element_type=F32)

        query = (project(0) + mixing_bias[0]).astype(BF16).reshape(length, local_heads, HD)
        keys = project(1).astype(BF16).reshape(length, local_heads, HD)
        vals = (project(2) + mixing_bias[1]).astype(BF16).reshape(length, local_heads, HD)
        masked = biased_scores(query, keys, blocks, first_head)
        row_top = jnp.max(masked, axis=-1, keepdims=True)
        logsum = row_top + jnp.log(jnp.sum(jnp.exp(masked - row_top), axis=-1, keepdims=True))
        probs_low = jnp.exp(masked - logsum).astype(BF16)
        attended = (
            jnp.einsum("hqk,khd->qhd", probs_low, vals, preferred_element_type=F32)
            .reshape(length, local_width)
            .astype(BF16)
        )
    if fast:
        most = max(width, units)
        vectors = jnp.stack(
            [
                jnp.pad(one, (0, most - one.shape[0]))
                for one in (output_bias, second_gain, second_shift, expand_bias, first_gain, shrink_bias)
            ]
        )
        total, second_low, activ_low, pre_grad, partial_mlp, second_part, expand_bias_part = mlp_call(
            n_tensor, attended, output_weight, inputs, cotangent, expand_weight, shrink_weight, vectors
        )
    else:
        partial_out = jnp.dot(attended, output_weight, preferred_element_type=F32)
        resid = lax.psum(partial_out.astype(BF16), "tensor").astype(F32)
        hidden_state = source + (resid + output_bias)
        second_low = layer_norm(hidden_state, second_gain, second_shift).astype(BF16)
        pre_act = jnp.dot(second_low, expand_weight, preferred_element_type=F32) + expand_bias
        activ_low = gelu_exact(pre_act).astype(BF16)
        partial_mlp = jnp.dot(activ_low, shrink_weight, preferred_element_type=F32)
        act_grad = jnp.einsum("td,fd->tf", cotangent, shrink_weight, preferred_element_type=F32)
        _, gelu_pull = jax.vjp(gelu_exact, pre_act)
        pre_grad = gelu_pull(act_grad)[0].astype(BF16)
        expand_bias_part = jnp.sum(pre_grad.astype(F32), axis=0)
        second_part = jnp.einsum("tf,df->td", pre_grad, expand_weight, preferred_element_type=F32)
    if fast:
        outputs, shrink_sum, expand_sum, output_sum, mixing_sum, input_grad, small = back_call(
            n_tensor, second_part, partial_mlp, activ_low, cotangent, second_low, pre_grad, inputs, total,
            weights, normed_low, attended, expand_bias_part, vectors[:, :width], output_weight, query, keys, vals,
            logsum, slope, off,
        )
        outputs, input_grad = outputs.reshape(length, width), input_grad.reshape(length, width)
        shrink_weight_grad = shrink_sum.astype(F32).reshape(units, width)
        expand_weight_grad = expand_sum.astype(F32).reshape(width, units)
        mixing_weight_grad = mixing_sum.astype(F32).reshape(3, width, local_width).transpose(1, 0, 2)
        output_weight_grad = output_sum.astype(F32).reshape(local_width, width)
        first_gain_grad, first_shift_grad, second_gain_grad, second_shift_grad = small[0], small[1], small[2], small[3]
        output_bias_grad, expand_bias_grad, shrink_bias_grad = small[4], small[5], small[6]
        mixing_bias_grad = small[7, : 2 * local_width].reshape(2, local_width)
    else:
        shrink_bias_part = jnp.sum(upstream, axis=0)
        shrink_part = jnp.einsum("tf,td->fd", activ_low, cotangent, preferred_element_type=F32)
        expand_part = jnp.einsum("td,tf->df", second_low, pre_grad, preferred_element_type=F32)

        mlp_sum = lax.psum(partial_mlp.astype(BF16), "tensor").astype(F32)
        second_grad = lax.psum(second_part.astype(BF16), "tensor").astype(F32)
        outputs = (hidden_state + mlp_sum + shrink_bias).astype(BF16)
        hidden_grad, second_gain_part, second_shift_part = norm_backward(
            hidden_state, second_gain, second_shift, second_grad
        )
        hidden_grad = hidden_grad + upstream
        resid_low = hidden_grad.astype(BF16)
        output_part = jnp.einsum("tc,td->cd", attended, resid_low, preferred_element_type=F32)
        output_bias_part = jnp.sum(resid_low.astype(F32), axis=0)
        attended_grad = (
            jnp.einsum("td,cd->tc", resid_low, output_weight, preferred_element_type=F32)
            .astype(BF16)
            .reshape(length, local_heads, HD)
        )
        probs = jnp.exp(biased_scores(query, keys, blocks, first_head) - logsum)
        probs_low = probs.astype(BF16)
        prob_grad = jnp.einsum("qhd,khd->hqk", attended_grad, vals, preferred_element_type=F32)
        vals_grad = jnp.einsum(
            "hqk,qhd->khd", probs_low, attended_grad, preferred_element_type=F32
        ).astype(BF16)
        row_delta = jnp.sum(probs * prob_grad, axis=-1, keepdims=True)
        score_grad = (probs * (prob_grad - row_delta)).astype(BF16)
        scale_factor = 1.0 / math.sqrt(HD)
        query_grad = (
            jnp.einsum("hqk,khd->qhd", score_grad, keys, preferred_element_type=F32) * scale_factor
        ).astype(BF16)
        keys_grad = (
            jnp.einsum("hqk,qhd->khd", score_grad, query, preferred_element_type=F32) * scale_factor
        ).astype(BF16)
        grads = [one.reshape(length, local_width) for one in (query_grad, keys_grad, vals_grad)]
        mixing_bias_part = jnp.stack(
            [jnp.sum(grads[0].astype(F32), axis=0), jnp.sum(grads[2].astype(F32), axis=0)]
        )
        mixing_part = jnp.stack(
            [jnp.einsum("td,tc->dc", normed_low, one, preferred_element_type=F32) for one in grads]
        )
        normed_part = sum(
            jnp.einsum("tc,dc->td", one, weights[k], preferred_element_type=F32)
            for k, one in enumerate(grads)
        )
        normed_grad = lax.psum(normed_part.astype(BF16), "tensor").astype(F32)
        source_grad, first_gain_part, first_shift_part = norm_backward(
            source, first_gain, first_shift, normed_grad
        )
        input_grad = (source_grad + hidden_grad).astype(BF16)
        summed = lax.psum(
            (
                first_gain_part, first_shift_part, mixing_part, mixing_bias_part, output_part, output_bias_part,
                second_gain_part, second_shift_part, expand_part, expand_bias_part, shrink_part, shrink_bias_part,
            ),
            "dp",
        )
        first_gain_grad, first_shift_grad, mixing_weight_grad, mixing_bias_grad = summed[:4]
        mixing_weight_grad = mixing_weight_grad.transpose(1, 0, 2)
        output_weight_grad, output_bias_grad, second_gain_grad, second_shift_grad = summed[4:8]
        expand_weight_grad, expand_bias_grad, shrink_weight_grad, shrink_bias_grad = summed[8:]
    return (
        outputs,
        input_grad,
        first_gain_grad,
        first_shift_grad,
        mixing_weight_grad,
        mixing_bias_grad,
        output_weight_grad,
        output_bias_grad,
        second_gain_grad,
        second_shift_grad,
        expand_weight_grad,
        expand_bias_grad,
        shrink_weight_grad,
        shrink_bias_grad,
    )


def solution(mesh):
    in_specs = (
        P("dp", None),
        P("dp", None),
        P(),
        P(),
        P(None, None, "tensor"),
        P(None, "tensor"),
        P("tensor", None),
        P(),
        P(),
        P(),
        P(None, "tensor"),
        P("tensor"),
        P("tensor", None),
        P(),
        P("dp", None),
    )
    out_specs = (
        P("dp", None),
        P("dp", None),
        P(),
        P(),
        P(None, None, "tensor"),
        P(None, "tensor"),
        P("tensor", None),
        P(),
        P(),
        P(),
        P(None, "tensor"),
        P("tensor"),
        P("tensor", None),
        P(),
    )
    n_tensor = mesh.shape["tensor"]
    fast = mesh.shape["dp"] == 8 and n_tensor in (2, 4)
    return jax.shard_map(
        functools.partial(on_device, fast, n_tensor),
        mesh=mesh,
        in_specs=in_specs,
        out_specs=out_specs,
        check_vma=False,
    )
```

```python
import functools
import math

import jax
import jax.numpy as jnp
from jax import lax
from jax.experimental import pallas as pl
from jax.experimental.pallas import tpu as pltpu
from jax.sharding import PartitionSpec as P

H = 32
HD = 64
EPS = 1e-05
F32 = jnp.float32
BF16 = jnp.bfloat16
MESH = pl.DeviceIdType.MESH


def layer_norm(values, scale_gain, shift_bias):
    row_mean = jnp.mean(values, axis=-1, keepdims=True)
    centred = values - row_mean
    row_var = jnp.mean(centred * centred, axis=-1, keepdims=True)
    return centred * lax.rsqrt(row_var + EPS) * scale_gain + shift_bias


def norm_backward(values, scale_gain, shift_bias, upstream):
    _, pull_back = jax.vjp(layer_norm, values, scale_gain, shift_bias)
    return pull_back(upstream)


def gelu_exact(values):
    return jax.nn.gelu(values, approximate=False)


def biased_scores(query, keys, blocks, first_head):
    length, local_heads, head_width = query.shape
    scores = jnp.einsum("qhd,khd->hqk", query, keys, preferred_element_type=F32) * (
        1.0 / math.sqrt(head_width)
    )
    heads_index = (first_head + jnp.arange(local_heads)).astype(F32)
    slopes = 2.0 ** (-8.0 * (heads_index + 1.0) / H)
    places = jnp.arange(length)
    offsets = (places[None, :] - places[:, None]).astype(F32)
    scores = scores + slopes[:, None, None] * offsets[None]
    allowed = blocks[None, :] <= blocks[:, None]
    return jnp.where(allowed[None], scores, -1e30)


def add_rows(dst, src, step):
    rows = dst.shape[0]

    def body(i, carry):
        at = pl.ds(pl.multiple_of(i * step, step), step)
        dst[at, :] = (dst[at, :].astype(F32) + src[at, :].astype(F32)).astype(BF16)
        return carry

    lax.fori_loop(0, rows // step, body, 0)


def remote(src, dst, send, recv, axis, to):
    return pltpu.make_async_remote_copy(
        src_ref=src,
        dst_ref=dst,
        send_sem=send,
        recv_sem=recv,
        device_id={axis: to},
        device_id_type=MESH,
    )


class Chain:
    def __init__(self, n, refs, slack=1):
        self.part, self.outer_in, self.inner_in, self.s_in, self.s_out, self.r_outer, self.r_inner = refs
        i = lax.axis_index("tensor")
        left = i < n // 2
        depth = jnp.where(left, i, n - 1 - i)
        self.inner = jnp.where(left, i + 1, i - 1)
        self.has_outer = depth > 0
        self.outer = jnp.where(self.has_outer, jnp.where(left, i - 1, i + 1), self.inner)
        self.is_mid = depth == n // 2 - 1
        self.first = slack * depth
        self.lag = slack * (n - 1 - depth)
        self.most_lag = slack * (n - 1)

    @staticmethod
    def scratch(count, block):
        dma = pltpu.SemaphoreType.DMA
        return [pltpu.VMEM((count, *block), BF16)] * 3 + [dma((count,))] * 4

    def to_mid(self, k):
        return remote(
            self.part.at[k], self.inner_in.at[k], self.s_in.at[k], self.r_inner.at[k], "tensor", self.inner
        )

    def to_inner(self, k):
        return remote(
            self.part.at[k], self.outer_in.at[k], self.s_in.at[k], self.r_outer.at[k], "tensor", self.inner
        )

    def to_outer(self, k):
        return remote(
            self.inner_in.at[k], self.inner_in.at[k], self.s_out.at[k], self.r_inner.at[k], "tensor", self.outer
        )

    def greet(self, barrier):
        pl.semaphore_signal(barrier, inc=1, device_id={"tensor": self.inner}, device_id_type=MESH)

        @pl.when(self.has_outer)
        def _():
            pl.semaphore_signal(barrier, inc=1, device_id={"tensor": self.outer}, device_id_type=MESH)

    def wait_greetings(self, barrier, others):
        @pl.when(self.has_outer)
        def _():
            pl.semaphore_wait(barrier, others + 2)

        @pl.when(jnp.logical_not(self.has_outer))
        def _():
            pl.semaphore_wait(barrier, others + 1)

    def reduce(self, k):
        @pl.when(self.has_outer)
        def _():
            self.to_inner(k).wait_recv()
            add_rows(self.part.at[k], self.outer_in.at[k], 16)

        @pl.when(self.is_mid)
        def _():
            self.to_mid(k).start()

        @pl.when(jnp.logical_not(self.is_mid))
        def _():
            self.to_inner(k).start()

    def spread(self, k):
        self.to_mid(k).wait_recv()

        @pl.when(self.is_mid)
        def _():
            add_rows(self.inner_in.at[k], self.part.at[k], 16)

        @pl.when(self.has_outer)
        def _():
            self.to_outer(k).start()

    def drain(self, k):
        self.to_mid(k).wait_send()

        @pl.when(self.has_outer)
        def _():
            self.to_outer(k).wait_send()


def between(k, count):
    return jnp.logical_and(k >= 0, k < count)


def pair_forward(pair, q, k, v, slope, off, tile, attended, lse):
    length = q.shape[0]
    lanes = pl.ds(pl.multiple_of(pair * 2 * HD, 2 * HD), 2 * HD)
    masks = [lane_half(odd).astype(BF16) for odd in range(2)]
    gains = [slope[pl.ds(2 * pair + odd, 1), 0:1] for odd in range(2)]
    for j in range(length // tile):
        rows = slice(j * tile, (j + 1) * tile)
        most = min(length, (j + 2) * tile)
        here = q[rows, lanes]
        scores = [
            lax.dot_general(
                k[0:most, lanes], here * masks[odd], (((1,), (1,)), ((), ())), preferred_element_type=F32
            )
            for odd in range(2)
        ]
        got = []
        for odd in range(2):
            raised = scores[odd] * (1.0 / math.sqrt(HD)) + gains[odd] * off[0:most, rows]
            top = jnp.max(raised, axis=0, keepdims=True)
            raised = jnp.exp(raised - top)
            total = jnp.sum(raised, axis=0, keepdims=True)
            lse[pl.ds(2 * pair + odd, 1), rows] = top + jnp.log(total)
            probs = (raised * (1.0 / total)).astype(BF16)
            got.append(
                lax.dot_general(
                    v[0:most, lanes], probs, (((0,), (0,)), ((), ())), preferred_element_type=F32
                )
            )
        both = jnp.concatenate([got[0][:HD], got[1][HD:]], axis=0)
        attended[rows, lanes] = both.T.astype(BF16)


def head_kernel(heads, *refs):
    (src_h, w_h, vec_h, bias_h, slope_h, blocks_h), refs = refs[:6], refs[6:]
    (normed_h, q_h, k_h, v_h, att_h, lse_h, off_h), refs = refs[:7], refs[7:]
    (src, w, vec, bias, slope, blocks), refs = refs[:6], refs[6:]
    (normed, q, k, v, att, lse, off), refs = refs[:7], refs[7:]
    load, w_load, store = refs
    length, width = src.shape
    loads = [
        pltpu.make_async_copy(a, b, load.at[j])
        for j, (a, b) in enumerate(
            ((src_h, src), (vec_h, vec), (blocks_h, blocks), (bias_h, bias), (slope_h, slope))
        )
    ]
    w_loads = [pltpu.make_async_copy(w_h.at[m], w.at[m], w_load.at[m]) for m in range(3)]
    for one in loads + w_loads:
        one.start()
    for one in loads:
        one.wait()
    step, groups = 16, 4

    def normalize(i, carry):
        ats = [pl.ds(pl.multiple_of((i * groups + g) * step, step), step) for g in range(groups)]
        values = [src[at, :].astype(F32) for at in ats]
        centred = [one - jnp.sum(one, axis=-1, keepdims=True) / width for one in values]
        spread = [lax.rsqrt(jnp.sum(one * one, axis=-1, keepdims=True) / width + EPS) for one in centred]
        for at, one, by in zip(ats, centred, spread):
            normed[at, :] = (one * by * vec[0:1, :] + vec[1:2, :]).astype(BF16)
        return carry

    lax.fori_loop(0, length // (step * groups), normalize, 0)

    here = blocks[...].astype(F32)
    there = jnp.broadcast_to(here, (8, length)).T[:, 0:1]
    for j in range(length // 256):
        cols = slice(j * 256, (j + 1) * 256)
        distance = (
            lax.broadcasted_iota(jnp.int32, (length, 256), 0)
            - lax.broadcasted_iota(jnp.int32, (length, 256), 1)
            - j * 256
        ).astype(F32)
        off[:, cols] = jnp.where(there <= here[:, cols], distance, -1e30)

    for m, to in enumerate((q, k, v)):
        w_loads[m].wait()

        def project(i, carry, m=m, to=to):
            at = pl.ds(pl.multiple_of(i * 256, 256), 256)
            to[at, :] = (
                jnp.dot(normed[at, :], w[m], preferred_element_type=F32) + bias[m : m + 1, :]
            ).astype(BF16)
            return carry

        lax.fori_loop(0, length // 256, project, 0)

    stores = [
        pltpu.make_async_copy(a, b, store.at[j])
        for j, (a, b) in enumerate(
            ((normed, normed_h), (off, off_h), (q, q_h), (k, k_h), (v, v_h), (att, att_h), (lse, lse_h))
        )
    ]
    for one in stores[:5]:
        one.start()

    def attend(pair, carry):
        pair_forward(pair, q, k, v, slope, off, HEAD_TILE, att, lse)
        return carry

    lax.fori_loop(0, heads // 2, attend, 0)
    for one in stores[5:]:
        one.start()
    for one in stores:
        one.wait()


def head_call(src, w, vec, bias, slope, blocks):
    length, width = src.shape
    local = w.shape[2]
    heads = local // HD
    inputs = (src, w, vec, bias, slope, blocks)
    shapes = [
        ((length, width), BF16),
        *[((length, local), BF16)] * 4,
        ((heads, length), F32),
        ((length, length), F32),
    ]
    dma = pltpu.SemaphoreType.DMA
    return pl.pallas_call(
        functools.partial(head_kernel, heads),
        out_shape=[jax.ShapeDtypeStruct(*one) for one in shapes],
        in_specs=[pl.BlockSpec(memory_space=pl.ANY)] * len(inputs),
        out_specs=[pl.BlockSpec(memory_space=pl.ANY)] * len(shapes),
        scratch_shapes=[
            *[pltpu.VMEM(one.shape, one.dtype) for one in inputs],
            *[pltpu.VMEM(*one) for one in shapes],
            dma((5,)),
            dma((3,)),
            dma((7,)),
        ],
        compiler_params=pltpu.CompilerParams(vmem_limit_bytes=60 << 20),
    )(*inputs)


ROWS = 32
SLACK = 2
BLOCK_ROWS = 256
TILE = 512


def mlp_kernel(n, length, *refs):
    (att_h, wo_h, src_h, dy_h, wu_h, wd_h, vec_h), refs = refs[:7], refs[7:]
    (tot_h, second_h, activ_h, pre_h, mlp_h, grad_h, bias_h), refs = refs[:7], refs[7:]
    (att, wo, src, dy, wu, wd, vec, second, activ, pre, mlp, grad, bias), refs = refs[:13], refs[13:]
    load, store, tot_store, *refs = refs
    chain = Chain(n, refs, SLACK)
    width = wo.shape[1]
    units = wu.shape[1]
    chunks = length // ROWS
    blocks = length // BLOCK_ROWS
    per_block = BLOCK_ROWS // ROWS
    group = 4

    loads = [
        pltpu.make_async_copy(a, b, load.at[k])
        for k, (a, b) in enumerate(
            ((att_h, att), (wo_h, wo), (vec_h, vec), (src_h, src), (wu_h, wu), (dy_h, dy), (wd_h, wd))
        )
    ]
    for one in loads:
        one.start()
    barrier = pltpu.get_barrier_semaphore()
    chain.greet(barrier)
    bias[...] = jnp.zeros_like(bias)
    chain.wait_greetings(barrier, 0)
    for one in loads[:3]:
        one.wait()

    def tot_copy(k):
        return pltpu.make_async_copy(chain.inner_in.at[k], tot_h.at[k], tot_store.at[k])

    def block_copies(b):
        at = pl.ds(pl.multiple_of(b * BLOCK_ROWS, BLOCK_ROWS), BLOCK_ROWS)
        pairs = ((second, second_h), (activ, activ_h), (pre, pre_h), (mlp, mlp_h), (grad, grad_h))
        return [
            pltpu.make_async_copy(a.at[at], h.at[at], store.at[b, j]) for j, (a, h) in enumerate(pairs)
        ]

    def produce(g):
        rows = group * ROWS
        left = att[pl.ds(pl.multiple_of(g * rows, rows), rows), :]
        for j in range(width // 512):
            cols = pl.ds(j * 512, 512)
            got = jnp.dot(left, wo[:, cols], preferred_element_type=F32).astype(BF16)
            for q in range(group):
                chain.part[g * group + q, :, cols] = got[q * ROWS : (q + 1) * ROWS]

    def normalize(b):
        step, groups = 16, 4

        def body(i, carry):
            ats, values = [], []
            for g in range(groups):
                r = i * groups + g
                at = pl.ds(pl.multiple_of(b * BLOCK_ROWS + r * step, step), step)
                k = b * per_block + r // (ROWS // step)
                inside = pl.ds(pl.multiple_of((r % (ROWS // step)) * step, step), step)
                ats.append(at)
                values.append(
                    src[at, :].astype(F32) + (chain.inner_in[k, inside, :].astype(F32) + vec[0:1, :width])
                )
            centred = [one - jnp.mean(one, axis=-1, keepdims=True) for one in values]
            spread = [lax.rsqrt(jnp.mean(one * one, axis=-1, keepdims=True) + EPS) for one in centred]
            for at, one, by in zip(ats, centred, spread):
                second[at, :] = (one * by * vec[1:2, :width] + vec[2:3, :width]).astype(BF16)
            return carry

        lax.fori_loop(0, BLOCK_ROWS // (step * groups), body, 0)

    def hidden_tile(b, j):
        at = pl.ds(pl.multiple_of(b * BLOCK_ROWS, BLOCK_ROWS), BLOCK_ROWS)
        cols = pl.ds(pl.multiple_of(j * TILE, TILE), TILE)
        value = jnp.dot(second[at, :], wu[:, cols], preferred_element_type=F32) + vec[3:4, cols]
        back = lax.dot_general(
            dy[at, :], wd[cols, :], (((1,), (1,)), ((), ())), preferred_element_type=F32
        )
        below = 0.5 + 0.5 * lax.erf(value * math.sqrt(0.5))
        density = jnp.exp(-0.5 * value * value) * (1.0 / math.sqrt(2.0 * math.pi))
        activ[at, cols] = (value * below).astype(BF16)
        low = (back * (below + value * density)).astype(BF16)
        pre[at, cols] = low
        bias[:, cols] += jnp.sum(low.astype(F32).reshape(BLOCK_ROWS // 8, 8, TILE), axis=0)

    def out_tile(b, j):
        at = pl.ds(pl.multiple_of(b * BLOCK_ROWS, BLOCK_ROWS), BLOCK_ROWS)
        cols = pl.ds(pl.multiple_of(j * TILE, TILE), TILE)
        mlp[at, cols] = jnp.dot(activ[at, :], wd[:, cols], preferred_element_type=F32).astype(BF16)
        grad[at, cols] = lax.dot_general(
            pre[at, :], wu[cols, :], (((1,), (1,)), ((), ())), preferred_element_type=F32
        ).astype(BF16)

    ahead = units // TILE
    steps = ahead + width // TILE
    per_tick = -(-steps // per_block)
    first_tick = per_block + chain.most_lag

    def tick(t, carry):
        @pl.when(jnp.logical_and(t % group == 0, t < chunks))
        def _():
            produce(t // group)

        ready = t - chain.first

        @pl.when(between(ready, chunks))
        def _():
            chain.reduce(ready)

        back = t - chain.lag

        @pl.when(between(back, chunks))
        def _():
            chain.spread(back)
            tot_copy(back).start()

        late = t - first_tick

        @pl.when(late == 0)
        def _():
            for one in loads[3:]:
                one.wait()

        @pl.when(between(late, blocks * per_block))
        def _():
            b = late // per_block
            for q in range(per_tick):
                s = (late % per_block) * per_tick + q

                @pl.when(s == 0)
                def _():
                    normalize(b)

                @pl.when(s < ahead)
                def _():
                    hidden_tile(b, s)

                @pl.when(between(s - ahead, width // TILE))
                def _():
                    out_tile(b, s - ahead)

                @pl.when(s == steps - 1)
                def _():
                    for one in block_copies(b):
                        one.start()

        return carry

    lax.fori_loop(0, chunks + first_tick, tick, 0)
    bias_copy = pltpu.make_async_copy(bias, bias_h, load.at[0])
    bias_copy.start()

    def drain(k, carry):
        chain.drain(k)
        tot_copy(k).wait()
        return carry

    lax.fori_loop(0, chunks, drain, 0)
    for b in range(blocks):
        for one in block_copies(b):
            one.wait()
    bias_copy.wait()


def mlp_call(n, att, wo, src, dy, wu, wd, vec):
    length, width = src.shape
    units = wu.shape[1]
    chunks = length // ROWS
    dma = pltpu.SemaphoreType.DMA
    inputs = (att, wo, src, dy, wu, wd, vec)
    outs = [(chunks, ROWS, width), (length, width), (length, units), (length, units)]
    outs += [(length, width), (length, width)]
    out_shape = [jax.ShapeDtypeStruct(one, BF16) for one in outs] + [jax.ShapeDtypeStruct((8, units), F32)]
    scratch = [pltpu.VMEM(one.shape, one.dtype) for one in inputs]
    scratch += [pltpu.VMEM(one.shape, one.dtype) for one in out_shape[1:]]
    scratch += [dma((7,)), dma((length // BLOCK_ROWS, 5)), dma((chunks,))]
    scratch += Chain.scratch(chunks, (ROWS, width))
    return pl.pallas_call(
        functools.partial(mlp_kernel, n, length),
        out_shape=out_shape,
        in_specs=[pl.BlockSpec(memory_space=pl.ANY)] * len(inputs),
        out_specs=[pl.BlockSpec(memory_space=pl.ANY)] * len(out_shape),
        scratch_shapes=scratch,
        compiler_params=pltpu.CompilerParams(
            collective_id=0, has_side_effects=True, vmem_limit_bytes=60 << 20
        ),
    )(*inputs)


class Ring:
    def __init__(self, n, refs, slots, slack):
        self.chain = Chain(n, refs, slack)
        self.slots = slots
        self.gone = self.chain.most_lag + 2

    def at(self, k):
        return lax.rem(k, self.slots)

    def reduce(self, k):
        self.chain.reduce(self.at(k))

    def spread(self, k):
        self.chain.spread(self.at(k))

    def retire(self, k):
        self.chain.drain(self.at(k))


class Cube:
    def __init__(self, refs, keep, step, apart=1):
        (self.fin, self.give, self.c0, self.r1, self.r2), refs = refs[:5], refs[5:]
        self.s0, self.q0, self.s1, self.q1, self.s2, self.q2, self.s3, self.q3, self.s4, self.q4, self.kept = refs
        self.keep_of, self.step, self.apart = keep, step, apart
        self.gone = 6 * apart
        self.slots = self.gone + 1
        d = lax.axis_index("dp")
        self.c, self.x, self.y = d % 2, (d // 2) % 2, d // 4
        self.to_c, self.to_x, self.to_y = d + 1 - 2 * self.c, d + 2 - 4 * self.x, d + 4 - 8 * self.y
        self.stages = (self.stage1, self.stage2, self.stage3, self.stage4, self.stage5, self.retire)

    @classmethod
    def scratch(cls, block, apart=1):
        dma, n = pltpu.SemaphoreType.DMA, 6 * apart + 1
        return [
            pltpu.VMEM((n, 2, 2, 2, *block), BF16),
            pltpu.VMEM((n, 2, 2, *block), BF16),
            pltpu.VMEM((n, 2, 2, *block), BF16),
            pltpu.VMEM((n, 2, *block), BF16),
            pltpu.VMEM((n, 2, *block), BF16),
            *[dma((n,))] * 2,
            *[dma((n, 2))] * 6,
            *[dma((n,))] * 3,
        ]

    def peer(self, m):
        moves = (1 - 2 * self.c, 2 - 4 * self.x, 4 - 8 * self.y)
        return lax.axis_index("dp") + sum(move for bit, move in enumerate(moves) if m >> bit & 1)

    def slot(self, k):
        return lax.rem(k, self.slots)

    def half(self, k):
        p = self.slot(k)
        return remote(self.give.at[p], self.c0.at[p], self.s0.at[p], self.q0.at[p], "dp", self.to_c)

    def quarters(self, p):
        return self.fin.at[p, self.c, 0, self.x], self.fin.at[p, self.c, 1, self.y]

    def hop1(self, k):
        p, fin, c = self.slot(k), self.fin, self.c
        return (
            remote(fin.at[p, c, 0, 1 - self.x], self.r1.at[p, 0], self.s1.at[p, 0], self.q1.at[p, 0], "dp", self.to_x),
            remote(fin.at[p, c, 1, 1 - self.y], self.r1.at[p, 1], self.s1.at[p, 1], self.q1.at[p, 1], "dp", self.to_y),
        )

    def hop2(self, k):
        p = self.slot(k)
        a, b = self.quarters(p)
        return (
            remote(a, self.r2.at[p, 0], self.s2.at[p, 0], self.q2.at[p, 0], "dp", self.to_y),
            remote(b, self.r2.at[p, 1], self.s2.at[p, 1], self.q2.at[p, 1], "dp", self.to_x),
        )

    def hop3(self, k):
        p = self.slot(k)
        a, b = self.quarters(p)
        return (
            remote(a, a, self.s3.at[p, 0], self.q3.at[p, 0], "dp", self.to_x),
            remote(b, b, self.s3.at[p, 1], self.q3.at[p, 1], "dp", self.to_y),
        )

    def hop4(self, k):
        p = self.slot(k)
        mine = self.fin.at[p, self.c]
        return remote(mine, mine, self.s4.at[p], self.q4.at[p], "dp", self.to_c)

    def kept_wait(self, k):
        p = self.slot(k)
        pltpu.make_async_copy(self.fin.at[p], self.fin.at[p], self.kept.at[p]).wait()

    def add_quarters(self, k, got):
        p = self.slot(k)
        for j, quarter in enumerate(self.quarters(p)):
            add_rows(quarter, got.at[p, j], self.step)

    def stage1(self, k):
        self.half(k).wait()
        p = self.slot(k)
        for a in range(2):
            for b in range(2):
                add_rows(self.fin.at[p, self.c, a, b], self.c0.at[p, a, b], self.step)
        for one in self.hop1(k):
            one.start()

    def stage2(self, k):
        for one in self.hop1(k):
            one.wait()
        self.add_quarters(k, self.r1)
        for one in self.hop2(k):
            one.start()

    def stage3(self, k):
        for one in self.hop2(k):
            one.wait()
        self.add_quarters(k, self.r2)
        for one in self.hop3(k):
            one.start()

    def stage4(self, k):
        for one in self.hop3(k):
            one.wait_recv()
        self.hop4(k).start()

    def stage5(self, k):
        self.hop4(k).wait_recv()
        p = self.slot(k)
        self.keep_of(k, self.fin.at[p], self.kept.at[p])

    def retire(self, k):
        for one in self.hop3(k) + (self.hop4(k),):
            one.wait_send()
        self.kept_wait(k)

    def tick(self, t, count):
        for late, stage in reversed(tuple(enumerate(self.stages, 1))):
            k = t - late * self.apart

            @pl.when(between(k, count))
            def _(stage=stage, k=k):
                stage(k)


def weighted(left, right):
    return lax.dot_general(left, right, (((0,), (0,)), ((), ())), preferred_element_type=F32).astype(BF16)


def lane_half(odd):
    return (lax.broadcasted_iota(jnp.int32, (1, 2 * HD), 1) // HD == odd).astype(F32)


def head_backward(head, q, k, v, up, lse, slope, off, tile, grads, acc):
    q_grad, k_grad, v_grad = grads
    k_acc, v_acc = acc
    length = q.shape[0]
    odd = lax.rem(head, 2)
    mask = lane_half(odd).astype(BF16)
    lanes = pl.ds(pl.multiple_of((head // 2) * 2 * HD, 2 * HD), 2 * HD)
    scale = 1.0 / math.sqrt(HD)
    gain = slope[pl.ds(head, 1), 0:1]
    nt = (((1,), (1,)), ((), ()))
    for j in range(length // tile):
        rows = slice(j * tile, (j + 1) * tile)
        most = min(length, (j + 2) * tile)
        q_here = q[rows, lanes]
        up_here = up[rows, lanes] * mask
        k_here = k[0:most, lanes] * mask
        scores = lax.dot_general(k_here, q_here, nt, preferred_element_type=F32)
        probs = jnp.exp(scores * scale + gain * off[0:most, rows] - lse[pl.ds(head, 1), rows])
        back = lax.dot_general(v[0:most, lanes], up_here, nt, preferred_element_type=F32)
        delta = jnp.sum(probs * back, axis=0, keepdims=True)
        score_grad = (probs * (back - delta)).astype(BF16)
        v_part = jnp.dot(probs.astype(BF16), up_here, preferred_element_type=F32)
        k_part = jnp.dot(score_grad, q_here * mask, preferred_element_type=F32)
        if j == 0:
            v_acc[0:most, :] = v_part
            k_acc[0:most, :] = k_part
            if most < length:
                v_acc[most:length, :] = jnp.zeros((length - most, 2 * HD), F32)
                k_acc[most:length, :] = jnp.zeros((length - most, 2 * HD), F32)
        else:
            v_acc[0:most, :] += v_part
            k_acc[0:most, :] += k_part
        q_part = lax.dot_general(k_here, score_grad, (((0,), (0,)), ((), ())), preferred_element_type=F32)
        mine = (q_part.T * scale).astype(BF16)

        @pl.when(odd == 0)
        def _(rows=rows, mine=mine):
            q_grad[rows, lanes] = mine

        @pl.when(odd == 1)
        def _(rows=rows, mine=mine):
            q_grad[rows, lanes] += mine

    for to, got, factor in ((k_grad, k_acc, scale), (v_grad, v_acc, 1.0)):

        @pl.when(odd == 0)
        def _(to=to, got=got, factor=factor):
            to[:, lanes] = (got[...] * factor).astype(BF16)

        @pl.when(odd == 1)
        def _(to=to, got=got, factor=factor):
            to[:, lanes] += (got[...] * factor).astype(BF16)


ROWS_BACK = 48
BACK_SLOTS = 12
BACK_SLACK = 2
BACK_APART = 2
BACK_COLUMNS = 1024
HEAD_TILE = 256
PIECE = 256
GROUP = 4


def back_kernel(n, heads, *refs):
    (grad_h, mlp_h, activ_h, dy_h, second_h, pre_h, src_h, tot_h, w_h, normed_h, att_h, eb_h), refs = refs[:12], refs[12:]
    smalls_h, refs = refs[:8], refs[8:]
    (out_h, shrink_out, expand_out, wo_out, mix_out, input_h, small_out), refs = refs[:7], refs[7:]
    (left, dy, pre, src, tot, out, resid, w, att, eb), refs = refs[:10], refs[10:]
    smalls, refs = refs[:8], refs[8:]
    vec, wo, q, k, v, lse, slope, off = smalls
    (up, grads, k_acc, v_acc, cols, buf, got_small, last), refs = refs[:8], refs[8:]
    (load, left_sem, part_sem, row_sem, out_sem, ss, sq, ls, lq), refs = refs[:9], refs[9:]
    ring, refs = Ring(n, refs[:7], BACK_SLOTS, BACK_SLACK), refs[7:]
    chain = ring.chain
    width, local = dy.shape[1], q.shape[1]
    rows, per_sum = ROWS_BACK, grad_h.shape[0]
    loaded_z, total_z = 2 * per_sum, 3 * per_sum
    per_row = width // BACK_COLUMNS
    first = activ_h.shape[1] // PIECE
    total_left = first + second_h.shape[1] // PIECE
    to_output = total_left * per_row
    to_mixing = to_output + local // PIECE * per_row
    pair = BACK_COLUMNS // local
    per_matrix = width // PIECE // pair
    total_p = to_mixing + 3 * per_matrix

    def keep(p, piece_ref, sem):
        here = pl.ds(pl.multiple_of(lax.rem(p, per_row) * BACK_COLUMNS, BACK_COLUMNS), BACK_COLUMNS)
        for lo, hi, to in (
            (0, first * per_row, shrink_out),
            (first * per_row, to_output, expand_out),
            (to_output, to_mixing, wo_out),
        ):

            @pl.when(jnp.logical_and(p >= lo, p < hi))
            def _(lo=lo, to=to):
                pltpu.make_async_copy(piece_ref, to.at[(p - lo) // per_row, :, :, :, :, here], sem).start()

        @pl.when(p >= to_mixing)
        def _():
            i = p - to_mixing
            for j in range(pair):
                pltpu.make_async_copy(
                    piece_ref.at[:, :, :, :, pl.ds(j * local, local)],
                    mix_out.at[i // per_matrix, lax.rem(i, per_matrix) * pair + j],
                    sem,
                ).start()

    cube = Cube(refs, keep, PIECE // 8, BACK_APART)

    loads = [pltpu.make_async_copy(a, b, load.at[j]) for j, (a, b) in enumerate(zip(smalls_h, smalls))]
    pairs = ((dy_h, dy), (pre_h, pre), (w_h, w), (att_h, att), (eb_h, eb), (normed_h, dy))
    loads += [pltpu.make_async_copy(a, b, load.at[8 + j]) for j, (a, b) in enumerate(pairs)]

    def part_load(j, which):
        return pltpu.make_async_copy(
            (grad_h, mlp_h)[which].at[lax.rem(j, per_sum)], chain.part.at[ring.at(j)], part_sem.at[ring.at(j)]
        )

    def part_start(j):
        @pl.when(j < per_sum)
        def _():
            part_load(j, 0).start()

        @pl.when(between(j - per_sum, per_sum))
        def _():
            part_load(j, 1).start()

    def left_load(r, which):
        at = (r - which * first) * PIECE
        return pltpu.make_async_copy(
            (activ_h, second_h)[which].at[:, pl.ds(pl.multiple_of(at, PIECE), PIECE)],
            left.at[lax.rem(r, 2)],
            left_sem.at[lax.rem(r, 2)],
        )

    def left_start(r):
        @pl.when(r < first)
        def _():
            left_load(r, 0).start()

        @pl.when(between(r - first, total_left - first))
        def _():
            left_load(r, 1).start()

    def row_loads(j):
        at, chunk = lax.rem(j, 2), lax.rem(j, per_sum)
        return (
            pltpu.make_async_copy(src_h.at[chunk], src.at[at], row_sem.at[at, 0]),
            pltpu.make_async_copy(tot_h.at[chunk], tot.at[at], row_sem.at[at, 1]),
        )

    def out_store(j, to):
        at = lax.rem(j, 2)
        return pltpu.make_async_copy(out.at[at], to.at[lax.rem(j, per_sum)], out_sem.at[at])

    part_start(0)
    left_start(0)
    loads[8].start()
    part_start(1)
    for one in loads[:8] + [loads[9]]:
        one.start()
    barrier = pltpu.get_barrier_semaphore()
    chain.greet(barrier)
    for m in range(1, 8):
        pl.semaphore_signal(barrier, inc=1, device_id={"dp": cube.peer(m)}, device_id_type=MESH)
    cols[...] = jnp.zeros_like(cols)
    buf[...] = jnp.zeros_like(buf)
    chain.wait_greetings(barrier, 7)
    loads[8].wait()

    def product(p, columns, right):
        to = cube.slot(p)
        count = PIECE // 8
        for side, store in ((1 - cube.c, cube.give.at[to]), (cube.c, cube.fin.at[to, cube.c])):
            for j in range(BACK_COLUMNS // 512):
                got = weighted(columns(j, side), right(j))
                for a in range(2):
                    for b in range(2):
                        lo = (2 * a + b) * count
                        store[a, b, :, j * 512 : (j + 1) * 512] = got[lo : lo + count]

    half = PIECE // 2

    def produce(p):
        r, part = p // per_row, lax.rem(p, per_row)

        @pl.when(r < total_left)
        def _():
            at = lax.rem(r, 2)

            @pl.when(part == 0)
            def _():
                left_start(r + 1)
                pltpu.make_async_copy(activ_h.at[:, pl.ds(0, PIECE)], left.at[at], left_sem.at[at]).wait()

            def columns(j, side):
                return left[at, :, pl.ds(pl.multiple_of(side * half, half), half)]

            for which, ref in enumerate((dy, pre)):

                def right(j, ref=ref):
                    return ref[:, pl.ds(pl.multiple_of(part * BACK_COLUMNS + j * 512, 512), 512)]

                @pl.when((r >= first) == bool(which))
                def _(right=right):
                    product(p, columns, right)

        @pl.when(between(p - to_output, to_mixing - to_output))
        def _():
            tile = r - total_left

            def columns(j, side):
                return att[:, pl.ds(pl.multiple_of(tile * PIECE + side * half, half), half)]

            def right(j):
                return resid[:, pl.ds(pl.multiple_of(part * BACK_COLUMNS + j * 512, 512), 512)]

            product(p, columns, right)

        @pl.when(p >= to_mixing)
        def _():
            i = p - to_mixing
            tile = lax.rem(i, per_matrix) * pair

            def columns(j, side):
                return dy[:, pl.ds(pl.multiple_of((tile + j) * PIECE + side * half, half), half)]

            def right(j):
                return grads[i // per_matrix]

            product(p, columns, right)

        cube.half(p).start()

    def produce_rows(g):
        at = pl.ds(pl.multiple_of(g * GROUP * rows, GROUP * rows), GROUP * rows)
        for j in range(width // 512):
            here = pl.ds(j * 512, 512)
            total = sum(
                lax.dot_general(
                    grads[m, at, :], w[m, here, :], (((1,), (1,)), ((), ())), preferred_element_type=F32
                )
                for m in range(3)
            ).astype(BF16)
            for i in range(GROUP):
                chain.part[ring.at(loaded_z + g * GROUP + i), :, here] = total[i * rows : (i + 1) * rows]

    def row_sum(x):
        return jnp.sum(x, axis=-1, keepdims=True)

    def norm_back(values, downs, gain):
        centred = [one - row_sum(one) / width for one in values]
        spread = [lax.rsqrt(row_sum(one * one) / width + EPS) for one in centred]
        normal = [one * by for one, by in zip(centred, spread)]
        scaled = [one * gain for one in downs]
        flat = [row_sum(one) / width for one in scaled]
        slope_of = [row_sum(one * other) / width for one, other in zip(scaled, normal)]
        back = [
            by * (one - low - other * high)
            for by, one, low, other, high in zip(spread, scaled, flat, normal, slope_of)
        ]
        return normal, back

    def each_rows(j, what):
        step = 16
        start = lax.rem(j, per_sum) * rows
        what(
            [slice(i * step, (i + 1) * step) for i in range(rows // step)],
            [pl.ds(pl.multiple_of(start + i * step, step), step) for i in range(rows // step)],
        )

    def gather(start, *items):
        for c, item in enumerate(items):
            cols[start + c] += item[0:8] + item[8:16]

    def hidden_rows(at, here):
        return src[at, here, :].astype(F32) + (tot[at, here, :].astype(F32) + vec[0:1, :])

    def rows_back(j):
        at, slot = lax.rem(j, 2), ring.at(j)

        def what(heres, theres):
            downs = [chain.inner_in[slot, here, :].astype(F32) for here in heres]
            normals, backs = norm_back([hidden_rows(at, here) for here in heres], downs, vec[1:2, :])
            for there, down, normal, back in zip(theres, downs, normals, backs):
                given = dy[there, :].astype(F32)
                low = (back + given).astype(BF16)
                resid[there, :] = low
                gather(0, down * normal, down, low.astype(F32))
                gather(5, given)

        each_rows(j, what)
        there = pl.ds(pl.multiple_of(j * rows, rows), rows)
        up[there, :] = lax.dot_general(
            resid[there, :], wo[...], (((1,), (1,)), ((), ())), preferred_element_type=F32
        ).astype(BF16)

    def rows_out(j):
        at, slot = lax.rem(j, 2), ring.at(j)

        def what(heres, theres):
            for here in heres:
                out[at, here, :] = (
                    hidden_rows(at, here) + chain.inner_in[slot, here, :].astype(F32) + vec[5:6, :]
                ).astype(BF16)

        each_rows(j, what)
        out_store(j, out_h).start()

    def rows_front(j):
        at, slot = lax.rem(j, 2), ring.at(j)

        def what(heres, theres):
            downs = [chain.inner_in[slot, here, :].astype(F32) for here in heres]
            normals, backs = norm_back([src[at, here, :].astype(F32) for here in heres], downs, vec[4:5, :])
            for here, there, down, normal, back in zip(heres, theres, downs, normals, backs):
                out[at, here, :] = (back + resid[there, :].astype(F32)).astype(BF16)
                gather(3, down * normal, down)

        each_rows(j, what)
        out_store(j, input_h).start()

    def swap(j):
        to = (cube.to_c, cube.to_x, cube.to_y)[j]
        return remote(buf.at[j], got_small.at[j], ss.at[j], sq.at[j], "dp", to)

    def small_step(j):
        if j == 0:
            for row, item in ((2, cols[0]), (3, cols[1]), (4, cols[2]), (5, eb[...]), (6, cols[5])):
                buf[0, row : row + 1, :] = jnp.sum(item, axis=0, keepdims=True)
        else:
            swap(j - 1).wait()
            buf[j] = buf[j - 1] + got_small[j - 1]
        if j < 3:
            swap(j).start()

    def last_copy(m):
        return remote(last.at[0], last.at[m], ls.at[m], lq.at[m], "dp", cube.peer(m))

    def last_start():
        for row in range(2):
            last[0, row : row + 1, :] = jnp.sum(cols[3 + row], axis=0, keepdims=True)
        for m in range(1, 8):
            last_copy(m).start()

    def last_end():
        for m in range(1, 8):
            last_copy(m).wait()
        two = [last[m] + last[m + 1] for m in range(0, 8, 2)]
        buf[3, 0:2, :] = (two[0] + two[1]) + (two[2] + two[3])

    late = chain.most_lag + 1
    heads_at = late + per_sum

    def tick(t, carry):
        gone = t - ring.gone

        @pl.when(between(gone, total_z))
        def _():
            ring.retire(gone)

        part_start(t + 2)

        @pl.when(jnp.logical_and(between(t - loaded_z, per_sum), lax.rem(t - loaded_z, GROUP) == 0))
        def _():
            produce_rows((t - loaded_z) // GROUP)

        ready = t - chain.first

        @pl.when(between(ready, total_z))
        def _():
            @pl.when(ready < loaded_z)
            def _():
                part_load(ready, 0).wait()

            ring.reduce(ready)

        back = t - chain.lag

        @pl.when(between(back, total_z))
        def _():
            ring.spread(back)

        cube.tick(t, total_p)

        @pl.when(t == 2)
        def _():
            for one in loads[:8] + [loads[9]]:
                one.wait()
            for one in loads[10:13]:
                one.start()

        @pl.when(t == heads_at)
        def _():
            for one in loads[10:13]:
                one.wait()
            loads[13].start()

        @pl.when(t == to_mixing)
        def _():
            loads[13].wait()

        @pl.when(t < total_p)
        def _():
            produce(t)

        chunk = t - late

        @pl.when(between(chunk + 1, total_z))
        def _():
            for one in row_loads(chunk + 1):
                one.start()

        @pl.when(between(chunk - 2 - per_sum, total_z - per_sum))
        def _():
            out_store(chunk - 2, out_h).wait()

        @pl.when(between(chunk, total_z))
        def _():
            for one in row_loads(chunk):
                one.wait()

            for which, what in enumerate((rows_back, rows_out, rows_front)):

                @pl.when(between(chunk - which * per_sum, per_sum))
                def _(what=what):
                    what(chunk)

        head = t - heads_at

        @pl.when(between(head, heads))
        def _():
            head_backward(
                head, q, k, v, up, lse, slope, off, HEAD_TILE, (grads.at[0], grads.at[1], grads.at[2]), (k_acc, v_acc)
            )

        @pl.when(head == heads)
        def _():
            for j, m in enumerate((0, 2)):
                buf[0, 7:8, j * local : (j + 1) * local] = jnp.sum(
                    grads[m].astype(F32), axis=0, keepdims=True
                )

        for j in range(4):

            @pl.when(t == loaded_z + 2 + 2 * j)
            def _(j=j):
                small_step(j)

        for j, step in enumerate((last_start, last_end)):

            @pl.when(t == late + total_z + j)
            def _(step=step):
                step()

        return carry

    assert heads_at + heads <= loaded_z and heads_at + 1 < to_output
    lax.fori_loop(0, max(total_z + late + 2, total_p + cube.gone), tick, 0)
    small_store = pltpu.make_async_copy(buf.at[3], small_out, load.at[0])
    small_store.start()
    small_store.wait()


def back_call(n, grad, mlp, activ, dy, second, pre, src, tot, w, normed, att, eb, vec, wo, q, k, v, lse, slope, off):
    length, width = dy.shape
    local = q.shape[1]
    chunks = length // ROWS_BACK
    dma = pltpu.SemaphoreType.DMA

    def cut(one):
        return one.reshape(chunks, ROWS_BACK, one.shape[-1])

    smalls = (vec, wo, q, k, v, lse, slope, off)
    inputs = (cut(grad), cut(mlp), activ, dy, second, pre, cut(src), cut(tot), w, normed, att, eb, *smalls)
    piece = (2, 2, 2, PIECE // 8)
    shapes = [
        ((chunks, ROWS_BACK, width), BF16),
        ((activ.shape[1] // PIECE, *piece, width), BF16),
        ((second.shape[1] // PIECE, *piece, width), BF16),
        ((local // PIECE, *piece, width), BF16),
        ((3, width // PIECE, *piece, local), BF16),
        ((chunks, ROWS_BACK, width), BF16),
        ((8, width), F32),
    ]
    slots = BACK_SLOTS
    scratch = [
        pltpu.VMEM((2, length, PIECE), BF16),
        pltpu.VMEM(dy.shape, BF16),
        pltpu.VMEM(pre.shape, BF16),
        *[pltpu.VMEM((2, ROWS_BACK, width), BF16)] * 3,
        pltpu.VMEM(dy.shape, BF16),
        *[pltpu.VMEM(one.shape, one.dtype) for one in (w, att, eb)],
        *[pltpu.VMEM(one.shape, one.dtype) for one in smalls],
        pltpu.VMEM(q.shape, BF16),
        pltpu.VMEM((3, *q.shape), BF16),
        *[pltpu.VMEM((length, 2 * HD), F32)] * 2,
        pltpu.VMEM((6, 8, width), F32),
        pltpu.VMEM((4, 8, width), F32),
        pltpu.VMEM((3, 8, width), F32),
        pltpu.VMEM((8, 2, width), F32),
        dma((14,)),
        dma((2,)),
        dma((slots,)),
        dma((2, 2)),
        dma((2,)),
        dma((3,)),
        dma((3,)),
        dma((8,)),
        dma((8,)),
        *Chain.scratch(slots, (ROWS_BACK, width)),
        *Cube.scratch((PIECE // 8, BACK_COLUMNS), BACK_APART),
    ]
    return pl.pallas_call(
        functools.partial(back_kernel, n, local // HD),
        out_shape=[jax.ShapeDtypeStruct(*one) for one in shapes],
        in_specs=[pl.BlockSpec(memory_space=pl.ANY)] * len(inputs),
        out_specs=[pl.BlockSpec(memory_space=pl.ANY)] * len(shapes),
        scratch_shapes=scratch,
        compiler_params=pltpu.CompilerParams(
            collective_id=1, has_side_effects=True, vmem_limit_bytes=61 << 20
        ),
    )(*inputs)


def on_device(
    fast,
    n_tensor,
    inputs,
    block_ids,
    first_gain,
    first_shift,
    mixing_weight,
    mixing_bias,
    output_weight,
    output_bias,
    second_gain,
    second_shift,
    expand_weight,
    expand_bias,
    shrink_weight,
    shrink_bias,
    cotangent,
):
    source = inputs.astype(F32)
    upstream = cotangent.astype(F32)
    length, width = source.shape
    blocks = block_ids[0]
    local_width = mixing_weight.shape[2]
    local_heads = local_width // HD
    units = expand_weight.shape[1]
    first_head = lax.axis_index("tensor") * local_heads
    weights = mixing_weight.transpose(1, 0, 2)
    if fast:
        numbers = (first_head + jnp.arange(local_heads)).astype(F32)
        slope = jnp.broadcast_to((2.0 ** (-8.0 * (numbers + 1.0) / H))[:, None], (local_heads, 128))
        bias = jnp.stack([mixing_bias[0], jnp.zeros_like(mixing_bias[0]), mixing_bias[1]])
        normed_low, query, keys, vals, attended, logsum, off = head_call(
            inputs, weights, jnp.stack([first_gain, first_shift]), bias, slope, block_ids
        )
    else:
        normed_low = layer_norm(source, first_gain, first_shift).astype(BF16)

        def project(k):
            return jnp.dot(normed_low, weights[k], preferred_element_type=F32)

        query = (project(0) + mixing_bias[0]).astype(BF16).reshape(length, local_heads, HD)
        keys = project(1).astype(BF16).reshape(length, local_heads, HD)
        vals = (project(2) + mixing_bias[1]).astype(BF16).reshape(length, local_heads, HD)
        masked = biased_scores(query, keys, blocks, first_head)
        row_top = jnp.max(masked, axis=-1, keepdims=True)
        logsum = row_top + jnp.log(jnp.sum(jnp.exp(masked - row_top), axis=-1, keepdims=True))
        probs_low = jnp.exp(masked - logsum).astype(BF16)
        attended = (
            jnp.einsum("hqk,khd->qhd", probs_low, vals, preferred_element_type=F32)
            .reshape(length, local_width)
            .astype(BF16)
        )
    if fast:
        most = max(width, units)
        vectors = jnp.stack(
            [
                jnp.pad(one, (0, most - one.shape[0]))
                for one in (output_bias, second_gain, second_shift, expand_bias, first_gain, shrink_bias)
            ]
        )
        total, second_low, activ_low, pre_grad, partial_mlp, second_part, expand_bias_part = mlp_call(
            n_tensor, attended, output_weight, inputs, cotangent, expand_weight, shrink_weight, vectors
        )
    else:
        partial_out = jnp.dot(attended, output_weight, preferred_element_type=F32)
        resid = lax.psum(partial_out.astype(BF16), "tensor").astype(F32)
        hidden_state = source + (resid + output_bias)
        second_low = layer_norm(hidden_state, second_gain, second_shift).astype(BF16)
        pre_act = jnp.dot(second_low, expand_weight, preferred_element_type=F32) + expand_bias
        activ_low = gelu_exact(pre_act).astype(BF16)
        partial_mlp = jnp.dot(activ_low, shrink_weight, preferred_element_type=F32)
        act_grad = jnp.einsum("td,fd->tf", cotangent, shrink_weight, preferred_element_type=F32)
        _, gelu_pull = jax.vjp(gelu_exact, pre_act)
        pre_grad = gelu_pull(act_grad)[0].astype(BF16)
        expand_bias_part = jnp.sum(pre_grad.astype(F32), axis=0)
        second_part = jnp.einsum("tf,df->td", pre_grad, expand_weight, preferred_element_type=F32)
    if fast:
        outputs, shrink_sum, expand_sum, output_sum, mixing_sum, input_grad, small = back_call(
            n_tensor, second_part, partial_mlp, activ_low, cotangent, second_low, pre_grad, inputs, total,
            weights, normed_low, attended, expand_bias_part, vectors[:, :width], output_weight, query, keys, vals,
            logsum, slope, off,
        )
        outputs, input_grad = outputs.reshape(length, width), input_grad.reshape(length, width)
        shrink_weight_grad = shrink_sum.astype(F32).reshape(units, width)
        expand_weight_grad = expand_sum.astype(F32).reshape(width, units)
        mixing_weight_grad = mixing_sum.astype(F32).reshape(3, width, local_width).transpose(1, 0, 2)
        output_weight_grad = output_sum.astype(F32).reshape(local_width, width)
        first_gain_grad, first_shift_grad, second_gain_grad, second_shift_grad = small[0], small[1], small[2], small[3]
        output_bias_grad, expand_bias_grad, shrink_bias_grad = small[4], small[5], small[6]
        mixing_bias_grad = small[7, : 2 * local_width].reshape(2, local_width)
    else:
        shrink_bias_part = jnp.sum(upstream, axis=0)
        shrink_part = jnp.einsum("tf,td->fd", activ_low, cotangent, preferred_element_type=F32)
        expand_part = jnp.einsum("td,tf->df", second_low, pre_grad, preferred_element_type=F32)

        mlp_sum = lax.psum(partial_mlp.astype(BF16), "tensor").astype(F32)
        second_grad = lax.psum(second_part.astype(BF16), "tensor").astype(F32)
        outputs = (hidden_state + mlp_sum + shrink_bias).astype(BF16)
        hidden_grad, second_gain_part, second_shift_part = norm_backward(
            hidden_state, second_gain, second_shift, second_grad
        )
        hidden_grad = hidden_grad + upstream
        resid_low = hidden_grad.astype(BF16)
        output_part = jnp.einsum("tc,td->cd", attended, resid_low, preferred_element_type=F32)
        output_bias_part = jnp.sum(resid_low.astype(F32), axis=0)
        attended_grad = (
            jnp.einsum("td,cd->tc", resid_low, output_weight, preferred_element_type=F32)
            .astype(BF16)
            .reshape(length, local_heads, HD)
        )
        probs = jnp.exp(biased_scores(query, keys, blocks, first_head) - logsum)
        probs_low = probs.astype(BF16)
        prob_grad = jnp.einsum("qhd,khd->hqk", attended_grad, vals, preferred_element_type=F32)
        vals_grad = jnp.einsum(
            "hqk,qhd->khd", probs_low, attended_grad, preferred_element_type=F32
        ).astype(BF16)
        row_delta = jnp.sum(probs * prob_grad, axis=-1, keepdims=True)
        score_grad = (probs * (prob_grad - row_delta)).astype(BF16)
        scale_factor = 1.0 / math.sqrt(HD)
        query_grad = (
            jnp.einsum("hqk,khd->qhd", score_grad, keys, preferred_element_type=F32) * scale_factor
        ).astype(BF16)
        keys_grad = (
            jnp.einsum("hqk,qhd->khd", score_grad, query, preferred_element_type=F32) * scale_factor
        ).astype(BF16)
        grads = [one.reshape(length, local_width) for one in (query_grad, keys_grad, vals_grad)]
        mixing_bias_part = jnp.stack(
            [jnp.sum(grads[0].astype(F32), axis=0), jnp.sum(grads[2].astype(F32), axis=0)]
        )
        mixing_part = jnp.stack(
            [jnp.einsum("td,tc->dc", normed_low, one, preferred_element_type=F32) for one in grads]
        )
        normed_part = sum(
            jnp.einsum("tc,dc->td", one, weights[k], preferred_element_type=F32)
            for k, one in enumerate(grads)
        )
        normed_grad = lax.psum(normed_part.astype(BF16), "tensor").astype(F32)
        source_grad, first_gain_part, first_shift_part = norm_backward(
            source, first_gain, first_shift, normed_grad
        )
        input_grad = (source_grad + hidden_grad).astype(BF16)
        summed = lax.psum(
            (
                first_gain_part, first_shift_part, mixing_part, mixing_bias_part, output_part, output_bias_part,
                second_gain_part, second_shift_part, expand_part, expand_bias_part, shrink_part, shrink_bias_part,
            ),
            "dp",
        )
        first_gain_grad, first_shift_grad, mixing_weight_grad, mixing_bias_grad = summed[:4]
        mixing_weight_grad = mixing_weight_grad.transpose(1, 0, 2)
        output_weight_grad, output_bias_grad, second_gain_grad, second_shift_grad = summed[4:8]
        expand_weight_grad, expand_bias_grad, shrink_weight_grad, shrink_bias_grad = summed[8:]
    return (
        outputs,
        input_grad,
        first_gain_grad,
        first_shift_grad,
        mixing_weight_grad,
        mixing_bias_grad,
        output_weight_grad,
        output_bias_grad,
        second_gain_grad,
        second_shift_grad,
        expand_weight_grad,
        expand_bias_grad,
        shrink_weight_grad,
        shrink_bias_grad,
    )


def solution(mesh):
    in_specs = (
        P("dp", None),
        P("dp", None),
        P(),
        P(),
        P(None, None, "tensor"),
        P(None, "tensor"),
        P("tensor", None),
        P(),
        P(),
        P(),
        P(None, "tensor"),
        P("tensor"),
        P("tensor", None),
        P(),
        P("dp", None),
    )
    out_specs = (
        P("dp", None),
        P("dp", None),
        P(),
        P(),
        P(None, None, "tensor"),
        P(None, "tensor"),
        P("tensor", None),
        P(),
        P(),
        P(),
        P(None, "tensor"),
        P("tensor"),
        P("tensor", None),
        P(),
    )
    n_tensor = mesh.shape["tensor"]
    fast = mesh.shape["dp"] == 8 and n_tensor in (2, 4)
    return jax.shard_map(
        functools.partial(on_device, fast, n_tensor),
        mesh=mesh,
        in_specs=in_specs,
        out_specs=out_specs,
        check_vma=False,
    )
```

```python
import functools
import math

import jax
import jax.numpy as jnp
from jax import lax
from jax.experimental import pallas as pl
from jax.experimental.pallas import tpu as pltpu
from jax.sharding import PartitionSpec as P

H = 32
HD = 64
EPS = 1e-05
F32 = jnp.float32
BF16 = jnp.bfloat16
MESH = pl.DeviceIdType.MESH


def layer_norm(values, scale_gain, shift_bias):
    row_mean = jnp.mean(values, axis=-1, keepdims=True)
    centred = values - row_mean
    row_var = jnp.mean(centred * centred, axis=-1, keepdims=True)
    return centred * lax.rsqrt(row_var + EPS) * scale_gain + shift_bias


def norm_backward(values, scale_gain, shift_bias, upstream):
    _, pull_back = jax.vjp(layer_norm, values, scale_gain, shift_bias)
    return pull_back(upstream)


def gelu_exact(values):
    return jax.nn.gelu(values, approximate=False)


def biased_scores(query, keys, blocks, first_head):
    length, local_heads, head_width = query.shape
    scores = jnp.einsum("qhd,khd->hqk", query, keys, preferred_element_type=F32) * (
        1.0 / math.sqrt(head_width)
    )
    heads_index = (first_head + jnp.arange(local_heads)).astype(F32)
    slopes = 2.0 ** (-8.0 * (heads_index + 1.0) / H)
    places = jnp.arange(length)
    offsets = (places[None, :] - places[:, None]).astype(F32)
    scores = scores + slopes[:, None, None] * offsets[None]
    allowed = blocks[None, :] <= blocks[:, None]
    return jnp.where(allowed[None], scores, -1e30)


def add_rows(dst, src, step):
    rows = dst.shape[0]

    def body(i, carry):
        at = pl.ds(pl.multiple_of(i * step, step), step)
        dst[at, :] = (dst[at, :].astype(F32) + src[at, :].astype(F32)).astype(BF16)
        return carry

    lax.fori_loop(0, rows // step, body, 0)


def remote(src, dst, send, recv, axis, to):
    return pltpu.make_async_remote_copy(
        src_ref=src,
        dst_ref=dst,
        send_sem=send,
        recv_sem=recv,
        device_id={axis: to},
        device_id_type=MESH,
    )


class Chain:
    def __init__(self, n, refs, slack=1):
        self.part, self.outer_in, self.inner_in, self.s_in, self.s_out, self.r_outer, self.r_inner = refs
        i = lax.axis_index("tensor")
        left = i < n // 2
        depth = jnp.where(left, i, n - 1 - i)
        self.inner = jnp.where(left, i + 1, i - 1)
        self.has_outer = depth > 0
        self.outer = jnp.where(self.has_outer, jnp.where(left, i - 1, i + 1), self.inner)
        self.is_mid = depth == n // 2 - 1
        self.first = slack * depth
        self.lag = slack * (n - 1 - depth)
        self.most_lag = slack * (n - 1)

    @staticmethod
    def scratch(count, block):
        dma = pltpu.SemaphoreType.DMA
        return [pltpu.VMEM((count, *block), BF16)] * 3 + [dma((count,))] * 4

    def to_mid(self, k):
        return remote(
            self.part.at[k], self.inner_in.at[k], self.s_in.at[k], self.r_inner.at[k], "tensor", self.inner
        )

    def to_inner(self, k):
        return remote(
            self.part.at[k], self.outer_in.at[k], self.s_in.at[k], self.r_outer.at[k], "tensor", self.inner
        )

    def to_outer(self, k):
        return remote(
            self.inner_in.at[k], self.inner_in.at[k], self.s_out.at[k], self.r_inner.at[k], "tensor", self.outer
        )

    def greet(self, barrier):
        pl.semaphore_signal(barrier, inc=1, device_id={"tensor": self.inner}, device_id_type=MESH)

        @pl.when(self.has_outer)
        def _():
            pl.semaphore_signal(barrier, inc=1, device_id={"tensor": self.outer}, device_id_type=MESH)

    def wait_greetings(self, barrier, others):
        @pl.when(self.has_outer)
        def _():
            pl.semaphore_wait(barrier, others + 2)

        @pl.when(jnp.logical_not(self.has_outer))
        def _():
            pl.semaphore_wait(barrier, others + 1)

    def reduce(self, k):
        @pl.when(self.has_outer)
        def _():
            self.to_inner(k).wait_recv()
            add_rows(self.part.at[k], self.outer_in.at[k], 16)

        @pl.when(self.is_mid)
        def _():
            self.to_mid(k).start()

        @pl.when(jnp.logical_not(self.is_mid))
        def _():
            self.to_inner(k).start()

    def spread(self, k):
        self.to_mid(k).wait_recv()

        @pl.when(self.is_mid)
        def _():
            add_rows(self.inner_in.at[k], self.part.at[k], 16)

        @pl.when(self.has_outer)
        def _():
            self.to_outer(k).start()

    def drain(self, k):
        self.to_mid(k).wait_send()

        @pl.when(self.has_outer)
        def _():
            self.to_outer(k).wait_send()


def between(k, count):
    return jnp.logical_and(k >= 0, k < count)


def pair_forward(pair, q, k, v, slope, off, tile, attended, lse):
    length = q.shape[0]
    lanes = pl.ds(pl.multiple_of(pair * 2 * HD, 2 * HD), 2 * HD)
    masks = [lane_half(odd).astype(BF16) for odd in range(2)]
    gains = [slope[pl.ds(2 * pair + odd, 1), 0:1] for odd in range(2)]
    for j in range(length // tile):
        rows = slice(j * tile, (j + 1) * tile)
        most = min(length, (j + 2) * tile)
        here = q[rows, lanes]
        scores = [
            lax.dot_general(
                k[0:most, lanes], here * masks[odd], (((1,), (1,)), ((), ())), preferred_element_type=F32
            )
            for odd in range(2)
        ]
        got = []
        for odd in range(2):
            raised = scores[odd] * (1.0 / math.sqrt(HD)) + gains[odd] * off[0:most, rows]
            top = jnp.max(raised, axis=0, keepdims=True)
            raised = jnp.exp(raised - top)
            total = jnp.sum(raised, axis=0, keepdims=True)
            lse[pl.ds(2 * pair + odd, 1), rows] = top + jnp.log(total)
            probs = (raised * (1.0 / total)).astype(BF16)
            got.append(
                lax.dot_general(
                    v[0:most, lanes], probs, (((0,), (0,)), ((), ())), preferred_element_type=F32
                )
            )
        both = jnp.concatenate([got[0][:HD], got[1][HD:]], axis=0)
        attended[rows, lanes] = both.T.astype(BF16)


def head_kernel(heads, *refs):
    (src_h, w_h, vec_h, bias_h, slope_h, blocks_h), refs = refs[:6], refs[6:]
    (normed_h, q_h, k_h, v_h, att_h, lse_h, off_h), refs = refs[:7], refs[7:]
    (src, w, vec, bias, slope, blocks), refs = refs[:6], refs[6:]
    (normed, q, k, v, att, lse, off), refs = refs[:7], refs[7:]
    load, w_load, store = refs
    length, width = src.shape
    loads = [
        pltpu.make_async_copy(a, b, load.at[j])
        for j, (a, b) in enumerate(
            ((src_h, src), (vec_h, vec), (blocks_h, blocks), (bias_h, bias), (slope_h, slope))
        )
    ]
    w_loads = [pltpu.make_async_copy(w_h.at[m], w.at[m], w_load.at[m]) for m in range(3)]
    for one in loads + w_loads:
        one.start()
    for one in loads:
        one.wait()
    step, groups = 16, 4

    def normalize(i, carry):
        ats = [pl.ds(pl.multiple_of((i * groups + g) * step, step), step) for g in range(groups)]
        values = [src[at, :].astype(F32) for at in ats]
        centred = [one - jnp.sum(one, axis=-1, keepdims=True) / width for one in values]
        spread = [lax.rsqrt(jnp.sum(one * one, axis=-1, keepdims=True) / width + EPS) for one in centred]
        for at, one, by in zip(ats, centred, spread):
            normed[at, :] = (one * by * vec[0:1, :] + vec[1:2, :]).astype(BF16)
        return carry

    lax.fori_loop(0, length // (step * groups), normalize, 0)

    here = blocks[...].astype(F32)
    there = jnp.broadcast_to(here, (8, length)).T[:, 0:1]
    for j in range(length // 256):
        cols = slice(j * 256, (j + 1) * 256)
        distance = (
            lax.broadcasted_iota(jnp.int32, (length, 256), 0)
            - lax.broadcasted_iota(jnp.int32, (length, 256), 1)
            - j * 256
        ).astype(F32)
        off[:, cols] = jnp.where(there <= here[:, cols], distance, -1e30)

    for m, to in enumerate((q, k, v)):
        w_loads[m].wait()

        def project(i, carry, m=m, to=to):
            at = pl.ds(pl.multiple_of(i * 256, 256), 256)
            to[at, :] = (
                jnp.dot(normed[at, :], w[m], preferred_element_type=F32) + bias[m : m + 1, :]
            ).astype(BF16)
            return carry

        lax.fori_loop(0, length // 256, project, 0)

    stores = [
        pltpu.make_async_copy(a, b, store.at[j])
        for j, (a, b) in enumerate(
            ((normed, normed_h), (off, off_h), (q, q_h), (k, k_h), (v, v_h), (att, att_h), (lse, lse_h))
        )
    ]
    for one in stores[:5]:
        one.start()

    def attend(pair, carry):
        pair_forward(pair, q, k, v, slope, off, HEAD_TILE, att, lse)
        return carry

    lax.fori_loop(0, heads // 2, attend, 0)
    for one in stores[5:]:
        one.start()
    for one in stores:
        one.wait()


def head_call(src, w, vec, bias, slope, blocks):
    length, width = src.shape
    local = w.shape[2]
    heads = local // HD
    inputs = (src, w, vec, bias, slope, blocks)
    shapes = [
        ((length, width), BF16),
        *[((length, local), BF16)] * 4,
        ((heads, length), F32),
        ((length, length), F32),
    ]
    dma = pltpu.SemaphoreType.DMA
    return pl.pallas_call(
        functools.partial(head_kernel, heads),
        out_shape=[jax.ShapeDtypeStruct(*one) for one in shapes],
        in_specs=[pl.BlockSpec(memory_space=pl.ANY)] * len(inputs),
        out_specs=[pl.BlockSpec(memory_space=pl.ANY)] * len(shapes),
        scratch_shapes=[
            *[pltpu.VMEM(one.shape, one.dtype) for one in inputs],
            *[pltpu.VMEM(*one) for one in shapes],
            dma((5,)),
            dma((3,)),
            dma((7,)),
        ],
        compiler_params=pltpu.CompilerParams(vmem_limit_bytes=60 << 20),
    )(*inputs)


ROWS = 32
SLACK = 2
BLOCK_ROWS = 256
TILE = 1024


def mlp_kernel(n, length, *refs):
    (att_h, wo_h, src_h, dy_h, wu_h, wd_h, vec_h), refs = refs[:7], refs[7:]
    (tot_h, second_h, activ_h, pre_h, mlp_h, grad_h, bias_h), refs = refs[:7], refs[7:]
    (att, wo, src, dy, wu, wd, vec, second, activ, pre, mlp, grad, bias), refs = refs[:13], refs[13:]
    load, store, tot_store, *refs = refs
    chain = Chain(n, refs, SLACK)
    width = wo.shape[1]
    units = wu.shape[1]
    chunks = length // ROWS
    blocks = length // BLOCK_ROWS
    per_block = BLOCK_ROWS // ROWS
    group = 4

    loads = [
        pltpu.make_async_copy(a, b, load.at[k])
        for k, (a, b) in enumerate(
            ((att_h, att), (wo_h, wo), (vec_h, vec), (src_h, src), (wu_h, wu), (dy_h, dy), (wd_h, wd))
        )
    ]
    for one in loads:
        one.start()
    barrier = pltpu.get_barrier_semaphore()
    chain.greet(barrier)
    bias[...] = jnp.zeros_like(bias)
    chain.wait_greetings(barrier, 0)
    for one in loads[:3]:
        one.wait()

    def tot_copy(k):
        return pltpu.make_async_copy(chain.inner_in.at[k], tot_h.at[k], tot_store.at[k])

    def block_copies(b):
        at = pl.ds(pl.multiple_of(b * BLOCK_ROWS, BLOCK_ROWS), BLOCK_ROWS)
        pairs = ((second, second_h), (activ, activ_h), (pre, pre_h), (mlp, mlp_h), (grad, grad_h))
        return [
            pltpu.make_async_copy(a.at[at], h.at[at], store.at[b, j]) for j, (a, h) in enumerate(pairs)
        ]

    def produce(g):
        rows = group * ROWS
        left = att[pl.ds(pl.multiple_of(g * rows, rows), rows), :]
        for j in range(width // 512):
            cols = pl.ds(j * 512, 512)
            got = jnp.dot(left, wo[:, cols], preferred_element_type=F32).astype(BF16)
            for q in range(group):
                chain.part[g * group + q, :, cols] = got[q * ROWS : (q + 1) * ROWS]

    def normalize(b):
        step, groups = 16, 4

        def body(i, carry):
            ats, values = [], []
            for g in range(groups):
                r = i * groups + g
                at = pl.ds(pl.multiple_of(b * BLOCK_ROWS + r * step, step), step)
                k = b * per_block + r // (ROWS // step)
                inside = pl.ds(pl.multiple_of((r % (ROWS // step)) * step, step), step)
                ats.append(at)
                values.append(
                    src[at, :].astype(F32) + (chain.inner_in[k, inside, :].astype(F32) + vec[0:1, :width])
                )
            centred = [one - jnp.mean(one, axis=-1, keepdims=True) for one in values]
            spread = [lax.rsqrt(jnp.mean(one * one, axis=-1, keepdims=True) + EPS) for one in centred]
            for at, one, by in zip(ats, centred, spread):
                second[at, :] = (one * by * vec[1:2, :width] + vec[2:3, :width]).astype(BF16)
            return carry

        lax.fori_loop(0, BLOCK_ROWS // (step * groups), body, 0)

    def hidden_tile(b, j):
        at = pl.ds(pl.multiple_of(b * BLOCK_ROWS, BLOCK_ROWS), BLOCK_ROWS)
        cols = pl.ds(pl.multiple_of(j * TILE, TILE), TILE)
        value = jnp.dot(second[at, :], wu[:, cols], preferred_element_type=F32) + vec[3:4, cols]
        back = lax.dot_general(
            dy[at, :], wd[cols, :], (((1,), (1,)), ((), ())), preferred_element_type=F32
        )
        below = 0.5 + 0.5 * lax.erf(value * math.sqrt(0.5))
        density = jnp.exp(-0.5 * value * value) * (1.0 / math.sqrt(2.0 * math.pi))
        activ[at, cols] = (value * below).astype(BF16)
        low = (back * (below + value * density)).astype(BF16)
        pre[at, cols] = low
        bias[:, cols] += jnp.sum(low.astype(F32).reshape(BLOCK_ROWS // 8, 8, TILE), axis=0)

    def out_tile(b, j):
        at = pl.ds(pl.multiple_of(b * BLOCK_ROWS, BLOCK_ROWS), BLOCK_ROWS)
        cols = pl.ds(pl.multiple_of(j * TILE, TILE), TILE)
        mlp[at, cols] = jnp.dot(activ[at, :], wd[:, cols], preferred_element_type=F32).astype(BF16)
        grad[at, cols] = lax.dot_general(
            pre[at, :], wu[cols, :], (((1,), (1,)), ((), ())), preferred_element_type=F32
        ).astype(BF16)

    ahead = units // TILE
    steps = ahead + width // TILE
    per_tick = -(-steps // per_block)
    first_tick = per_block + chain.most_lag

    def tick(t, carry):
        @pl.when(jnp.logical_and(t % group == 0, t < chunks))
        def _():
            produce(t // group)

        ready = t - chain.first

        @pl.when(between(ready, chunks))
        def _():
            chain.reduce(ready)

        back = t - chain.lag

        @pl.when(between(back, chunks))
        def _():
            chain.spread(back)
            tot_copy(back).start()

        late = t - first_tick

        @pl.when(late == 0)
        def _():
            for one in loads[3:]:
                one.wait()

        @pl.when(between(late, blocks * per_block))
        def _():
            b = late // per_block
            for q in range(per_tick):
                s = (late % per_block) * per_tick + q

                @pl.when(s == 0)
                def _():
                    normalize(b)

                @pl.when(s < ahead)
                def _():
                    hidden_tile(b, s)

                @pl.when(between(s - ahead, width // TILE))
                def _():
                    out_tile(b, s - ahead)

                @pl.when(s == steps - 1)
                def _():
                    for one in block_copies(b):
                        one.start()

        return carry

    lax.fori_loop(0, chunks + first_tick, tick, 0)
    bias_copy = pltpu.make_async_copy(bias, bias_h, load.at[0])
    bias_copy.start()

    def drain(k, carry):
        chain.drain(k)
        tot_copy(k).wait()
        return carry

    lax.fori_loop(0, chunks, drain, 0)
    for b in range(blocks):
        for one in block_copies(b):
            one.wait()
    bias_copy.wait()


def mlp_call(n, att, wo, src, dy, wu, wd, vec):
    length, width = src.shape
    units = wu.shape[1]
    chunks = length // ROWS
    dma = pltpu.SemaphoreType.DMA
    inputs = (att, wo, src, dy, wu, wd, vec)
    outs = [(chunks, ROWS, width), (length, width), (length, units), (length, units)]
    outs += [(length, width), (length, width)]
    out_shape = [jax.ShapeDtypeStruct(one, BF16) for one in outs] + [jax.ShapeDtypeStruct((8, units), F32)]
    scratch = [pltpu.VMEM(one.shape, one.dtype) for one in inputs]
    scratch += [pltpu.VMEM(one.shape, one.dtype) for one in out_shape[1:]]
    scratch += [dma((7,)), dma((length // BLOCK_ROWS, 5)), dma((chunks,))]
    scratch += Chain.scratch(chunks, (ROWS, width))
    return pl.pallas_call(
        functools.partial(mlp_kernel, n, length),
        out_shape=out_shape,
        in_specs=[pl.BlockSpec(memory_space=pl.ANY)] * len(inputs),
        out_specs=[pl.BlockSpec(memory_space=pl.ANY)] * len(out_shape),
        scratch_shapes=scratch,
        compiler_params=pltpu.CompilerParams(
            collective_id=0, has_side_effects=True, vmem_limit_bytes=60 << 20
        ),
    )(*inputs)


class Ring:
    def __init__(self, n, refs, slots, slack):
        self.chain = Chain(n, refs, slack)
        self.slots = slots
        self.gone = self.chain.most_lag + 2

    def at(self, k):
        return lax.rem(k, self.slots)

    def reduce(self, k):
        self.chain.reduce(self.at(k))

    def spread(self, k):
        self.chain.spread(self.at(k))

    def retire(self, k):
        self.chain.drain(self.at(k))


class Cube:
    def __init__(self, refs, keep, step, apart=1):
        (self.fin, self.give, self.c0, self.r1, self.r2), refs = refs[:5], refs[5:]
        self.s0, self.q0, self.s1, self.q1, self.s2, self.q2, self.s3, self.q3, self.s4, self.q4, self.kept = refs
        self.keep_of, self.step, self.apart = keep, step, apart
        self.gone = 6 * apart
        self.slots = self.gone + 1
        d = lax.axis_index("dp")
        self.c, self.x, self.y = d % 2, (d // 2) % 2, d // 4
        self.to_c, self.to_x, self.to_y = d + 1 - 2 * self.c, d + 2 - 4 * self.x, d + 4 - 8 * self.y
        self.stages = (self.stage1, self.stage2, self.stage3, self.stage4, self.stage5, self.retire)

    @classmethod
    def scratch(cls, block, apart=1):
        dma, n = pltpu.SemaphoreType.DMA, 6 * apart + 1
        return [
            pltpu.VMEM((n, 2, 2, 2, *block), BF16),
            pltpu.VMEM((n, 2, 2, *block), BF16),
            pltpu.VMEM((n, 2, 2, *block), BF16),
            pltpu.VMEM((n, 2, *block), BF16),
            pltpu.VMEM((n, 2, *block), BF16),
            *[dma((n,))] * 2,
            *[dma((n, 2))] * 6,
            *[dma((n,))] * 3,
        ]

    def peer(self, m):
        moves = (1 - 2 * self.c, 2 - 4 * self.x, 4 - 8 * self.y)
        return lax.axis_index("dp") + sum(move for bit, move in enumerate(moves) if m >> bit & 1)

    def slot(self, k):
        return lax.rem(k, self.slots)

    def half(self, k):
        p = self.slot(k)
        return remote(self.give.at[p], self.c0.at[p], self.s0.at[p], self.q0.at[p], "dp", self.to_c)

    def quarters(self, p):
        return self.fin.at[p, self.c, 0, self.x], self.fin.at[p, self.c, 1, self.y]

    def hop1(self, k):
        p, fin, c = self.slot(k), self.fin, self.c
        return (
            remote(fin.at[p, c, 0, 1 - self.x], self.r1.at[p, 0], self.s1.at[p, 0], self.q1.at[p, 0], "dp", self.to_x),
            remote(fin.at[p, c, 1, 1 - self.y], self.r1.at[p, 1], self.s1.at[p, 1], self.q1.at[p, 1], "dp", self.to_y),
        )

    def hop2(self, k):
        p = self.slot(k)
        a, b = self.quarters(p)
        return (
            remote(a, self.r2.at[p, 0], self.s2.at[p, 0], self.q2.at[p, 0], "dp", self.to_y),
            remote(b, self.r2.at[p, 1], self.s2.at[p, 1], self.q2.at[p, 1], "dp", self.to_x),
        )

    def hop3(self, k):
        p = self.slot(k)
        a, b = self.quarters(p)
        return (
            remote(a, a, self.s3.at[p, 0], self.q3.at[p, 0], "dp", self.to_x),
            remote(b, b, self.s3.at[p, 1], self.q3.at[p, 1], "dp", self.to_y),
        )

    def hop4(self, k):
        p = self.slot(k)
        mine = self.fin.at[p, self.c]
        return remote(mine, mine, self.s4.at[p], self.q4.at[p], "dp", self.to_c)

    def kept_wait(self, k):
        p = self.slot(k)
        pltpu.make_async_copy(self.fin.at[p], self.fin.at[p], self.kept.at[p]).wait()

    def add_quarters(self, k, got):
        p = self.slot(k)
        for j, quarter in enumerate(self.quarters(p)):
            add_rows(quarter, got.at[p, j], self.step)

    def stage1(self, k):
        self.half(k).wait()
        p = self.slot(k)
        for a in range(2):
            for b in range(2):
                add_rows(self.fin.at[p, self.c, a, b], self.c0.at[p, a, b], self.step)
        for one in self.hop1(k):
            one.start()

    def stage2(self, k):
        for one in self.hop1(k):
            one.wait()
        self.add_quarters(k, self.r1)
        for one in self.hop2(k):
            one.start()

    def stage3(self, k):
        for one in self.hop2(k):
            one.wait()
        self.add_quarters(k, self.r2)
        for one in self.hop3(k):
            one.start()

    def stage4(self, k):
        for one in self.hop3(k):
            one.wait_recv()
        self.hop4(k).start()

    def stage5(self, k):
        self.hop4(k).wait_recv()
        p = self.slot(k)
        self.keep_of(k, self.fin.at[p], self.kept.at[p])

    def retire(self, k):
        for one in self.hop3(k) + (self.hop4(k),):
            one.wait_send()
        self.kept_wait(k)

    def tick(self, t, count):
        for late, stage in reversed(tuple(enumerate(self.stages, 1))):
            k = t - late * self.apart

            @pl.when(between(k, count))
            def _(stage=stage, k=k):
                stage(k)


def weighted(left, right):
    return lax.dot_general(left, right, (((0,), (0,)), ((), ())), preferred_element_type=F32).astype(BF16)


def lane_half(odd):
    return (lax.broadcasted_iota(jnp.int32, (1, 2 * HD), 1) // HD == odd).astype(F32)


def head_backward(head, q, k, v, up, lse, slope, off, tile, grads, acc):
    q_grad, k_grad, v_grad = grads
    k_acc, v_acc = acc
    length = q.shape[0]
    odd = lax.rem(head, 2)
    mask = lane_half(odd).astype(BF16)
    lanes = pl.ds(pl.multiple_of((head // 2) * 2 * HD, 2 * HD), 2 * HD)
    scale = 1.0 / math.sqrt(HD)
    gain = slope[pl.ds(head, 1), 0:1]
    nt = (((1,), (1,)), ((), ()))
    for j in range(length // tile):
        rows = slice(j * tile, (j + 1) * tile)
        most = min(length, (j + 2) * tile)
        q_here = q[rows, lanes]
        up_here = up[rows, lanes] * mask
        k_here = k[0:most, lanes] * mask
        scores = lax.dot_general(k_here, q_here, nt, preferred_element_type=F32)
        probs = jnp.exp(scores * scale + gain * off[0:most, rows] - lse[pl.ds(head, 1), rows])
        back = lax.dot_general(v[0:most, lanes], up_here, nt, preferred_element_type=F32)
        delta = jnp.sum(probs * back, axis=0, keepdims=True)
        score_grad = (probs * (back - delta)).astype(BF16)
        v_part = jnp.dot(probs.astype(BF16), up_here, preferred_element_type=F32)
        k_part = jnp.dot(score_grad, q_here * mask, preferred_element_type=F32)
        if j == 0:
            v_acc[0:most, :] = v_part
            k_acc[0:most, :] = k_part
            if most < length:
                v_acc[most:length, :] = jnp.zeros((length - most, 2 * HD), F32)
                k_acc[most:length, :] = jnp.zeros((length - most, 2 * HD), F32)
        else:
            v_acc[0:most, :] += v_part
            k_acc[0:most, :] += k_part
        q_part = lax.dot_general(k_here, score_grad, (((0,), (0,)), ((), ())), preferred_element_type=F32)
        mine = (q_part.T * scale).astype(BF16)

        @pl.when(odd == 0)
        def _(rows=rows, mine=mine):
            q_grad[rows, lanes] = mine

        @pl.when(odd == 1)
        def _(rows=rows, mine=mine):
            q_grad[rows, lanes] += mine

    for to, got, factor in ((k_grad, k_acc, scale), (v_grad, v_acc, 1.0)):

        @pl.when(odd == 0)
        def _(to=to, got=got, factor=factor):
            to[:, lanes] = (got[...] * factor).astype(BF16)

        @pl.when(odd == 1)
        def _(to=to, got=got, factor=factor):
            to[:, lanes] += (got[...] * factor).astype(BF16)


ROWS_BACK = 48
BACK_SLOTS = 12
BACK_SLACK = 2
BACK_APART = 2
BACK_COLUMNS = 1024
HEAD_TILE = 256
PIECE = 256
GROUP = 4


def back_kernel(n, heads, *refs):
    (grad_h, mlp_h, activ_h, dy_h, second_h, pre_h, src_h, tot_h, w_h, normed_h, att_h, eb_h), refs = refs[:12], refs[12:]
    smalls_h, refs = refs[:8], refs[8:]
    (out_h, shrink_out, expand_out, wo_out, mix_out, input_h, small_out), refs = refs[:7], refs[7:]
    (left, dy, pre, src, tot, out, resid, w, att, eb), refs = refs[:10], refs[10:]
    smalls, refs = refs[:8], refs[8:]
    vec, wo, q, k, v, lse, slope, off = smalls
    (up, grads, k_acc, v_acc, cols, buf, got_small, last), refs = refs[:8], refs[8:]
    (load, left_sem, part_sem, row_sem, out_sem, ss, sq, ls, lq), refs = refs[:9], refs[9:]
    ring, refs = Ring(n, refs[:7], BACK_SLOTS, BACK_SLACK), refs[7:]
    chain = ring.chain
    width, local = dy.shape[1], q.shape[1]
    rows, per_sum = ROWS_BACK, grad_h.shape[0]
    loaded_z, total_z = 2 * per_sum, 3 * per_sum
    per_row = width // BACK_COLUMNS
    first = activ_h.shape[1] // PIECE
    total_left = first + second_h.shape[1] // PIECE
    to_output = total_left * per_row
    to_mixing = to_output + local // PIECE * per_row
    pair = BACK_COLUMNS // local
    per_matrix = width // PIECE // pair
    total_p = to_mixing + 3 * per_matrix

    def keep(p, piece_ref, sem):
        here = pl.ds(pl.multiple_of(lax.rem(p, per_row) * BACK_COLUMNS, BACK_COLUMNS), BACK_COLUMNS)
        for lo, hi, to in (
            (0, first * per_row, shrink_out),
            (first * per_row, to_output, expand_out),
            (to_output, to_mixing, wo_out),
        ):

            @pl.when(jnp.logical_and(p >= lo, p < hi))
            def _(lo=lo, to=to):
                pltpu.make_async_copy(piece_ref, to.at[(p - lo) // per_row, :, :, :, :, here], sem).start()

        @pl.when(p >= to_mixing)
        def _():
            i = p - to_mixing
            for j in range(pair):
                pltpu.make_async_copy(
                    piece_ref.at[:, :, :, :, pl.ds(j * local, local)],
                    mix_out.at[i // per_matrix, lax.rem(i, per_matrix) * pair + j],
                    sem,
                ).start()

    cube = Cube(refs, keep, PIECE // 8, BACK_APART)

    loads = [pltpu.make_async_copy(a, b, load.at[j]) for j, (a, b) in enumerate(zip(smalls_h, smalls))]
    pairs = ((dy_h, dy), (pre_h, pre), (w_h, w), (att_h, att), (eb_h, eb), (normed_h, dy))
    loads += [pltpu.make_async_copy(a, b, load.at[8 + j]) for j, (a, b) in enumerate(pairs)]

    def part_load(j, which):
        return pltpu.make_async_copy(
            (grad_h, mlp_h)[which].at[lax.rem(j, per_sum)], chain.part.at[ring.at(j)], part_sem.at[ring.at(j)]
        )

    def part_start(j):
        @pl.when(j < per_sum)
        def _():
            part_load(j, 0).start()

        @pl.when(between(j - per_sum, per_sum))
        def _():
            part_load(j, 1).start()

    def left_load(r, which):
        at = (r - which * first) * PIECE
        return pltpu.make_async_copy(
            (activ_h, second_h)[which].at[:, pl.ds(pl.multiple_of(at, PIECE), PIECE)],
            left.at[lax.rem(r, 2)],
            left_sem.at[lax.rem(r, 2)],
        )

    def left_start(r):
        @pl.when(r < first)
        def _():
            left_load(r, 0).start()

        @pl.when(between(r - first, total_left - first))
        def _():
            left_load(r, 1).start()

    def row_loads(j):
        at, chunk = lax.rem(j, 2), lax.rem(j, per_sum)
        return (
            pltpu.make_async_copy(src_h.at[chunk], src.at[at], row_sem.at[at, 0]),
            pltpu.make_async_copy(tot_h.at[chunk], tot.at[at], row_sem.at[at, 1]),
        )

    def out_store(j, to):
        at = lax.rem(j, 2)
        return pltpu.make_async_copy(out.at[at], to.at[lax.rem(j, per_sum)], out_sem.at[at])

    part_start(0)
    left_start(0)
    loads[8].start()
    part_start(1)
    for one in loads[:8] + [loads[9]]:
        one.start()
    barrier = pltpu.get_barrier_semaphore()
    chain.greet(barrier)
    for m in range(1, 8):
        pl.semaphore_signal(barrier, inc=1, device_id={"dp": cube.peer(m)}, device_id_type=MESH)
    cols[...] = jnp.zeros_like(cols)
    buf[...] = jnp.zeros_like(buf)
    chain.wait_greetings(barrier, 7)
    loads[8].wait()

    def product(p, columns, right):
        to = cube.slot(p)
        count = PIECE // 8
        for side, store in ((1 - cube.c, cube.give.at[to]), (cube.c, cube.fin.at[to, cube.c])):
            for j in range(BACK_COLUMNS // 512):
                got = weighted(columns(j, side), right(j))
                for a in range(2):
                    for b in range(2):
                        lo = (2 * a + b) * count
                        store[a, b, :, j * 512 : (j + 1) * 512] = got[lo : lo + count]

    half = PIECE // 2

    def produce(p):
        r, part = p // per_row, lax.rem(p, per_row)

        @pl.when(r < total_left)
        def _():
            at = lax.rem(r, 2)

            @pl.when(part == 0)
            def _():
                left_start(r + 1)
                pltpu.make_async_copy(activ_h.at[:, pl.ds(0, PIECE)], left.at[at], left_sem.at[at]).wait()

            def columns(j, side):
                return left[at, :, pl.ds(pl.multiple_of(side * half, half), half)]

            for which, ref in enumerate((dy, pre)):

                def right(j, ref=ref):
                    return ref[:, pl.ds(pl.multiple_of(part * BACK_COLUMNS + j * 512, 512), 512)]

                @pl.when((r >= first) == bool(which))
                def _(right=right):
                    product(p, columns, right)

        @pl.when(between(p - to_output, to_mixing - to_output))
        def _():
            tile = r - total_left

            def columns(j, side):
                return att[:, pl.ds(pl.multiple_of(tile * PIECE + side * half, half), half)]

            def right(j):
                return resid[:, pl.ds(pl.multiple_of(part * BACK_COLUMNS + j * 512, 512), 512)]

            product(p, columns, right)

        @pl.when(p >= to_mixing)
        def _():
            i = p - to_mixing
            tile = lax.rem(i, per_matrix) * pair

            def columns(j, side):
                return dy[:, pl.ds(pl.multiple_of((tile + j) * PIECE + side * half, half), half)]

            def right(j):
                return grads[i // per_matrix]

            product(p, columns, right)

        cube.half(p).start()

    def produce_rows(g):
        at = pl.ds(pl.multiple_of(g * GROUP * rows, GROUP * rows), GROUP * rows)
        for j in range(width // 512):
            here = pl.ds(j * 512, 512)
            total = sum(
                lax.dot_general(
                    grads[m, at, :], w[m, here, :], (((1,), (1,)), ((), ())), preferred_element_type=F32
                )
                for m in range(3)
            ).astype(BF16)
            for i in range(GROUP):
                chain.part[ring.at(loaded_z + g * GROUP + i), :, here] = total[i * rows : (i + 1) * rows]

    def row_sum(x):
        return jnp.sum(x, axis=-1, keepdims=True)

    def norm_back(values, downs, gain):
        centred = [one - row_sum(one) / width for one in values]
        spread = [lax.rsqrt(row_sum(one * one) / width + EPS) for one in centred]
        normal = [one * by for one, by in zip(centred, spread)]
        scaled = [one * gain for one in downs]
        flat = [row_sum(one) / width for one in scaled]
        slope_of = [row_sum(one * other) / width for one, other in zip(scaled, normal)]
        back = [
            by * (one - low - other * high)
            for by, one, low, other, high in zip(spread, scaled, flat, normal, slope_of)
        ]
        return normal, back

    def each_rows(j, what):
        step = 16
        start = lax.rem(j, per_sum) * rows
        what(
            [slice(i * step, (i + 1) * step) for i in range(rows // step)],
            [pl.ds(pl.multiple_of(start + i * step, step), step) for i in range(rows // step)],
        )

    def gather(start, *items):
        for c, item in enumerate(items):
            cols[start + c] += item[0:8] + item[8:16]

    def hidden_rows(at, here):
        return src[at, here, :].astype(F32) + (tot[at, here, :].astype(F32) + vec[0:1, :])

    def rows_back(j):
        at, slot = lax.rem(j, 2), ring.at(j)

        def what(heres, theres):
            downs = [chain.inner_in[slot, here, :].astype(F32) for here in heres]
            normals, backs = norm_back([hidden_rows(at, here) for here in heres], downs, vec[1:2, :])
            for there, down, normal, back in zip(theres, downs, normals, backs):
                given = dy[there, :].astype(F32)
                low = (back + given).astype(BF16)
                resid[there, :] = low
                gather(0, down * normal, down, low.astype(F32))
                gather(5, given)

        each_rows(j, what)
        there = pl.ds(pl.multiple_of(j * rows, rows), rows)
        up[there, :] = lax.dot_general(
            resid[there, :], wo[...], (((1,), (1,)), ((), ())), preferred_element_type=F32
        ).astype(BF16)

    def rows_out(j):
        at, slot = lax.rem(j, 2), ring.at(j)

        def what(heres, theres):
            for here in heres:
                out[at, here, :] = (
                    hidden_rows(at, here) + chain.inner_in[slot, here, :].astype(F32) + vec[5:6, :]
                ).astype(BF16)

        each_rows(j, what)
        out_store(j, out_h).start()

    def rows_front(j):
        at, slot = lax.rem(j, 2), ring.at(j)

        def what(heres, theres):
            downs = [chain.inner_in[slot, here, :].astype(F32) for here in heres]
            normals, backs = norm_back([src[at, here, :].astype(F32) for here in heres], downs, vec[4:5, :])
            for here, there, down, normal, back in zip(heres, theres, downs, normals, backs):
                out[at, here, :] = (back + resid[there, :].astype(F32)).astype(BF16)
                gather(3, down * normal, down)

        each_rows(j, what)
        out_store(j, input_h).start()

    def swap(j):
        to = (cube.to_c, cube.to_x, cube.to_y)[j]
        return remote(buf.at[j], got_small.at[j], ss.at[j], sq.at[j], "dp", to)

    def small_step(j):
        if j == 0:
            for row, item in ((2, cols[0]), (3, cols[1]), (4, cols[2]), (5, eb[...]), (6, cols[5])):
                buf[0, row : row + 1, :] = jnp.sum(item, axis=0, keepdims=True)
        else:
            swap(j - 1).wait()
            buf[j] = buf[j - 1] + got_small[j - 1]
        if j < 3:
            swap(j).start()

    def last_copy(m):
        return remote(last.at[0], last.at[m], ls.at[m], lq.at[m], "dp", cube.peer(m))

    def last_start():
        for row in range(2):
            last[0, row : row + 1, :] = jnp.sum(cols[3 + row], axis=0, keepdims=True)
        for m in range(1, 8):
            last_copy(m).start()

    def last_end():
        for m in range(1, 8):
            last_copy(m).wait()
        two = [last[m] + last[m + 1] for m in range(0, 8, 2)]
        buf[3, 0:2, :] = (two[0] + two[1]) + (two[2] + two[3])

    late = chain.most_lag + 1
    heads_at = late + per_sum

    def tick(t, carry):
        gone = t - ring.gone

        @pl.when(between(gone, total_z))
        def _():
            ring.retire(gone)

        part_start(t + 2)

        @pl.when(jnp.logical_and(between(t - loaded_z, per_sum), lax.rem(t - loaded_z, GROUP) == 0))
        def _():
            produce_rows((t - loaded_z) // GROUP)

        ready = t - chain.first

        @pl.when(between(ready, total_z))
        def _():
            @pl.when(ready < loaded_z)
            def _():
                part_load(ready, 0).wait()

            ring.reduce(ready)

        back = t - chain.lag

        @pl.when(between(back, total_z))
        def _():
            ring.spread(back)

        cube.tick(t, total_p)

        @pl.when(t == 2)
        def _():
            for one in loads[:8] + [loads[9]]:
                one.wait()
            for one in loads[10:13]:
                one.start()

        @pl.when(t == heads_at)
        def _():
            for one in loads[10:13]:
                one.wait()
            loads[13].start()

        @pl.when(t == to_mixing)
        def _():
            loads[13].wait()

        @pl.when(t < total_p)
        def _():
            produce(t)

        chunk = t - late

        @pl.when(between(chunk + 1, total_z))
        def _():
            for one in row_loads(chunk + 1):
                one.start()

        @pl.when(between(chunk - 2 - per_sum, total_z - per_sum))
        def _():
            out_store(chunk - 2, out_h).wait()

        @pl.when(between(chunk, total_z))
        def _():
            for one in row_loads(chunk):
                one.wait()

            for which, what in enumerate((rows_back, rows_out, rows_front)):

                @pl.when(between(chunk - which * per_sum, per_sum))
                def _(what=what):
                    what(chunk)

        head = t - heads_at

        @pl.when(between(head, heads))
        def _():
            head_backward(
                head, q, k, v, up, lse, slope, off, HEAD_TILE, (grads.at[0], grads.at[1], grads.at[2]), (k_acc, v_acc)
            )

        @pl.when(head == heads)
        def _():
            for j, m in enumerate((0, 2)):
                buf[0, 7:8, j * local : (j + 1) * local] = jnp.sum(
                    grads[m].astype(F32), axis=0, keepdims=True
                )

        for j in range(4):

            @pl.when(t == loaded_z + 2 + 2 * j)
            def _(j=j):
                small_step(j)

        for j, step in enumerate((last_start, last_end)):

            @pl.when(t == late + total_z + j)
            def _(step=step):
                step()

        return carry

    assert heads_at + heads <= loaded_z and heads_at + 1 < to_output
    lax.fori_loop(0, max(total_z + late + 2, total_p + cube.gone), tick, 0)
    small_store = pltpu.make_async_copy(buf.at[3], small_out, load.at[0])
    small_store.start()
    small_store.wait()


def back_call(n, grad, mlp, activ, dy, second, pre, src, tot, w, normed, att, eb, vec, wo, q, k, v, lse, slope, off):
    length, width = dy.shape
    local = q.shape[1]
    chunks = length // ROWS_BACK
    dma = pltpu.SemaphoreType.DMA

    def cut(one):
        return one.reshape(chunks, ROWS_BACK, one.shape[-1])

    smalls = (vec, wo, q, k, v, lse, slope, off)
    inputs = (cut(grad), cut(mlp), activ, dy, second, pre, cut(src), cut(tot), w, normed, att, eb, *smalls)
    piece = (2, 2, 2, PIECE // 8)
    shapes = [
        ((chunks, ROWS_BACK, width), BF16),
        ((activ.shape[1] // PIECE, *piece, width), BF16),
        ((second.shape[1] // PIECE, *piece, width), BF16),
        ((local // PIECE, *piece, width), BF16),
        ((3, width // PIECE, *piece, local), BF16),
        ((chunks, ROWS_BACK, width), BF16),
        ((8, width), F32),
    ]
    slots = BACK_SLOTS
    scratch = [
        pltpu.VMEM((2, length, PIECE), BF16),
        pltpu.VMEM(dy.shape, BF16),
        pltpu.VMEM(pre.shape, BF16),
        *[pltpu.VMEM((2, ROWS_BACK, width), BF16)] * 3,
        pltpu.VMEM(dy.shape, BF16),
        *[pltpu.VMEM(one.shape, one.dtype) for one in (w, att, eb)],
        *[pltpu.VMEM(one.shape, one.dtype) for one in smalls],
        pltpu.VMEM(q.shape, BF16),
        pltpu.VMEM((3, *q.shape), BF16),
        *[pltpu.VMEM((length, 2 * HD), F32)] * 2,
        pltpu.VMEM((6, 8, width), F32),
        pltpu.VMEM((4, 8, width), F32),
        pltpu.VMEM((3, 8, width), F32),
        pltpu.VMEM((8, 2, width), F32),
        dma((14,)),
        dma((2,)),
        dma((slots,)),
        dma((2, 2)),
        dma((2,)),
        dma((3,)),
        dma((3,)),
        dma((8,)),
        dma((8,)),
        *Chain.scratch(slots, (ROWS_BACK, width)),
        *Cube.scratch((PIECE // 8, BACK_COLUMNS), BACK_APART),
    ]
    return pl.pallas_call(
        functools.partial(back_kernel, n, local // HD),
        out_shape=[jax.ShapeDtypeStruct(*one) for one in shapes],
        in_specs=[pl.BlockSpec(memory_space=pl.ANY)] * len(inputs),
        out_specs=[pl.BlockSpec(memory_space=pl.ANY)] * len(shapes),
        scratch_shapes=scratch,
        compiler_params=pltpu.CompilerParams(
            collective_id=1, has_side_effects=True, vmem_limit_bytes=61 << 20
        ),
    )(*inputs)


def on_device(
    fast,
    n_tensor,
    inputs,
    block_ids,
    first_gain,
    first_shift,
    mixing_weight,
    mixing_bias,
    output_weight,
    output_bias,
    second_gain,
    second_shift,
    expand_weight,
    expand_bias,
    shrink_weight,
    shrink_bias,
    cotangent,
):
    source = inputs.astype(F32)
    upstream = cotangent.astype(F32)
    length, width = source.shape
    blocks = block_ids[0]
    local_width = mixing_weight.shape[2]
    local_heads = local_width // HD
    units = expand_weight.shape[1]
    first_head = lax.axis_index("tensor") * local_heads
    weights = mixing_weight.transpose(1, 0, 2)
    if fast:
        numbers = (first_head + jnp.arange(local_heads)).astype(F32)
        slope = jnp.broadcast_to((2.0 ** (-8.0 * (numbers + 1.0) / H))[:, None], (local_heads, 128))
        bias = jnp.stack([mixing_bias[0], jnp.zeros_like(mixing_bias[0]), mixing_bias[1]])
        normed_low, query, keys, vals, attended, logsum, off = head_call(
            inputs, weights, jnp.stack([first_gain, first_shift]), bias, slope, block_ids
        )
    else:
        normed_low = layer_norm(source, first_gain, first_shift).astype(BF16)

        def project(k):
            return jnp.dot(normed_low, weights[k], preferred_element_type=F32)

        query = (project(0) + mixing_bias[0]).astype(BF16).reshape(length, local_heads, HD)
        keys = project(1).astype(BF16).reshape(length, local_heads, HD)
        vals = (project(2) + mixing_bias[1]).astype(BF16).reshape(length, local_heads, HD)
        masked = biased_scores(query, keys, blocks, first_head)
        row_top = jnp.max(masked, axis=-1, keepdims=True)
        logsum = row_top + jnp.log(jnp.sum(jnp.exp(masked - row_top), axis=-1, keepdims=True))
        probs_low = jnp.exp(masked - logsum).astype(BF16)
        attended = (
            jnp.einsum("hqk,khd->qhd", probs_low, vals, preferred_element_type=F32)
            .reshape(length, local_width)
            .astype(BF16)
        )
    if fast:
        most = max(width, units)
        vectors = jnp.stack(
            [
                jnp.pad(one, (0, most - one.shape[0]))
                for one in (output_bias, second_gain, second_shift, expand_bias, first_gain, shrink_bias)
            ]
        )
        total, second_low, activ_low, pre_grad, partial_mlp, second_part, expand_bias_part = mlp_call(
            n_tensor, attended, output_weight, inputs, cotangent, expand_weight, shrink_weight, vectors
        )
    else:
        partial_out = jnp.dot(attended, output_weight, preferred_element_type=F32)
        resid = lax.psum(partial_out.astype(BF16), "tensor").astype(F32)
        hidden_state = source + (resid + output_bias)
        second_low = layer_norm(hidden_state, second_gain, second_shift).astype(BF16)
        pre_act = jnp.dot(second_low, expand_weight, preferred_element_type=F32) + expand_bias
        activ_low = gelu_exact(pre_act).astype(BF16)
        partial_mlp = jnp.dot(activ_low, shrink_weight, preferred_element_type=F32)
        act_grad = jnp.einsum("td,fd->tf", cotangent, shrink_weight, preferred_element_type=F32)
        _, gelu_pull = jax.vjp(gelu_exact, pre_act)
        pre_grad = gelu_pull(act_grad)[0].astype(BF16)
        expand_bias_part = jnp.sum(pre_grad.astype(F32), axis=0)
        second_part = jnp.einsum("tf,df->td", pre_grad, expand_weight, preferred_element_type=F32)
    if fast:
        outputs, shrink_sum, expand_sum, output_sum, mixing_sum, input_grad, small = back_call(
            n_tensor, second_part, partial_mlp, activ_low, cotangent, second_low, pre_grad, inputs, total,
            weights, normed_low, attended, expand_bias_part, vectors[:, :width], output_weight, query, keys, vals,
            logsum, slope, off,
        )
        outputs, input_grad = outputs.reshape(length, width), input_grad.reshape(length, width)
        shrink_weight_grad = shrink_sum.astype(F32).reshape(units, width)
        expand_weight_grad = expand_sum.astype(F32).reshape(width, units)
        mixing_weight_grad = mixing_sum.astype(F32).reshape(3, width, local_width).transpose(1, 0, 2)
        output_weight_grad = output_sum.astype(F32).reshape(local_width, width)
        first_gain_grad, first_shift_grad, second_gain_grad, second_shift_grad = small[0], small[1], small[2], small[3]
        output_bias_grad, expand_bias_grad, shrink_bias_grad = small[4], small[5], small[6]
        mixing_bias_grad = small[7, : 2 * local_width].reshape(2, local_width)
    else:
        shrink_bias_part = jnp.sum(upstream, axis=0)
        shrink_part = jnp.einsum("tf,td->fd", activ_low, cotangent, preferred_element_type=F32)
        expand_part = jnp.einsum("td,tf->df", second_low, pre_grad, preferred_element_type=F32)

        mlp_sum = lax.psum(partial_mlp.astype(BF16), "tensor").astype(F32)
        second_grad = lax.psum(second_part.astype(BF16), "tensor").astype(F32)
        outputs = (hidden_state + mlp_sum + shrink_bias).astype(BF16)
        hidden_grad, second_gain_part, second_shift_part = norm_backward(
            hidden_state, second_gain, second_shift, second_grad
        )
        hidden_grad = hidden_grad + upstream
        resid_low = hidden_grad.astype(BF16)
        output_part = jnp.einsum("tc,td->cd", attended, resid_low, preferred_element_type=F32)
        output_bias_part = jnp.sum(resid_low.astype(F32), axis=0)
        attended_grad = (
            jnp.einsum("td,cd->tc", resid_low, output_weight, preferred_element_type=F32)
            .astype(BF16)
            .reshape(length, local_heads, HD)
        )
        probs = jnp.exp(biased_scores(query, keys, blocks, first_head) - logsum)
        probs_low = probs.astype(BF16)
        prob_grad = jnp.einsum("qhd,khd->hqk", attended_grad, vals, preferred_element_type=F32)
        vals_grad = jnp.einsum(
            "hqk,qhd->khd", probs_low, attended_grad, preferred_element_type=F32
        ).astype(BF16)
        row_delta = jnp.sum(probs * prob_grad, axis=-1, keepdims=True)
        score_grad = (probs * (prob_grad - row_delta)).astype(BF16)
        scale_factor = 1.0 / math.sqrt(HD)
        query_grad = (
            jnp.einsum("hqk,khd->qhd", score_grad, keys, preferred_element_type=F32) * scale_factor
        ).astype(BF16)
        keys_grad = (
            jnp.einsum("hqk,qhd->khd", score_grad, query, preferred_element_type=F32) * scale_factor
        ).astype(BF16)
        grads = [one.reshape(length, local_width) for one in (query_grad, keys_grad, vals_grad)]
        mixing_bias_part = jnp.stack(
            [jnp.sum(grads[0].astype(F32), axis=0), jnp.sum(grads[2].astype(F32), axis=0)]
        )
        mixing_part = jnp.stack(
            [jnp.einsum("td,tc->dc", normed_low, one, preferred_element_type=F32) for one in grads]
        )
        normed_part = sum(
            jnp.einsum("tc,dc->td", one, weights[k], preferred_element_type=F32)
            for k, one in enumerate(grads)
        )
        normed_grad = lax.psum(normed_part.astype(BF16), "tensor").astype(F32)
        source_grad, first_gain_part, first_shift_part = norm_backward(
            source, first_gain, first_shift, normed_grad
        )
        input_grad = (source_grad + hidden_grad).astype(BF16)
        summed = lax.psum(
            (
                first_gain_part, first_shift_part, mixing_part, mixing_bias_part, output_part, output_bias_part,
                second_gain_part, second_shift_part, expand_part, expand_bias_part, shrink_part, shrink_bias_part,
            ),
            "dp",
        )
        first_gain_grad, first_shift_grad, mixing_weight_grad, mixing_bias_grad = summed[:4]
        mixing_weight_grad = mixing_weight_grad.transpose(1, 0, 2)
        output_weight_grad, output_bias_grad, second_gain_grad, second_shift_grad = summed[4:8]
        expand_weight_grad, expand_bias_grad, shrink_weight_grad, shrink_bias_grad = summed[8:]
    return (
        outputs,
        input_grad,
        first_gain_grad,
        first_shift_grad,
        mixing_weight_grad,
        mixing_bias_grad,
        output_weight_grad,
        output_bias_grad,
        second_gain_grad,
        second_shift_grad,
        expand_weight_grad,
        expand_bias_grad,
        shrink_weight_grad,
        shrink_bias_grad,
    )


def solution(mesh):
    in_specs = (
        P("dp", None),
        P("dp", None),
        P(),
        P(),
        P(None, None, "tensor"),
        P(None, "tensor"),
        P("tensor", None),
        P(),
        P(),
        P(),
        P(None, "tensor"),
        P("tensor"),
        P("tensor", None),
        P(),
        P("dp", None),
    )
    out_specs = (
        P("dp", None),
        P("dp", None),
        P(),
        P(),
        P(None, None, "tensor"),
        P(None, "tensor"),
        P("tensor", None),
        P(),
        P(),
        P(),
        P(None, "tensor"),
        P("tensor"),
        P("tensor", None),
        P(),
    )
    n_tensor = mesh.shape["tensor"]
    fast = mesh.shape["dp"] == 8 and n_tensor in (2, 4)
    return jax.shard_map(
        functools.partial(on_device, fast, n_tensor),
        mesh=mesh,
        in_specs=in_specs,
        out_specs=out_specs,
        check_vma=False,
    )
```

```python
import functools
import math

import jax
import jax.numpy as jnp
from jax import lax
from jax.experimental import pallas as pl
from jax.experimental.pallas import tpu as pltpu
from jax.sharding import PartitionSpec as P

H = 32
HD = 64
EPS = 1e-05
F32 = jnp.float32
BF16 = jnp.bfloat16
MESH = pl.DeviceIdType.MESH


def layer_norm(values, scale_gain, shift_bias):
    row_mean = jnp.mean(values, axis=-1, keepdims=True)
    centred = values - row_mean
    row_var = jnp.mean(centred * centred, axis=-1, keepdims=True)
    return centred * lax.rsqrt(row_var + EPS) * scale_gain + shift_bias


def norm_backward(values, scale_gain, shift_bias, upstream):
    _, pull_back = jax.vjp(layer_norm, values, scale_gain, shift_bias)
    return pull_back(upstream)


def gelu_exact(values):
    return jax.nn.gelu(values, approximate=False)


def biased_scores(query, keys, blocks, first_head):
    length, local_heads, head_width = query.shape
    scores = jnp.einsum("qhd,khd->hqk", query, keys, preferred_element_type=F32) * (
        1.0 / math.sqrt(head_width)
    )
    heads_index = (first_head + jnp.arange(local_heads)).astype(F32)
    slopes = 2.0 ** (-8.0 * (heads_index + 1.0) / H)
    places = jnp.arange(length)
    offsets = (places[None, :] - places[:, None]).astype(F32)
    scores = scores + slopes[:, None, None] * offsets[None]
    allowed = blocks[None, :] <= blocks[:, None]
    return jnp.where(allowed[None], scores, -1e30)


def add_rows(dst, src, step):
    rows = dst.shape[0]

    def body(i, carry):
        at = pl.ds(pl.multiple_of(i * step, step), step)
        dst[at, :] = (dst[at, :].astype(F32) + src[at, :].astype(F32)).astype(BF16)
        return carry

    lax.fori_loop(0, rows // step, body, 0)


def remote(src, dst, send, recv, axis, to):
    return pltpu.make_async_remote_copy(
        src_ref=src,
        dst_ref=dst,
        send_sem=send,
        recv_sem=recv,
        device_id={axis: to},
        device_id_type=MESH,
    )


class Chain:
    def __init__(self, n, refs, slack=1):
        self.part, self.outer_in, self.inner_in, self.s_in, self.s_out, self.r_outer, self.r_inner = refs
        i = lax.axis_index("tensor")
        left = i < n // 2
        depth = jnp.where(left, i, n - 1 - i)
        self.inner = jnp.where(left, i + 1, i - 1)
        self.has_outer = depth > 0
        self.outer = jnp.where(self.has_outer, jnp.where(left, i - 1, i + 1), self.inner)
        self.is_mid = depth == n // 2 - 1
        self.first = slack * depth
        self.lag = slack * (n - 1 - depth)
        self.most_lag = slack * (n - 1)

    @staticmethod
    def scratch(count, block):
        dma = pltpu.SemaphoreType.DMA
        return [pltpu.VMEM((count, *block), BF16)] * 3 + [dma((count,))] * 4

    def to_mid(self, k):
        return remote(
            self.part.at[k], self.inner_in.at[k], self.s_in.at[k], self.r_inner.at[k], "tensor", self.inner
        )

    def to_inner(self, k):
        return remote(
            self.part.at[k], self.outer_in.at[k], self.s_in.at[k], self.r_outer.at[k], "tensor", self.inner
        )

    def to_outer(self, k):
        return remote(
            self.inner_in.at[k], self.inner_in.at[k], self.s_out.at[k], self.r_inner.at[k], "tensor", self.outer
        )

    def greet(self, barrier):
        pl.semaphore_signal(barrier, inc=1, device_id={"tensor": self.inner}, device_id_type=MESH)

        @pl.when(self.has_outer)
        def _():
            pl.semaphore_signal(barrier, inc=1, device_id={"tensor": self.outer}, device_id_type=MESH)

    def wait_greetings(self, barrier, others):
        @pl.when(self.has_outer)
        def _():
            pl.semaphore_wait(barrier, others + 2)

        @pl.when(jnp.logical_not(self.has_outer))
        def _():
            pl.semaphore_wait(barrier, others + 1)

    def reduce(self, k):
        @pl.when(self.has_outer)
        def _():
            self.to_inner(k).wait_recv()
            add_rows(self.part.at[k], self.outer_in.at[k], 16)

        @pl.when(self.is_mid)
        def _():
            self.to_mid(k).start()

        @pl.when(jnp.logical_not(self.is_mid))
        def _():
            self.to_inner(k).start()

    def spread(self, k):
        self.to_mid(k).wait_recv()

        @pl.when(self.is_mid)
        def _():
            add_rows(self.inner_in.at[k], self.part.at[k], 16)

        @pl.when(self.has_outer)
        def _():
            self.to_outer(k).start()

    def drain(self, k):
        self.to_mid(k).wait_send()

        @pl.when(self.has_outer)
        def _():
            self.to_outer(k).wait_send()


def between(k, count):
    return jnp.logical_and(k >= 0, k < count)


def pair_forward(pair, q, k, v, slope, off, tile, attended, lse):
    length = q.shape[0]
    lanes = pl.ds(pl.multiple_of(pair * 2 * HD, 2 * HD), 2 * HD)
    masks = [lane_half(odd).astype(BF16) for odd in range(2)]
    gains = [slope[pl.ds(2 * pair + odd, 1), 0:1] for odd in range(2)]
    for j in range(length // tile):
        rows = slice(j * tile, (j + 1) * tile)
        most = min(length, (j + 2) * tile)
        here = q[rows, lanes]
        scores = [
            lax.dot_general(
                k[0:most, lanes], here * masks[odd], (((1,), (1,)), ((), ())), preferred_element_type=F32
            )
            for odd in range(2)
        ]
        got = []
        for odd in range(2):
            raised = scores[odd] * (1.0 / math.sqrt(HD)) + gains[odd] * off[0:most, rows]
            top = jnp.max(raised, axis=0, keepdims=True)
            raised = jnp.exp(raised - top)
            total = jnp.sum(raised, axis=0, keepdims=True)
            lse[pl.ds(2 * pair + odd, 1), rows] = top + jnp.log(total)
            probs = (raised * (1.0 / total)).astype(BF16)
            got.append(
                lax.dot_general(
                    v[0:most, lanes], probs, (((0,), (0,)), ((), ())), preferred_element_type=F32
                )
            )
        both = jnp.concatenate([got[0][:HD], got[1][HD:]], axis=0)
        attended[rows, lanes] = both.T.astype(BF16)


def head_kernel(heads, *refs):
    (src_h, w_h, vec_h, bias_h, slope_h, blocks_h), refs = refs[:6], refs[6:]
    (normed_h, q_h, k_h, v_h, att_h, lse_h, off_h), refs = refs[:7], refs[7:]
    (src, w, vec, bias, slope, blocks), refs = refs[:6], refs[6:]
    (normed, q, k, v, att, lse, off), refs = refs[:7], refs[7:]
    load, w_load, store = refs
    length, width = src.shape
    loads = [
        pltpu.make_async_copy(a, b, load.at[j])
        for j, (a, b) in enumerate(
            ((src_h, src), (vec_h, vec), (blocks_h, blocks), (bias_h, bias), (slope_h, slope))
        )
    ]
    w_loads = [pltpu.make_async_copy(w_h.at[m], w.at[m], w_load.at[m]) for m in range(3)]
    for one in loads + w_loads:
        one.start()
    for one in loads:
        one.wait()
    step, groups = 16, 4

    def normalize(i, carry):
        ats = [pl.ds(pl.multiple_of((i * groups + g) * step, step), step) for g in range(groups)]
        values = [src[at, :].astype(F32) for at in ats]
        centred = [one - jnp.sum(one, axis=-1, keepdims=True) / width for one in values]
        spread = [lax.rsqrt(jnp.sum(one * one, axis=-1, keepdims=True) / width + EPS) for one in centred]
        for at, one, by in zip(ats, centred, spread):
            normed[at, :] = (one * by * vec[0:1, :] + vec[1:2, :]).astype(BF16)
        return carry

    lax.fori_loop(0, length // (step * groups), normalize, 0)

    here = blocks[...].astype(F32)
    there = jnp.broadcast_to(here, (8, length)).T[:, 0:1]
    for j in range(length // 256):
        cols = slice(j * 256, (j + 1) * 256)
        distance = (
            lax.broadcasted_iota(jnp.int32, (length, 256), 0)
            - lax.broadcasted_iota(jnp.int32, (length, 256), 1)
            - j * 256
        ).astype(F32)
        off[:, cols] = jnp.where(there <= here[:, cols], distance, -1e30)

    for m, to in enumerate((q, k, v)):
        w_loads[m].wait()

        to[...] = (
            jnp.dot(normed[...], w[m], preferred_element_type=F32) + bias[m : m + 1, :]
        ).astype(BF16)

    stores = [
        pltpu.make_async_copy(a, b, store.at[j])
        for j, (a, b) in enumerate(
            ((normed, normed_h), (off, off_h), (q, q_h), (k, k_h), (v, v_h), (att, att_h), (lse, lse_h))
        )
    ]
    for one in stores[:5]:
        one.start()

    def attend(pair, carry):
        pair_forward(pair, q, k, v, slope, off, HEAD_TILE, att, lse)
        return carry

    lax.fori_loop(0, heads // 2, attend, 0)
    for one in stores[5:]:
        one.start()
    for one in stores:
        one.wait()


def head_call(src, w, vec, bias, slope, blocks):
    length, width = src.shape
    local = w.shape[2]
    heads = local // HD
    inputs = (src, w, vec, bias, slope, blocks)
    shapes = [
        ((length, width), BF16),
        *[((length, local), BF16)] * 4,
        ((heads, length), F32),
        ((length, length), F32),
    ]
    dma = pltpu.SemaphoreType.DMA
    return pl.pallas_call(
        functools.partial(head_kernel, heads),
        out_shape=[jax.ShapeDtypeStruct(*one) for one in shapes],
        in_specs=[pl.BlockSpec(memory_space=pl.ANY)] * len(inputs),
        out_specs=[pl.BlockSpec(memory_space=pl.ANY)] * len(shapes),
        scratch_shapes=[
            *[pltpu.VMEM(one.shape, one.dtype) for one in inputs],
            *[pltpu.VMEM(*one) for one in shapes],
            dma((5,)),
            dma((3,)),
            dma((7,)),
        ],
        compiler_params=pltpu.CompilerParams(vmem_limit_bytes=60 << 20),
    )(*inputs)


ROWS = 32
SLACK = 2
BLOCK_ROWS = 256
TILE = 1024


def mlp_kernel(n, length, *refs):
    (att_h, wo_h, src_h, dy_h, wu_h, wd_h, vec_h), refs = refs[:7], refs[7:]
    (tot_h, second_h, activ_h, pre_h, mlp_h, grad_h, bias_h), refs = refs[:7], refs[7:]
    (att, wo, src, dy, wu, wd, vec, second, activ, pre, mlp, grad, bias), refs = refs[:13], refs[13:]
    load, store, tot_store, *refs = refs
    chain = Chain(n, refs, SLACK)
    width = wo.shape[1]
    units = wu.shape[1]
    chunks = length // ROWS
    blocks = length // BLOCK_ROWS
    per_block = BLOCK_ROWS // ROWS
    group = 4

    loads = [
        pltpu.make_async_copy(a, b, load.at[k])
        for k, (a, b) in enumerate(
            ((att_h, att), (wo_h, wo), (vec_h, vec), (src_h, src), (wu_h, wu), (dy_h, dy), (wd_h, wd))
        )
    ]
    for one in loads:
        one.start()
    barrier = pltpu.get_barrier_semaphore()
    chain.greet(barrier)
    bias[...] = jnp.zeros_like(bias)
    chain.wait_greetings(barrier, 0)
    for one in loads[:3]:
        one.wait()

    def tot_copy(k):
        return pltpu.make_async_copy(chain.inner_in.at[k], tot_h.at[k], tot_store.at[k])

    def block_copies(b):
        at = pl.ds(pl.multiple_of(b * BLOCK_ROWS, BLOCK_ROWS), BLOCK_ROWS)
        pairs = ((second, second_h), (activ, activ_h), (pre, pre_h), (mlp, mlp_h), (grad, grad_h))
        return [
            pltpu.make_async_copy(a.at[at], h.at[at], store.at[b, j]) for j, (a, h) in enumerate(pairs)
        ]

    def produce(g):
        rows = group * ROWS
        left = att[pl.ds(pl.multiple_of(g * rows, rows), rows), :]
        for j in range(width // 512):
            cols = pl.ds(j * 512, 512)
            got = jnp.dot(left, wo[:, cols], preferred_element_type=F32).astype(BF16)
            for q in range(group):
                chain.part[g * group + q, :, cols] = got[q * ROWS : (q + 1) * ROWS]

    def normalize(b):
        step, groups = 16, 4

        def body(i, carry):
            ats, values = [], []
            for g in range(groups):
                r = i * groups + g
                at = pl.ds(pl.multiple_of(b * BLOCK_ROWS + r * step, step), step)
                k = b * per_block + r // (ROWS // step)
                inside = pl.ds(pl.multiple_of((r % (ROWS // step)) * step, step), step)
                ats.append(at)
                values.append(
                    src[at, :].astype(F32) + (chain.inner_in[k, inside, :].astype(F32) + vec[0:1, :width])
                )
            centred = [one - jnp.mean(one, axis=-1, keepdims=True) for one in values]
            spread = [lax.rsqrt(jnp.mean(one * one, axis=-1, keepdims=True) + EPS) for one in centred]
            for at, one, by in zip(ats, centred, spread):
                second[at, :] = (one * by * vec[1:2, :width] + vec[2:3, :width]).astype(BF16)
            return carry

        lax.fori_loop(0, BLOCK_ROWS // (step * groups), body, 0)

    def hidden_tile(b, j):
        at = pl.ds(pl.multiple_of(b * BLOCK_ROWS, BLOCK_ROWS), BLOCK_ROWS)
        cols = pl.ds(pl.multiple_of(j * TILE, TILE), TILE)
        value = jnp.dot(second[at, :], wu[:, cols], preferred_element_type=F32) + vec[3:4, cols]
        back = lax.dot_general(
            dy[at, :], wd[cols, :], (((1,), (1,)), ((), ())), preferred_element_type=F32
        )
        below = 0.5 + 0.5 * lax.erf(value * math.sqrt(0.5))
        density = jnp.exp(-0.5 * value * value) * (1.0 / math.sqrt(2.0 * math.pi))
        activ[at, cols] = (value * below).astype(BF16)
        low = (back * (below + value * density)).astype(BF16)
        pre[at, cols] = low
        bias[:, cols] += jnp.sum(low.astype(F32).reshape(BLOCK_ROWS // 8, 8, TILE), axis=0)

    def out_tile(b, j):
        at = pl.ds(pl.multiple_of(b * BLOCK_ROWS, BLOCK_ROWS), BLOCK_ROWS)
        cols = pl.ds(pl.multiple_of(j * TILE, TILE), TILE)
        mlp[at, cols] = jnp.dot(activ[at, :], wd[:, cols], preferred_element_type=F32).astype(BF16)
        grad[at, cols] = lax.dot_general(
            pre[at, :], wu[cols, :], (((1,), (1,)), ((), ())), preferred_element_type=F32
        ).astype(BF16)

    ahead = units // TILE
    steps = ahead + width // TILE
    per_tick = -(-steps // per_block)
    first_tick = per_block + chain.most_lag

    def tick(t, carry):
        @pl.when(jnp.logical_and(t % group == 0, t < chunks))
        def _():
            produce(t // group)

        ready = t - chain.first

        @pl.when(between(ready, chunks))
        def _():
            chain.reduce(ready)

        back = t - chain.lag

        @pl.when(between(back, chunks))
        def _():
            chain.spread(back)
            tot_copy(back).start()

        late = t - first_tick

        @pl.when(late == 0)
        def _():
            for one in loads[3:]:
                one.wait()

        @pl.when(between(late, blocks * per_block))
        def _():
            b = late // per_block
            for q in range(per_tick):
                s = (late % per_block) * per_tick + q

                @pl.when(s == 0)
                def _():
                    normalize(b)

                @pl.when(s < ahead)
                def _():
                    hidden_tile(b, s)

                @pl.when(between(s - ahead, width // TILE))
                def _():
                    out_tile(b, s - ahead)

                @pl.when(s == steps - 1)
                def _():
                    for one in block_copies(b):
                        one.start()

        return carry

    lax.fori_loop(0, chunks + first_tick, tick, 0)
    bias_copy = pltpu.make_async_copy(bias, bias_h, load.at[0])
    bias_copy.start()

    def drain(k, carry):
        chain.drain(k)
        tot_copy(k).wait()
        return carry

    lax.fori_loop(0, chunks, drain, 0)
    for b in range(blocks):
        for one in block_copies(b):
            one.wait()
    bias_copy.wait()


def mlp_call(n, att, wo, src, dy, wu, wd, vec):
    length, width = src.shape
    units = wu.shape[1]
    chunks = length // ROWS
    dma = pltpu.SemaphoreType.DMA
    inputs = (att, wo, src, dy, wu, wd, vec)
    outs = [(chunks, ROWS, width), (length, width), (length, units), (length, units)]
    outs += [(length, width), (length, width)]
    out_shape = [jax.ShapeDtypeStruct(one, BF16) for one in outs] + [jax.ShapeDtypeStruct((8, units), F32)]
    scratch = [pltpu.VMEM(one.shape, one.dtype) for one in inputs]
    scratch += [pltpu.VMEM(one.shape, one.dtype) for one in out_shape[1:]]
    scratch += [dma((7,)), dma((length // BLOCK_ROWS, 5)), dma((chunks,))]
    scratch += Chain.scratch(chunks, (ROWS, width))
    return pl.pallas_call(
        functools.partial(mlp_kernel, n, length),
        out_shape=out_shape,
        in_specs=[pl.BlockSpec(memory_space=pl.ANY)] * len(inputs),
        out_specs=[pl.BlockSpec(memory_space=pl.ANY)] * len(out_shape),
        scratch_shapes=scratch,
        compiler_params=pltpu.CompilerParams(
            collective_id=0, has_side_effects=True, vmem_limit_bytes=60 << 20
        ),
    )(*inputs)


class Ring:
    def __init__(self, n, refs, slots, slack):
        self.chain = Chain(n, refs, slack)
        self.slots = slots
        self.gone = self.chain.most_lag + 2

    def at(self, k):
        return lax.rem(k, self.slots)

    def reduce(self, k):
        self.chain.reduce(self.at(k))

    def spread(self, k):
        self.chain.spread(self.at(k))

    def retire(self, k):
        self.chain.drain(self.at(k))


class Cube:
    def __init__(self, refs, keep, step, apart=1):
        (self.fin, self.give, self.c0, self.r1, self.r2), refs = refs[:5], refs[5:]
        self.s0, self.q0, self.s1, self.q1, self.s2, self.q2, self.s3, self.q3, self.s4, self.q4, self.kept = refs
        self.keep_of, self.step, self.apart = keep, step, apart
        self.gone = 6 * apart
        self.slots = self.gone + 1
        d = lax.axis_index("dp")
        self.c, self.x, self.y = d % 2, (d // 2) % 2, d // 4
        self.to_c, self.to_x, self.to_y = d + 1 - 2 * self.c, d + 2 - 4 * self.x, d + 4 - 8 * self.y
        self.stages = (self.stage1, self.stage2, self.stage3, self.stage4, self.stage5, self.retire)

    @classmethod
    def scratch(cls, block, apart=1):
        dma, n = pltpu.SemaphoreType.DMA, 6 * apart + 1
        return [
            pltpu.VMEM((n, 2, 2, 2, *block), BF16),
            pltpu.VMEM((n, 2, 2, *block), BF16),
            pltpu.VMEM((n, 2, 2, *block), BF16),
            pltpu.VMEM((n, 2, *block), BF16),
            pltpu.VMEM((n, 2, *block), BF16),
            *[dma((n,))] * 2,
            *[dma((n, 2))] * 6,
            *[dma((n,))] * 3,
        ]

    def peer(self, m):
        moves = (1 - 2 * self.c, 2 - 4 * self.x, 4 - 8 * self.y)
        return lax.axis_index("dp") + sum(move for bit, move in enumerate(moves) if m >> bit & 1)

    def slot(self, k):
        return lax.rem(k, self.slots)

    def half(self, k):
        p = self.slot(k)
        return remote(self.give.at[p], self.c0.at[p], self.s0.at[p], self.q0.at[p], "dp", self.to_c)

    def quarters(self, p):
        return self.fin.at[p, self.c, 0, self.x], self.fin.at[p, self.c, 1, self.y]

    def hop1(self, k):
        p, fin, c = self.slot(k), self.fin, self.c
        return (
            remote(fin.at[p, c, 0, 1 - self.x], self.r1.at[p, 0], self.s1.at[p, 0], self.q1.at[p, 0], "dp", self.to_x),
            remote(fin.at[p, c, 1, 1 - self.y], self.r1.at[p, 1], self.s1.at[p, 1], self.q1.at[p, 1], "dp", self.to_y),
        )

    def hop2(self, k):
        p = self.slot(k)
        a, b = self.quarters(p)
        return (
            remote(a, self.r2.at[p, 0], self.s2.at[p, 0], self.q2.at[p, 0], "dp", self.to_y),
            remote(b, self.r2.at[p, 1], self.s2.at[p, 1], self.q2.at[p, 1], "dp", self.to_x),
        )

    def hop3(self, k):
        p = self.slot(k)
        a, b = self.quarters(p)
        return (
            remote(a, a, self.s3.at[p, 0], self.q3.at[p, 0], "dp", self.to_x),
            remote(b, b, self.s3.at[p, 1], self.q3.at[p, 1], "dp", self.to_y),
        )

    def hop4(self, k):
        p = self.slot(k)
        mine = self.fin.at[p, self.c]
        return remote(mine, mine, self.s4.at[p], self.q4.at[p], "dp", self.to_c)

    def kept_wait(self, k):
        p = self.slot(k)
        pltpu.make_async_copy(self.fin.at[p], self.fin.at[p], self.kept.at[p]).wait()

    def add_quarters(self, k, got):
        p = self.slot(k)
        for j, quarter in enumerate(self.quarters(p)):
            add_rows(quarter, got.at[p, j], self.step)

    def stage1(self, k):
        self.half(k).wait()
        p = self.slot(k)
        for a in range(2):
            for b in range(2):
                add_rows(self.fin.at[p, self.c, a, b], self.c0.at[p, a, b], self.step)
        for one in self.hop1(k):
            one.start()

    def stage2(self, k):
        for one in self.hop1(k):
            one.wait()
        self.add_quarters(k, self.r1)
        for one in self.hop2(k):
            one.start()

    def stage3(self, k):
        for one in self.hop2(k):
            one.wait()
        self.add_quarters(k, self.r2)
        for one in self.hop3(k):
            one.start()

    def stage4(self, k):
        for one in self.hop3(k):
            one.wait_recv()
        self.hop4(k).start()

    def stage5(self, k):
        self.hop4(k).wait_recv()
        p = self.slot(k)
        self.keep_of(k, self.fin.at[p], self.kept.at[p])

    def retire(self, k):
        for one in self.hop3(k) + (self.hop4(k),):
            one.wait_send()
        self.kept_wait(k)

    def tick(self, t, count):
        for late, stage in reversed(tuple(enumerate(self.stages, 1))):
            k = t - late * self.apart

            @pl.when(between(k, count))
            def _(stage=stage, k=k):
                stage(k)


def weighted(left, right):
    return lax.dot_general(left, right, (((0,), (0,)), ((), ())), preferred_element_type=F32).astype(BF16)


def lane_half(odd):
    return (lax.broadcasted_iota(jnp.int32, (1, 2 * HD), 1) // HD == odd).astype(F32)


def head_backward(head, q, k, v, up, lse, slope, off, tile, grads, acc):
    q_grad, k_grad, v_grad = grads
    k_acc, v_acc = acc
    length = q.shape[0]
    odd = lax.rem(head, 2)
    mask = lane_half(odd).astype(BF16)
    lanes = pl.ds(pl.multiple_of((head // 2) * 2 * HD, 2 * HD), 2 * HD)
    scale = 1.0 / math.sqrt(HD)
    gain = slope[pl.ds(head, 1), 0:1]
    nt = (((1,), (1,)), ((), ()))
    for j in range(length // tile):
        rows = slice(j * tile, (j + 1) * tile)
        most = min(length, (j + 2) * tile)
        q_here = q[rows, lanes]
        up_here = up[rows, lanes] * mask
        k_here = k[0:most, lanes] * mask
        scores = lax.dot_general(k_here, q_here, nt, preferred_element_type=F32)
        probs = jnp.exp(scores * scale + gain * off[0:most, rows] - lse[pl.ds(head, 1), rows])
        back = lax.dot_general(v[0:most, lanes], up_here, nt, preferred_element_type=F32)
        delta = jnp.sum(probs * back, axis=0, keepdims=True)
        score_grad = (probs * (back - delta)).astype(BF16)
        v_part = jnp.dot(probs.astype(BF16), up_here, preferred_element_type=F32)
        k_part = jnp.dot(score_grad, q_here * mask, preferred_element_type=F32)
        if j == 0:
            v_acc[0:most, :] = v_part
            k_acc[0:most, :] = k_part
            if most < length:
                v_acc[most:length, :] = jnp.zeros((length - most, 2 * HD), F32)
                k_acc[most:length, :] = jnp.zeros((length - most, 2 * HD), F32)
        else:
            v_acc[0:most, :] += v_part
            k_acc[0:most, :] += k_part
        q_part = lax.dot_general(k_here, score_grad, (((0,), (0,)), ((), ())), preferred_element_type=F32)
        mine = (q_part.T * scale).astype(BF16)

        @pl.when(odd == 0)
        def _(rows=rows, mine=mine):
            q_grad[rows, lanes] = mine

        @pl.when(odd == 1)
        def _(rows=rows, mine=mine):
            q_grad[rows, lanes] += mine

    for to, got, factor in ((k_grad, k_acc, scale), (v_grad, v_acc, 1.0)):

        @pl.when(odd == 0)
        def _(to=to, got=got, factor=factor):
            to[:, lanes] = (got[...] * factor).astype(BF16)

        @pl.when(odd == 1)
        def _(to=to, got=got, factor=factor):
            to[:, lanes] += (got[...] * factor).astype(BF16)


ROWS_BACK = 48
BACK_SLOTS = 12
BACK_SLACK = 2
BACK_APART = 2
BACK_COLUMNS = 1024
HEAD_TILE = 256
PIECE = 256
GROUP = 4


def back_kernel(n, heads, *refs):
    (grad_h, mlp_h, activ_h, dy_h, second_h, pre_h, src_h, tot_h, w_h, normed_h, att_h, eb_h), refs = refs[:12], refs[12:]
    smalls_h, refs = refs[:8], refs[8:]
    (out_h, shrink_out, expand_out, wo_out, mix_out, input_h, small_out), refs = refs[:7], refs[7:]
    (left, dy, pre, src, tot, out, resid, w, att, eb), refs = refs[:10], refs[10:]
    smalls, refs = refs[:8], refs[8:]
    vec, wo, q, k, v, lse, slope, off = smalls
    (up, grads, k_acc, v_acc, cols, buf, got_small, last), refs = refs[:8], refs[8:]
    (load, left_sem, part_sem, row_sem, out_sem, ss, sq, ls, lq), refs = refs[:9], refs[9:]
    ring, refs = Ring(n, refs[:7], BACK_SLOTS, BACK_SLACK), refs[7:]
    chain = ring.chain
    width, local = dy.shape[1], q.shape[1]
    rows, per_sum = ROWS_BACK, grad_h.shape[0]
    loaded_z, total_z = 2 * per_sum, 3 * per_sum
    per_row = width // BACK_COLUMNS
    first = activ_h.shape[1] // PIECE
    total_left = first + second_h.shape[1] // PIECE
    to_output = total_left * per_row
    to_mixing = to_output + local // PIECE * per_row
    pair = BACK_COLUMNS // local
    per_matrix = width // PIECE // pair
    total_p = to_mixing + 3 * per_matrix

    def keep(p, piece_ref, sem):
        here = pl.ds(pl.multiple_of(lax.rem(p, per_row) * BACK_COLUMNS, BACK_COLUMNS), BACK_COLUMNS)
        for lo, hi, to in (
            (0, first * per_row, shrink_out),
            (first * per_row, to_output, expand_out),
            (to_output, to_mixing, wo_out),
        ):

            @pl.when(jnp.logical_and(p >= lo, p < hi))
            def _(lo=lo, to=to):
                pltpu.make_async_copy(piece_ref, to.at[(p - lo) // per_row, :, :, :, :, here], sem).start()

        @pl.when(p >= to_mixing)
        def _():
            i = p - to_mixing
            for j in range(pair):
                pltpu.make_async_copy(
                    piece_ref.at[:, :, :, :, pl.ds(j * local, local)],
                    mix_out.at[i // per_matrix, lax.rem(i, per_matrix) * pair + j],
                    sem,
                ).start()

    cube = Cube(refs, keep, PIECE // 8, BACK_APART)

    loads = [pltpu.make_async_copy(a, b, load.at[j]) for j, (a, b) in enumerate(zip(smalls_h, smalls))]
    pairs = ((dy_h, dy), (pre_h, pre), (w_h, w), (att_h, att), (eb_h, eb), (normed_h, dy))
    loads += [pltpu.make_async_copy(a, b, load.at[8 + j]) for j, (a, b) in enumerate(pairs)]

    def part_load(j, which):
        return pltpu.make_async_copy(
            (grad_h, mlp_h)[which].at[lax.rem(j, per_sum)], chain.part.at[ring.at(j)], part_sem.at[ring.at(j)]
        )

    def part_start(j):
        @pl.when(j < per_sum)
        def _():
            part_load(j, 0).start()

        @pl.when(between(j - per_sum, per_sum))
        def _():
            part_load(j, 1).start()

    def left_load(r, which):
        at = (r - which * first) * PIECE
        return pltpu.make_async_copy(
            (activ_h, second_h)[which].at[:, pl.ds(pl.multiple_of(at, PIECE), PIECE)],
            left.at[lax.rem(r, 2)],
            left_sem.at[lax.rem(r, 2)],
        )

    def left_start(r):
        @pl.when(r < first)
        def _():
            left_load(r, 0).start()

        @pl.when(between(r - first, total_left - first))
        def _():
            left_load(r, 1).start()

    def row_loads(j):
        at, chunk = lax.rem(j, 2), lax.rem(j, per_sum)
        return (
            pltpu.make_async_copy(src_h.at[chunk], src.at[at], row_sem.at[at, 0]),
            pltpu.make_async_copy(tot_h.at[chunk], tot.at[at], row_sem.at[at, 1]),
        )

    def out_store(j, to):
        at = lax.rem(j, 2)
        return pltpu.make_async_copy(out.at[at], to.at[lax.rem(j, per_sum)], out_sem.at[at])

    part_start(0)
    left_start(0)
    loads[8].start()
    part_start(1)
    for one in loads[:8] + [loads[9]]:
        one.start()
    barrier = pltpu.get_barrier_semaphore()
    chain.greet(barrier)
    for m in range(1, 8):
        pl.semaphore_signal(barrier, inc=1, device_id={"dp": cube.peer(m)}, device_id_type=MESH)
    cols[...] = jnp.zeros_like(cols)
    buf[...] = jnp.zeros_like(buf)
    chain.wait_greetings(barrier, 7)
    loads[8].wait()

    def product(p, columns, right):
        to = cube.slot(p)
        count = PIECE // 8
        for side, store in ((1 - cube.c, cube.give.at[to]), (cube.c, cube.fin.at[to, cube.c])):
            for j in range(BACK_COLUMNS // 512):
                got = weighted(columns(j, side), right(j))
                for a in range(2):
                    for b in range(2):
                        lo = (2 * a + b) * count
                        store[a, b, :, j * 512 : (j + 1) * 512] = got[lo : lo + count]

    half = PIECE // 2

    def produce(p):
        r, part = p // per_row, lax.rem(p, per_row)

        @pl.when(r < total_left)
        def _():
            at = lax.rem(r, 2)

            @pl.when(part == 0)
            def _():
                left_start(r + 1)
                pltpu.make_async_copy(activ_h.at[:, pl.ds(0, PIECE)], left.at[at], left_sem.at[at]).wait()

            def columns(j, side):
                return left[at, :, pl.ds(pl.multiple_of(side * half, half), half)]

            for which, ref in enumerate((dy, pre)):

                def right(j, ref=ref):
                    return ref[:, pl.ds(pl.multiple_of(part * BACK_COLUMNS + j * 512, 512), 512)]

                @pl.when((r >= first) == bool(which))
                def _(right=right):
                    product(p, columns, right)

        @pl.when(between(p - to_output, to_mixing - to_output))
        def _():
            tile = r - total_left

            def columns(j, side):
                return att[:, pl.ds(pl.multiple_of(tile * PIECE + side * half, half), half)]

            def right(j):
                return resid[:, pl.ds(pl.multiple_of(part * BACK_COLUMNS + j * 512, 512), 512)]

            product(p, columns, right)

        @pl.when(p >= to_mixing)
        def _():
            i = p - to_mixing
            tile = lax.rem(i, per_matrix) * pair

            def columns(j, side):
                return dy[:, pl.ds(pl.multiple_of((tile + j) * PIECE + side * half, half), half)]

            def right(j):
                return grads[i // per_matrix]

            product(p, columns, right)

        cube.half(p).start()

    def produce_rows(g):
        at = pl.ds(pl.multiple_of(g * GROUP * rows, GROUP * rows), GROUP * rows)
        for j in range(width // 512):
            here = pl.ds(j * 512, 512)
            total = sum(
                lax.dot_general(
                    grads[m, at, :], w[m, here, :], (((1,), (1,)), ((), ())), preferred_element_type=F32
                )
                for m in range(3)
            ).astype(BF16)
            for i in range(GROUP):
                chain.part[ring.at(loaded_z + g * GROUP + i), :, here] = total[i * rows : (i + 1) * rows]

    def row_sum(x):
        return jnp.sum(x, axis=-1, keepdims=True)

    def norm_back(values, downs, gain):
        centred = [one - row_sum(one) / width for one in values]
        spread = [lax.rsqrt(row_sum(one * one) / width + EPS) for one in centred]
        normal = [one * by for one, by in zip(centred, spread)]
        scaled = [one * gain for one in downs]
        flat = [row_sum(one) / width for one in scaled]
        slope_of = [row_sum(one * other) / width for one, other in zip(scaled, normal)]
        back = [
            by * (one - low - other * high)
            for by, one, low, other, high in zip(spread, scaled, flat, normal, slope_of)
        ]
        return normal, back

    def each_rows(j, what):
        step = 16
        start = lax.rem(j, per_sum) * rows
        what(
            [slice(i * step, (i + 1) * step) for i in range(rows // step)],
            [pl.ds(pl.multiple_of(start + i * step, step), step) for i in range(rows // step)],
        )

    def gather(start, *items):
        for c, item in enumerate(items):
            cols[start + c] += item[0:8] + item[8:16]

    def hidden_rows(at, here):
        return src[at, here, :].astype(F32) + (tot[at, here, :].astype(F32) + vec[0:1, :])

    def rows_back(j):
        at, slot = lax.rem(j, 2), ring.at(j)

        def what(heres, theres):
            downs = [chain.inner_in[slot, here, :].astype(F32) for here in heres]
            normals, backs = norm_back([hidden_rows(at, here) for here in heres], downs, vec[1:2, :])
            for there, down, normal, back in zip(theres, downs, normals, backs):
                given = dy[there, :].astype(F32)
                low = (back + given).astype(BF16)
                resid[there, :] = low
                gather(0, down * normal, down, low.astype(F32))
                gather(5, given)

        each_rows(j, what)
        there = pl.ds(pl.multiple_of(j * rows, rows), rows)
        up[there, :] = lax.dot_general(
            resid[there, :], wo[...], (((1,), (1,)), ((), ())), preferred_element_type=F32
        ).astype(BF16)

    def rows_out(j):
        at, slot = lax.rem(j, 2), ring.at(j)

        def what(heres, theres):
            for here in heres:
                out[at, here, :] = (
                    hidden_rows(at, here) + chain.inner_in[slot, here, :].astype(F32) + vec[5:6, :]
                ).astype(BF16)

        each_rows(j, what)
        out_store(j, out_h).start()

    def rows_front(j):
        at, slot = lax.rem(j, 2), ring.at(j)

        def what(heres, theres):
            downs = [chain.inner_in[slot, here, :].astype(F32) for here in heres]
            normals, backs = norm_back([src[at, here, :].astype(F32) for here in heres], downs, vec[4:5, :])
            for here, there, down, normal, back in zip(heres, theres, downs, normals, backs):
                out[at, here, :] = (back + resid[there, :].astype(F32)).astype(BF16)
                gather(3, down * normal, down)

        each_rows(j, what)
        out_store(j, input_h).start()

    def swap(j):
        to = (cube.to_c, cube.to_x, cube.to_y)[j]
        return remote(buf.at[j], got_small.at[j], ss.at[j], sq.at[j], "dp", to)

    def small_step(j):
        if j == 0:
            for row, item in ((2, cols[0]), (3, cols[1]), (4, cols[2]), (5, eb[...]), (6, cols[5])):
                buf[0, row : row + 1, :] = jnp.sum(item, axis=0, keepdims=True)
        else:
            swap(j - 1).wait()
            buf[j] = buf[j - 1] + got_small[j - 1]
        if j < 3:
            swap(j).start()

    def last_copy(m):
        return remote(last.at[0], last.at[m], ls.at[m], lq.at[m], "dp", cube.peer(m))

    def last_start():
        for row in range(2):
            last[0, row : row + 1, :] = jnp.sum(cols[3 + row], axis=0, keepdims=True)
        for m in range(1, 8):
            last_copy(m).start()

    def last_end():
        for m in range(1, 8):
            last_copy(m).wait()
        two = [last[m] + last[m + 1] for m in range(0, 8, 2)]
        buf[3, 0:2, :] = (two[0] + two[1]) + (two[2] + two[3])

    late = chain.most_lag + 1
    heads_at = late + per_sum

    def tick(t, carry):
        gone = t - ring.gone

        @pl.when(between(gone, total_z))
        def _():
            ring.retire(gone)

        part_start(t + 2)

        @pl.when(jnp.logical_and(between(t - loaded_z, per_sum), lax.rem(t - loaded_z, GROUP) == 0))
        def _():
            produce_rows((t - loaded_z) // GROUP)

        ready = t - chain.first

        @pl.when(between(ready, total_z))
        def _():
            @pl.when(ready < loaded_z)
            def _():
                part_load(ready, 0).wait()

            ring.reduce(ready)

        back = t - chain.lag

        @pl.when(between(back, total_z))
        def _():
            ring.spread(back)

        cube.tick(t, total_p)

        @pl.when(t == 2)
        def _():
            for one in loads[:8] + [loads[9]]:
                one.wait()
            for one in loads[10:13]:
                one.start()

        @pl.when(t == heads_at)
        def _():
            for one in loads[10:13]:
                one.wait()
            loads[13].start()

        @pl.when(t == to_mixing)
        def _():
            loads[13].wait()

        @pl.when(t < total_p)
        def _():
            produce(t)

        chunk = t - late

        @pl.when(between(chunk + 1, total_z))
        def _():
            for one in row_loads(chunk + 1):
                one.start()

        @pl.when(between(chunk - 2 - per_sum, total_z - per_sum))
        def _():
            out_store(chunk - 2, out_h).wait()

        @pl.when(between(chunk, total_z))
        def _():
            for one in row_loads(chunk):
                one.wait()

            for which, what in enumerate((rows_back, rows_out, rows_front)):

                @pl.when(between(chunk - which * per_sum, per_sum))
                def _(what=what):
                    what(chunk)

        head = t - heads_at

        @pl.when(between(head, heads))
        def _():
            head_backward(
                head, q, k, v, up, lse, slope, off, HEAD_TILE, (grads.at[0], grads.at[1], grads.at[2]), (k_acc, v_acc)
            )

        @pl.when(head == heads)
        def _():
            for j, m in enumerate((0, 2)):
                buf[0, 7:8, j * local : (j + 1) * local] = jnp.sum(
                    grads[m].astype(F32), axis=0, keepdims=True
                )

        for j in range(4):

            @pl.when(t == loaded_z + 2 + 2 * j)
            def _(j=j):
                small_step(j)

        for j, step in enumerate((last_start, last_end)):

            @pl.when(t == late + total_z + j)
            def _(step=step):
                step()

        return carry

    assert heads_at + heads <= loaded_z and heads_at + 1 < to_output
    lax.fori_loop(0, max(total_z + late + 2, total_p + cube.gone), tick, 0)
    small_store = pltpu.make_async_copy(buf.at[3], small_out, load.at[0])
    small_store.start()
    small_store.wait()


def back_call(n, grad, mlp, activ, dy, second, pre, src, tot, w, normed, att, eb, vec, wo, q, k, v, lse, slope, off):
    length, width = dy.shape
    local = q.shape[1]
    chunks = length // ROWS_BACK
    dma = pltpu.SemaphoreType.DMA

    def cut(one):
        return one.reshape(chunks, ROWS_BACK, one.shape[-1])

    smalls = (vec, wo, q, k, v, lse, slope, off)
    inputs = (cut(grad), cut(mlp), activ, dy, second, pre, cut(src), cut(tot), w, normed, att, eb, *smalls)
    piece = (2, 2, 2, PIECE // 8)
    shapes = [
        ((chunks, ROWS_BACK, width), BF16),
        ((activ.shape[1] // PIECE, *piece, width), BF16),
        ((second.shape[1] // PIECE, *piece, width), BF16),
        ((local // PIECE, *piece, width), BF16),
        ((3, width // PIECE, *piece, local), BF16),
        ((chunks, ROWS_BACK, width), BF16),
        ((8, width), F32),
    ]
    slots = BACK_SLOTS
    scratch = [
        pltpu.VMEM((2, length, PIECE), BF16),
        pltpu.VMEM(dy.shape, BF16),
        pltpu.VMEM(pre.shape, BF16),
        *[pltpu.VMEM((2, ROWS_BACK, width), BF16)] * 3,
        pltpu.VMEM(dy.shape, BF16),
        *[pltpu.VMEM(one.shape, one.dtype) for one in (w, att, eb)],
        *[pltpu.VMEM(one.shape, one.dtype) for one in smalls],
        pltpu.VMEM(q.shape, BF16),
        pltpu.VMEM((3, *q.shape), BF16),
        *[pltpu.VMEM((length, 2 * HD), F32)] * 2,
        pltpu.VMEM((6, 8, width), F32),
        pltpu.VMEM((4, 8, width), F32),
        pltpu.VMEM((3, 8, width), F32),
        pltpu.VMEM((8, 2, width), F32),
        dma((14,)),
        dma((2,)),
        dma((slots,)),
        dma((2, 2)),
        dma((2,)),
        dma((3,)),
        dma((3,)),
        dma((8,)),
        dma((8,)),
        *Chain.scratch(slots, (ROWS_BACK, width)),
        *Cube.scratch((PIECE // 8, BACK_COLUMNS), BACK_APART),
    ]
    return pl.pallas_call(
        functools.partial(back_kernel, n, local // HD),
        out_shape=[jax.ShapeDtypeStruct(*one) for one in shapes],
        in_specs=[pl.BlockSpec(memory_space=pl.ANY)] * len(inputs),
        out_specs=[pl.BlockSpec(memory_space=pl.ANY)] * len(shapes),
        scratch_shapes=scratch,
        compiler_params=pltpu.CompilerParams(
            collective_id=1, has_side_effects=True, vmem_limit_bytes=61 << 20
        ),
    )(*inputs)


def on_device(
    fast,
    n_tensor,
    inputs,
    block_ids,
    first_gain,
    first_shift,
    mixing_weight,
    mixing_bias,
    output_weight,
    output_bias,
    second_gain,
    second_shift,
    expand_weight,
    expand_bias,
    shrink_weight,
    shrink_bias,
    cotangent,
):
    source = inputs.astype(F32)
    upstream = cotangent.astype(F32)
    length, width = source.shape
    blocks = block_ids[0]
    local_width = mixing_weight.shape[2]
    local_heads = local_width // HD
    units = expand_weight.shape[1]
    first_head = lax.axis_index("tensor") * local_heads
    weights = mixing_weight.transpose(1, 0, 2)
    if fast:
        numbers = (first_head + jnp.arange(local_heads)).astype(F32)
        slope = jnp.broadcast_to((2.0 ** (-8.0 * (numbers + 1.0) / H))[:, None], (local_heads, 128))
        bias = jnp.stack([mixing_bias[0], jnp.zeros_like(mixing_bias[0]), mixing_bias[1]])
        normed_low, query, keys, vals, attended, logsum, off = head_call(
            inputs, weights, jnp.stack([first_gain, first_shift]), bias, slope, block_ids
        )
    else:
        normed_low = layer_norm(source, first_gain, first_shift).astype(BF16)

        def project(k):
            return jnp.dot(normed_low, weights[k], preferred_element_type=F32)

        query = (project(0) + mixing_bias[0]).astype(BF16).reshape(length, local_heads, HD)
        keys = project(1).astype(BF16).reshape(length, local_heads, HD)
        vals = (project(2) + mixing_bias[1]).astype(BF16).reshape(length, local_heads, HD)
        masked = biased_scores(query, keys, blocks, first_head)
        row_top = jnp.max(masked, axis=-1, keepdims=True)
        logsum = row_top + jnp.log(jnp.sum(jnp.exp(masked - row_top), axis=-1, keepdims=True))
        probs_low = jnp.exp(masked - logsum).astype(BF16)
        attended = (
            jnp.einsum("hqk,khd->qhd", probs_low, vals, preferred_element_type=F32)
            .reshape(length, local_width)
            .astype(BF16)
        )
    if fast:
        most = max(width, units)
        vectors = jnp.stack(
            [
                jnp.pad(one, (0, most - one.shape[0]))
                for one in (output_bias, second_gain, second_shift, expand_bias, first_gain, shrink_bias)
            ]
        )
        total, second_low, activ_low, pre_grad, partial_mlp, second_part, expand_bias_part = mlp_call(
            n_tensor, attended, output_weight, inputs, cotangent, expand_weight, shrink_weight, vectors
        )
    else:
        partial_out = jnp.dot(attended, output_weight, preferred_element_type=F32)
        resid = lax.psum(partial_out.astype(BF16), "tensor").astype(F32)
        hidden_state = source + (resid + output_bias)
        second_low = layer_norm(hidden_state, second_gain, second_shift).astype(BF16)
        pre_act = jnp.dot(second_low, expand_weight, preferred_element_type=F32) + expand_bias
        activ_low = gelu_exact(pre_act).astype(BF16)
        partial_mlp = jnp.dot(activ_low, shrink_weight, preferred_element_type=F32)
        act_grad = jnp.einsum("td,fd->tf", cotangent, shrink_weight, preferred_element_type=F32)
        _, gelu_pull = jax.vjp(gelu_exact, pre_act)
        pre_grad = gelu_pull(act_grad)[0].astype(BF16)
        expand_bias_part = jnp.sum(pre_grad.astype(F32), axis=0)
        second_part = jnp.einsum("tf,df->td", pre_grad, expand_weight, preferred_element_type=F32)
    if fast:
        outputs, shrink_sum, expand_sum, output_sum, mixing_sum, input_grad, small = back_call(
            n_tensor, second_part, partial_mlp, activ_low, cotangent, second_low, pre_grad, inputs, total,
            weights, normed_low, attended, expand_bias_part, vectors[:, :width], output_weight, query, keys, vals,
            logsum, slope, off,
        )
        outputs, input_grad = outputs.reshape(length, width), input_grad.reshape(length, width)
        shrink_weight_grad = shrink_sum.astype(F32).reshape(units, width)
        expand_weight_grad = expand_sum.astype(F32).reshape(width, units)
        mixing_weight_grad = mixing_sum.astype(F32).reshape(3, width, local_width).transpose(1, 0, 2)
        output_weight_grad = output_sum.astype(F32).reshape(local_width, width)
        first_gain_grad, first_shift_grad, second_gain_grad, second_shift_grad = small[0], small[1], small[2], small[3]
        output_bias_grad, expand_bias_grad, shrink_bias_grad = small[4], small[5], small[6]
        mixing_bias_grad = small[7, : 2 * local_width].reshape(2, local_width)
    else:
        shrink_bias_part = jnp.sum(upstream, axis=0)
        shrink_part = jnp.einsum("tf,td->fd", activ_low, cotangent, preferred_element_type=F32)
        expand_part = jnp.einsum("td,tf->df", second_low, pre_grad, preferred_element_type=F32)

        mlp_sum = lax.psum(partial_mlp.astype(BF16), "tensor").astype(F32)
        second_grad = lax.psum(second_part.astype(BF16), "tensor").astype(F32)
        outputs = (hidden_state + mlp_sum + shrink_bias).astype(BF16)
        hidden_grad, second_gain_part, second_shift_part = norm_backward(
            hidden_state, second_gain, second_shift, second_grad
        )
        hidden_grad = hidden_grad + upstream
        resid_low = hidden_grad.astype(BF16)
        output_part = jnp.einsum("tc,td->cd", attended, resid_low, preferred_element_type=F32)
        output_bias_part = jnp.sum(resid_low.astype(F32), axis=0)
        attended_grad = (
            jnp.einsum("td,cd->tc", resid_low, output_weight, preferred_element_type=F32)
            .astype(BF16)
            .reshape(length, local_heads, HD)
        )
        probs = jnp.exp(biased_scores(query, keys, blocks, first_head) - logsum)
        probs_low = probs.astype(BF16)
        prob_grad = jnp.einsum("qhd,khd->hqk", attended_grad, vals, preferred_element_type=F32)
        vals_grad = jnp.einsum(
            "hqk,qhd->khd", probs_low, attended_grad, preferred_element_type=F32
        ).astype(BF16)
        row_delta = jnp.sum(probs * prob_grad, axis=-1, keepdims=True)
        score_grad = (probs * (prob_grad - row_delta)).astype(BF16)
        scale_factor = 1.0 / math.sqrt(HD)
        query_grad = (
            jnp.einsum("hqk,khd->qhd", score_grad, keys, preferred_element_type=F32) * scale_factor
        ).astype(BF16)
        keys_grad = (
            jnp.einsum("hqk,qhd->khd", score_grad, query, preferred_element_type=F32) * scale_factor
        ).astype(BF16)
        grads = [one.reshape(length, local_width) for one in (query_grad, keys_grad, vals_grad)]
        mixing_bias_part = jnp.stack(
            [jnp.sum(grads[0].astype(F32), axis=0), jnp.sum(grads[2].astype(F32), axis=0)]
        )
        mixing_part = jnp.stack(
            [jnp.einsum("td,tc->dc", normed_low, one, preferred_element_type=F32) for one in grads]
        )
        normed_part = sum(
            jnp.einsum("tc,dc->td", one, weights[k], preferred_element_type=F32)
            for k, one in enumerate(grads)
        )
        normed_grad = lax.psum(normed_part.astype(BF16), "tensor").astype(F32)
        source_grad, first_gain_part, first_shift_part = norm_backward(
            source, first_gain, first_shift, normed_grad
        )
        input_grad = (source_grad + hidden_grad).astype(BF16)
        summed = lax.psum(
            (
                first_gain_part, first_shift_part, mixing_part, mixing_bias_part, output_part, output_bias_part,
                second_gain_part, second_shift_part, expand_part, expand_bias_part, shrink_part, shrink_bias_part,
            ),
            "dp",
        )
        first_gain_grad, first_shift_grad, mixing_weight_grad, mixing_bias_grad = summed[:4]
        mixing_weight_grad = mixing_weight_grad.transpose(1, 0, 2)
        output_weight_grad, output_bias_grad, second_gain_grad, second_shift_grad = summed[4:8]
        expand_weight_grad, expand_bias_grad, shrink_weight_grad, shrink_bias_grad = summed[8:]
    return (
        outputs,
        input_grad,
        first_gain_grad,
        first_shift_grad,
        mixing_weight_grad,
        mixing_bias_grad,
        output_weight_grad,
        output_bias_grad,
        second_gain_grad,
        second_shift_grad,
        expand_weight_grad,
        expand_bias_grad,
        shrink_weight_grad,
        shrink_bias_grad,
    )


def solution(mesh):
    in_specs = (
        P("dp", None),
        P("dp", None),
        P(),
        P(),
        P(None, None, "tensor"),
        P(None, "tensor"),
        P("tensor", None),
        P(),
        P(),
        P(),
        P(None, "tensor"),
        P("tensor"),
        P("tensor", None),
        P(),
        P("dp", None),
    )
    out_specs = (
        P("dp", None),
        P("dp", None),
        P(),
        P(),
        P(None, None, "tensor"),
        P(None, "tensor"),
        P("tensor", None),
        P(),
        P(),
        P(),
        P(None, "tensor"),
        P("tensor"),
        P("tensor", None),
        P(),
    )
    n_tensor = mesh.shape["tensor"]
    fast = mesh.shape["dp"] == 8 and n_tensor in (2, 4)
    return jax.shard_map(
        functools.partial(on_device, fast, n_tensor),
        mesh=mesh,
        in_specs=in_specs,
        out_specs=out_specs,
        check_vma=False,
    )
```
